32 devices in a mesh: expert: 8 (over z, x), shard: 4 (over y, core).
Axes of the slice: x: 2, y: 2, z: 4, core: 2. Of those that a mesh axis runs over, the one named last changes fastest.
Arguments:
- tokens: bfloat16 [25216, 512], P(('expert', 'shard')), may hold values from -6 to 6
- teacher: bfloat16 [25216, 512], P(('expert', 'shard')), may hold values from -6 to 6
- valid_mask: int32 [25216], P(('expert', 'shard')), may hold values from 0 to 1, as said below
- routes: int32 [25216, 2], P(('expert', 'shard')), may hold values from 0 to 7, all different within a row; in each aligned block of 788 rows (0 to 787, 788 to 1575, ...) at most 394 rows name the same one
- mixer_weight: bfloat16 [512, 1536], P('shard'), may hold values from -0.25 to 0.25
- merge_weight: bfloat16 [512, 512], P('shard'), may hold values from -1 to 1
- router_weight: bfloat16 [512, 8], P('shard'), may hold values from -0.1875 to 0.1875
- norm_gain: bfloat16 [2, 512], P(None, 'shard'), may hold values from 0.5 to 1.5
- norm_shift: bfloat16 [2, 512], P(None, 'shard'), may hold values from -0.59765625 to 0.59765625
- up_weight: bfloat16 [8, 512, 2048], P('expert', None, 'shard'), may hold values from -0.25 to 0.25
- inner_bias: bfloat16 [8, 2048], P('expert', 'shard'), may hold values from -0.59765625 to 0.59765625
- down_weight: bfloat16 [8, 2048, 512], P('expert', 'shard'), may hold values from -0.75 to 0.75
- outer_bias: bfloat16 [8, 512], P('expert', 'shard'), may hold values from -6 to 6
Outputs:
- output: bfloat16 [25216, 512], P(('expert', 'shard'))
- loss_value: float32 [], replicated
- token_grad: float32 [25216, 512], P(('expert', 'shard'))
- mixer_grad: float32 [512, 1536], P('shard')
- merge_grad: float32 [512, 512], P('shard')
- router_grad: float32 [512, 8], P('shard')
- gain_grad: float32 [2, 512], P(None, 'shard')
- shift_grad: float32 [2, 512], P(None, 'shard')
- up_grad: float32 [8, 512, 2048], P('expert', None, 'shard')
- inner_grad: float32 [8, 2048], P('expert', 'shard')
- down_grad: float32 [8, 2048, 512], P('expert', 'shard')
- outer_grad: float32 [8, 512], P('expert', 'shard')
The draws below stay inside these ranges and needn't reach their ends.
Inputs may be any that keep to these rules, and one draw needn't show every extreme that they name: `routes`: each token names two different experts. Among the 2 x 788 choices of the tokens of one device no expert is named more than 394 times, a bound that some block reaches. `valid_mask`: the first of each device's 788 tokens is valid.
All inputs are finite; a program needn't handle non-finite values.
Results may differ from the reference program's by a relative error of at most 0.011.
Values may be sent and summed in bfloat16 or wider, within the bound.
No kernel may reach another device: no remote copies, remote signals or barrier semaphores. Data moves between devices by JAX's collectives and lax.ppermute only.
A program may use at most 192 MiB of HBM per device.

```python
import math
import jax
import jax.numpy as jnp
import numpy as np
from jax import lax

D = 512
HEADS = 8
HEAD_DIM = 64
F = 2048
SEQ = 197
IMG_DEV = 4
TOK_DEV = 788
TOKENS = 25216
EXPERTS = 8
CAP = 394


def draw_valid_mask(key, part):
    positions = jnp.arange(TOKENS, dtype=jnp.int32)
    device_block = positions // TOK_DEV
    blocks_all = TOKENS // TOK_DEV
    threshold = 350 + 600 * device_block // max(1, blocks_all - 1)
    random_rolls = jax.random.randint(key, (TOKENS,), 0, 1000, dtype=jnp.int32)
    is_valid = (random_rolls < threshold) | (positions % TOK_DEV == 0)
    return is_valid.astype(jnp.int32)


def levels(rng, extent, cuts, smallest, high):
    loudness = 1.0
    for position, parts in cuts:
        heights = jax.random.uniform(jax.random.fold_in(jax.random.fold_in(rng, 6), position), (parts,), jnp.float32, smallest / len(cuts), high / len(cuts))
        loudness = loudness * jnp.repeat(jnp.exp(heights), extent[position] // parts).reshape((-1,) + (1,) * (len(extent) - 1 - position))
    return loudness


def shared_out(stream_key, own, number, rows, amount, top, reach, slope):
    ranking = jax.random.permutation(stream_key, amount)
    packed, common = shares(amount, rows * top, reach, slope, True), shares(amount, rows * top, reach, slope, False)
    places = jnp.arange(amount)

    def named(lengths, turn):
        used = int((lengths > 0).sum())
        fixed = max(1, used // 4)
        moved = fixed + (places - fixed + turn * (used - fixed)) % max(1, amount - fixed)
        return jnp.zeros((amount,), jnp.int32).at[ranking[jnp.where(places < fixed, places, moved)]].set(jnp.asarray(lengths, jnp.int32))

    lengths = jnp.where(number % 4 == 0, named(packed, number // 4), named(common, number - number // 4 - 1))
    mixed = jax.random.permutation(jax.random.fold_in(own, 3), amount)
    giver, receiver = mixed[0:amount // 2 * 2:2], mixed[1:amount // 2 * 2:2]
    room = jnp.minimum(lengths[giver] - 1, reach - lengths[receiver]) // 2
    room = jnp.where((giver == ranking[0]) | (receiver == ranking[0]) | (lengths[receiver] == 0), 0, jnp.maximum(room, 0))
    moved = jax.random.randint(jax.random.fold_in(own, 4), (amount // 2,), 0, 1 << 20) % (room + 1)
    lengths = lengths.at[giver].add(-moved).at[receiver].add(moved)
    labels = jnp.searchsorted(jnp.cumsum(lengths), jnp.arange(rows * top), side="right").astype(jnp.int32)
    grid = labels.reshape(top, rows).T
    grid = grid[jax.random.permutation(jax.random.fold_in(own, 1), rows)]
    turn = jax.random.randint(jax.random.fold_in(own, 2), (rows, 1), 0, top)
    return jnp.take_along_axis(grid, (jnp.arange(top)[None, :] + turn) % top, axis=1)


def shares(amount, total, bound, lean, full):
    portions = [(1 << 20) // math.isqrt(rank ** lean) + 1 for rank in range(1, amount + 1)]
    largest = bound if full else min(bound, max(-(-total // amount), total * portions[0] // sum(portions)))
    least = 1 if total - largest >= amount - 1 else 0
    given, surplus = [largest] + [least] * (amount - 1), total - largest - least * (amount - 1)
    while surplus > 0:
        candidates = [i for i in range(1, amount) if given[i] < largest] or [i for i in range(1, amount) if given[i] < bound]
        mass, budget = sum([portions[i] for i in candidates]), surplus
        for i in candidates:
            extra = min(bound - given[i], max(1, budget * portions[i] // mass), surplus)
            given[i] = given[i] + extra
            surplus = surplus - extra
    return np.array(given)


def scatter_about(key, dims, width, bound, cuts=(), kind=jnp.bfloat16):
    result = width * jax.random.normal(key, dims, jnp.float32)
    if cuts:
        result = result * levels(key, dims, cuts, -0.22, 0.18)
    return jnp.clip(result, -bound, bound).astype(kind)


def setup_inputs(seed: int = 0) -> dict:
    splits = jax.random.split(jax.random.key(seed), 14)
    tokens = scatter_about(splits[0], (TOKENS, D), 1.0, 6.0, ((0, 32),))
    teacher = scatter_about(splits[1], (TOKENS, D), 1.0, 6.0, ((0, 32),))
    valid_mask = draw_valid_mask(jax.random.fold_in(splits[13], 71), 0)
    routes_keys = jax.random.split(jax.random.fold_in(splits[3], 1), TOKENS // TOK_DEV)
    routes_turns = jax.random.permutation(jax.random.fold_in(splits[3], 3), TOKENS // TOK_DEV)
    routes = jax.vmap(lambda own, number: shared_out(jax.random.fold_in(splits[3], 2), own, number, TOK_DEV, EXPERTS, 2, CAP, 1))(routes_keys, routes_turns).reshape((TOKENS, 2))
    mixer_weight = scatter_about(splits[4], (D, 3 * D), D ** -0.5, 0.25, ((0, 4),))
    merge_weight = scatter_about(splits[5], (D, D), (D // 16) ** -0.5, 1.0, ((0, 4),))
    router_weight = scatter_about(splits[6], (D, EXPERTS), (2 * D) ** -0.5, 0.1875, ((0, 4),))
    norm_gain = jnp.clip(1.0 + 0.1 * jax.random.normal(splits[7], (2, D), jnp.float32), 0.5, 1.5).astype(jnp.bfloat16)
    norm_shift = scatter_about(splits[8], (2, D), 0.1, 0.59765625, ((1, 4),))
    up_weight = scatter_about(splits[9], (EXPERTS, D, F), D ** -0.5, 0.25, ((0, 8), (2, 4)))
    inner_bias = scatter_about(splits[10], (EXPERTS, F), 0.1, 0.59765625, ((0, 8), (1, 4)))
    down_weight = scatter_about(splits[11], (EXPERTS, F, D), (max(1, 2 * F // (EXPERTS * EXPERTS))) ** -0.5, 0.75, ((0, 8), (1, 4)))
    outer_bias = scatter_about(splits[12], (EXPERTS, D), (max(1, EXPERTS // 16)), 6.0, ((0, 8), (1, 4)))
    return dict(tokens=tokens, teacher=teacher, valid_mask=valid_mask, routes=routes, mixer_weight=mixer_weight, merge_weight=merge_weight, router_weight=router_weight, norm_gain=norm_gain, norm_shift=norm_shift, up_weight=up_weight, inner_bias=inner_bias, down_weight=down_weight, outer_bias=outer_bias)


@jax.custom_vjp
def low(v):
    return lax.optimization_barrier(v.astype(jnp.bfloat16)).astype(jnp.float32)

@jax.custom_vjp
def low_back(v):
    return v

def low_keep(v):
    return (low(v), None)

def low_pass(kept, grad):
    return (grad,)

def back_keep(v):
    return (v, None)

def back_low(kept, grad):
    return (low(grad),)
low.defvjp(low_keep, low_pass)
low_back.defvjp(back_keep, back_low)
norm_eps = 1e-06
highest = lax.Precision.HIGHEST

def layer_norm(inputs, scale_row, shift_row):
    centered = inputs - lax.optimization_barrier(jnp.mean(inputs, axis=-1, keepdims=True))
    variance = lax.optimization_barrier(jnp.mean(centered * centered, axis=-1, keepdims=True))
    return centered * lax.rsqrt(variance + norm_eps) * scale_row + shift_row

def product(left, right):
    return jnp.dot(left, right, preferred_element_type=jnp.float32, precision=highest)

def attend(mixed_block):
    shaped = mixed_block.reshape(IMG_DEV, SEQ, 3, HEADS, HEAD_DIM)
    scaling = HEAD_DIM ** (-0.5)
    scores = low_back(jnp.einsum('bqhd,bkhd->bhqk', shaped[:, :, 0], shaped[:, :, 1], precision=highest) * scaling)
    weights = low(jax.nn.softmax(scores, axis=-1))
    attended = jnp.einsum('bhqk,bkhd->bqhd', weights, shaped[:, :, 2], precision=highest)
    return low_back(low(attended.reshape(TOK_DEV, D)))

def expert_apply(pieces):
    inputs, up_matrix, inner_row, down_matrix, outer_row = pieces
    hidden = low_back(product(inputs, up_matrix) + inner_row)
    active = low(jax.nn.gelu(hidden, approximate=True))
    return low_back(low(product(active, down_matrix) + outer_row))

def reference(tokens, teacher, valid_mask, routes, mixer_weight, merge_weight, router_weight, norm_gain, norm_shift, up_weight, inner_bias, down_weight, outer_bias):
    blocks = TOKENS // TOK_DEV
    per_block = routes.reshape(blocks, 2 * TOK_DEV)
    route_hot = (per_block[:, :, None] == jnp.arange(EXPERTS, dtype=jnp.int32)[None, None, :]).astype(jnp.int32)
    earlier = jnp.cumsum(route_hot, axis=1) - route_hot
    slot_index = lax.optimization_barrier(jnp.sum(earlier * route_hot, axis=2))
    buffer_rows = (jnp.arange(blocks, dtype=jnp.int32)[:, None] * CAP + slot_index).reshape(-1).astype(jnp.int32)
    expert_ids = routes.reshape(-1).astype(jnp.int32)
    valid_rows = valid_mask.astype(jnp.float32)
    valid_count = jnp.sum(valid_mask).astype(jnp.float32)
    target = teacher.astype(jnp.float32)

    def forward(token_rows, mixer_matrix, merge_matrix, router_matrix, gain_rows, shift_rows, up_all, inner_all, down_all, outer_all):
        normed = low(layer_norm(token_rows, gain_rows[0], shift_rows[0]))
        mixed_rows = low_back(low(product(normed, mixer_matrix)))
        attended = lax.map(jax.checkpoint(attend), mixed_rows.reshape(blocks, TOK_DEV, 3 * D)).reshape(TOKENS, D)
        residual = token_rows + low_back(product(attended, merge_matrix))
        normed_two = low(layer_norm(residual, gain_rows[1], shift_rows[1]))
        logits = low_back(product(normed_two, router_matrix))
        gate_values = jnp.take_along_axis(jax.nn.softmax(logits, axis=-1), routes, axis=1)
        dispatch = jnp.zeros((EXPERTS, blocks * CAP, D), jnp.float32).at[expert_ids, buffer_rows].set(jnp.repeat(normed_two, 2, axis=0))
        produced = lax.map(jax.checkpoint(expert_apply), (low_back(dispatch), up_all, inner_all, down_all, outer_all))
        picked = produced[expert_ids, buffer_rows].reshape(TOKENS, 2, D)
        block_out = residual + lax.optimization_barrier(jnp.sum(gate_values[:, :, None] * picked, axis=1))
        error_rows = block_out - target
        return (block_out, jnp.sum(valid_rows * lax.optimization_barrier(jnp.sum(error_rows * error_rows, axis=1))) / (2.0 * valid_count))
    (block_out, loss_value), pullback = jax.vjp(forward, tokens.astype(jnp.float32), mixer_weight.astype(jnp.float32), merge_weight.astype(jnp.float32), router_weight.astype(jnp.float32), norm_gain.astype(jnp.float32), norm_shift.astype(jnp.float32), up_weight.astype(jnp.float32), inner_bias.astype(jnp.float32), down_weight.astype(jnp.float32), outer_bias.astype(jnp.float32))
    gradients = pullback((jnp.zeros_like(block_out), jnp.asarray(TOKENS, jnp.float32)))
    return (block_out.astype(jnp.bfloat16), loss_value, gradients[0], gradients[1], gradients[2], gradients[3], gradients[4], gradients[5], gradients[6], gradients[7], gradients[8], gradients[9])
```

```python
import functools

import jax
import jax.numpy as jnp
from jax import lax
from jax.experimental import pallas as pl
from jax.experimental.pallas import tpu as pltpu
from jax.sharding import PartitionSpec as P

HEADS = 8
HEAD_DIM = 64
SEQ = 197
EPS = 1e-06
ROW = 16
WIN = 224
TILE = 160
GATHER = 128
MLP = 256
SCATTER = 256
LANES = 128
NEG = -1e30
SCALING = HEAD_DIM ** (-0.5)
GELU_C = 0.7978845608028654
GELU_K = 0.044715
f32 = jnp.float32
bf16 = jnp.bfloat16
VMEM_SPEC = pl.BlockSpec(memory_space=pltpu.VMEM)
SMEM_SPEC = pl.BlockSpec(memory_space=pltpu.SMEM)
ANY_SPEC = pl.BlockSpec(memory_space=pl.ANY)
VMEM_LIMIT = 60 * 1024 * 1024


def up_to(value, step):
    return (value + step - 1) // step * step


def dot(left, right):
    return jnp.dot(left, right, preferred_element_type=f32)


def dot_last(left, right):
    return lax.dot_general(left, right, (((1,), (1,)), ((), ())), preferred_element_type=f32)


def dot_first(left, right):
    return lax.dot_general(left, right, (((0,), (0,)), ((), ())), preferred_element_type=f32)


def swap(array, axis, ways, bit):
    return lax.ppermute(array, axis, [(i, i ^ bit) for i in range(ways)])


def cost(flops, bytes_accessed, transcendentals=0):
    return pl.CostEstimate(
        flops=int(flops), bytes_accessed=int(bytes_accessed), transcendentals=int(transcendentals)
    )


def params():
    return pltpu.CompilerParams(vmem_limit_bytes=VMEM_LIMIT)


def normalise(rows):
    mean = jnp.mean(rows, axis=-1, keepdims=True)
    centered = rows - mean
    variance = jnp.mean(centered * centered, axis=-1, keepdims=True)
    return centered, lax.rsqrt(variance + EPS)


def place_dense(shard, tiles, mixer, merge, sems):
    copies = []
    columns = mixer.shape[1]
    for k, tile in enumerate(tiles):
        rows = tile.shape[0]
        base = pl.multiple_of((shard ^ k) * rows, rows)
        copies.append(
            pltpu.make_async_copy(
                tile.at[:, 0:columns], mixer.at[pl.ds(base, rows)], sems.at[2 * k]
            )
        )
        copies.append(
            pltpu.make_async_copy(
                tile.at[:, columns : columns + merge.shape[1]],
                merge.at[pl.ds(base, rows)],
                sems.at[2 * k + 1],
            )
        )
    return copies


def place_columns(shard, smalls, into, first):
    width = into.shape[1] // len(smalls)
    for k, small in enumerate(smalls):
        if width % LANES == 0:
            base = pl.multiple_of((shard ^ k) * width, width)
            into[:, pl.ds(base, width)] = small[:, first : first + width]
            continue
        for place in range(len(smalls)):

            @pl.when((shard ^ k) == place)
            def _():
                into[:, place * width : (place + 1) * width] = small[:, first : first + width]


def image_window(image):
    start = pl.multiple_of(image * SEQ // ROW * ROW, ROW)
    offset = image * SEQ - start
    rows = lax.broadcasted_iota(jnp.int32, (WIN, 1), 0)
    columns = lax.broadcasted_iota(jnp.int32, (1, WIN), 1)
    row_in = (rows >= offset) & (rows < offset + SEQ)
    column_in = (columns >= offset) & (columns < offset + SEQ)
    return start, row_in, column_in


def attention_forward_kernel(n_tiles, images, norm_lane, *refs):
    shard_ref, tok = refs[0], refs[1]
    dense = refs[2 : 2 + n_tiles]
    smalls = refs[2 + n_tiles : 2 + 2 * n_tiles]
    qkv, att, lse, res, normed_two, mixer, merge, norms, sems = refs[2 + 2 * n_tiles :]
    shard = shard_ref[0]
    width = tok.shape[1]
    copies = place_dense(shard, dense, mixer, merge, sems)
    for copy in copies:
        copy.start()
    place_columns(shard, smalls, norms, norm_lane)
    for copy in copies:
        copy.wait()
    for t in range(tok.shape[0] // TILE):
        rows = slice(t * TILE, (t + 1) * TILE)
        centered, rate = normalise(tok[rows].astype(f32))
        normed = (centered * rate * norms[0:1] + norms[2:3]).astype(bf16)
        qkv[rows] = dot(normed, mixer[...]).astype(bf16)
        att[rows] = jnp.zeros((TILE, width), bf16)
        lse[rows] = jnp.zeros((TILE, LANES), f32)
    lane = lax.broadcasted_iota(jnp.int32, (1, LANES), 1)

    def image_step(image, carry):
        start, row_in, column_in = image_window(image)
        window = pl.ds(start, WIN)
        totals = jnp.zeros((WIN, LANES), f32)
        for slab in range(width // LANES):
            q = qkv[window, slab * LANES : (slab + 1) * LANES]
            k = qkv[window, width + slab * LANES : width + (slab + 1) * LANES]
            v = qkv[window, 2 * width + slab * LANES : 2 * width + (slab + 1) * LANES]
            outs = []
            for half in range(2):
                mine = (lane >= half * HEAD_DIM) & (lane < (half + 1) * HEAD_DIM)
                scores = dot_last(jnp.where(mine, q, jnp.zeros_like(q)), k) * SCALING
                scores = jnp.where(column_in, scores, NEG)
                top = jnp.max(scores, axis=-1, keepdims=True)
                powers = jnp.exp(scores - top)
                total = jnp.sum(powers, axis=-1, keepdims=True)
                low = jnp.where(row_in, powers * (1.0 / total), 0.0).astype(bf16)
                outs.append(dot(low, v))
                head = 2 * slab + half
                totals = jnp.where(lane == head, top + jnp.log(total), totals)
            out = jnp.where(lane < HEAD_DIM, outs[0], outs[1]).astype(bf16)
            columns = slice(slab * LANES, (slab + 1) * LANES)
            att[window, columns] = att[window, columns] + out
        lse[window] = jnp.where(row_in, totals, lse[window])
        return carry

    lax.fori_loop(images[0], images[1], image_step, 0)
    for t in range(tok.shape[0] // TILE):
        rows = slice(t * TILE, (t + 1) * TILE)
        residual = tok[rows].astype(f32) + dot(att[rows], merge[...])
        res[rows] = residual
        centered, rate = normalise(residual)
        normed_two[rows] = (centered * rate * norms[1:2] + norms[3:4]).astype(bf16)


def attention_forward(shard, tok, dense, smalls, images, norm_lane):
    rows, width = tok.shape
    n = len(dense)
    return pl.pallas_call(
        functools.partial(attention_forward_kernel, n, (0, images), norm_lane),
        name="attention_forward",
        out_shape=(
            jax.ShapeDtypeStruct((rows, 3 * width), bf16),
            jax.ShapeDtypeStruct((rows, width), bf16),
            jax.ShapeDtypeStruct((rows, LANES), f32),
            jax.ShapeDtypeStruct((rows, width), f32),
            jax.ShapeDtypeStruct((rows, width), bf16),
        ),
        in_specs=[SMEM_SPEC, VMEM_SPEC] + [ANY_SPEC] * n + [VMEM_SPEC] * n,
        out_specs=(VMEM_SPEC,) * 5,
        scratch_shapes=[
            pltpu.VMEM((width, 3 * width), bf16),
            pltpu.VMEM((width, width), bf16),
            pltpu.VMEM((8, width), f32),
            pltpu.SemaphoreType.DMA((2 * n,)),
        ],
        compiler_params=params(),
        cost_estimate=cost(2 * rows * width * width * 4.6, rows * width * 20, rows * SEQ * HEADS),
    )(shard, tok, *dense, *smalls)


def place_expert(shard, e_ref, dense, smalls, ups, downs, router, outer, up, down, sems, router_lane, inner):
    n = len(dense)
    copies = []
    for k in range(n):
        rows = dense[k].shape[0]
        base = pl.multiple_of((shard ^ k) * rows, rows)
        copies.append(
            pltpu.make_async_copy(
                dense[k].at[:, router_lane : router_lane + LANES],
                router.at[pl.ds(base, rows)],
                sems.at[4 * n + k],
            )
        )
    place_columns(shard, smalls, outer, inner)
    for j in range(2):
        for k in range(n):
            copies.append(pltpu.make_async_copy(ups[j * n + k], up.at[j, k], sems.at[2 * (j * n + k)]))
            copies.append(pltpu.make_async_copy(downs[j * n + k], down.at[j, k], sems.at[2 * (j * n + k) + 1]))
    for copy in copies:
        copy.start()
    return copies


def expert_gates(rows, router, expert, experts):
    lane = lax.broadcasted_iota(jnp.int32, (1, LANES), 1)
    logits = jnp.where(lane < experts, dot(rows, router), NEG)
    powers = jnp.exp(logits - jnp.max(logits, axis=-1, keepdims=True))
    probs = powers * (1.0 / jnp.sum(powers, axis=-1, keepdims=True))
    mine = lane == expert
    return probs, jnp.sum(jnp.where(mine, probs, 0.0), axis=-1, keepdims=True), mine


def gather_rows(j, group, counts, pos, blocks, into, offsets):
    width = into.shape[2]
    tokens = pos.shape[1]
    row = lax.broadcasted_iota(jnp.int32, (GATHER, 1), 0)

    def block_step(b, base):
        count = counts[2 * b + j]
        places = pos[pl.ds(2 * b + j, 1), :]
        offsets[j, b] = base

        def tile_step(i, carry):
            hot = jnp.where(places == row + i * GATHER, 1.0, 0.0).astype(bf16)
            at = pl.multiple_of(base + i * GATHER, ROW)
            into[j, pl.ds(at, GATHER), :] = dot(hot, blocks[b]).astype(bf16)
            return carry

        lax.fori_loop(0, (count + GATHER - 1) // GATHER, tile_step, 0)
        return base + (count + ROW - 1) // ROW * ROW

    end = lax.fori_loop(0, group, block_step, jnp.int32(0))
    into[j, pl.ds(pl.multiple_of(end, ROW), MLP), :] = jnp.zeros((MLP, width), bf16)
    return end


def scatter_rows(group, counts, places, source, outs, staged, sems, offsets, total):
    column = lax.broadcasted_iota(jnp.int32, (1, SCATTER), 1)

    def leave(b):
        return pltpu.make_async_copy(staged.at[b % 2], outs[b], sems.at[b % 2])

    for b in range(group):
        total[...] = jnp.zeros(total.shape, f32)
        for j in range(2):
            mine = places[:, 2 * b + j : 2 * b + j + 1]
            base = offsets[j, b]

            def tile_step(i, inner):
                hot = jnp.where(mine == column + i * SCATTER, 1.0, 0.0).astype(bf16)
                at = pl.multiple_of(base + i * SCATTER, ROW)
                total[...] += dot(hot, source[j, pl.ds(at, SCATTER), :])
                return inner

            lax.fori_loop(0, (counts[2 * b + j] + SCATTER - 1) // SCATTER, tile_step, 0)
        if b >= 2:
            leave(b - 2).wait()
        staged[b % 2] = total[...].astype(bf16)
        leave(b).start()
    for b in range(max(0, group - 2), group):
        leave(b).wait()


def block_copies(pieces, refs, blocks, sems, first):
    copies = []
    for n, (b, row, rows) in enumerate(pieces):
        copies.append(
            pltpu.make_async_copy(refs[n], blocks.at[b, pl.ds(row, rows)], sems.at[first + n])
        )
    return copies


def expert_forward_kernel(n, group, experts, router_lane, pieces, *refs):
    shard_ref, e_ref, counts, pos, places = refs[:5]
    refs = refs[5:]
    sources, refs = refs[: len(pieces)], refs[len(pieces) :]
    dense, smalls, refs = refs[:n], refs[n : 2 * n], refs[2 * n :]
    ups, downs, refs = refs[: 2 * n], refs[2 * n : 4 * n], refs[4 * n :]
    outs, refs = refs[:group], refs[group:]
    x_rows, y_rows = refs[:2]
    blocks, up, down, router, outer, scaled, total, staged, offsets, sems, block_sems, leave_sems = refs[2:]
    shard = shard_ref[0]
    hidden_width = up.shape[3]
    weights = place_expert(
        shard, e_ref, dense, smalls, ups, downs, router, outer, up, down, sems, router_lane, hidden_width
    )
    arrivals = block_copies(pieces, sources, blocks, block_sems, 0)
    for copy in arrivals:
        copy.start()
    for copy in arrivals:
        copy.wait()
    for copy in weights[:n]:
        copy.wait()
    for j in range(2):
        end = gather_rows(j, group, counts, pos, blocks, x_rows, offsets)
        for copy in weights[n + 2 * n * j : n + 2 * n * (j + 1)]:
            copy.wait()

        def tile_step(i, carry):
            at = pl.ds(pl.multiple_of(i * MLP, MLP), MLP)
            x = x_rows[j, at, :]
            _, gate, _ = expert_gates(x, router[...], e_ref[j], experts)
            acc = jnp.broadcast_to(outer[j : j + 1], (MLP, x.shape[1]))
            for k in range(n):
                hidden = dot(x, up[j, k]) + smalls[k][j : j + 1, 0:hidden_width]
                inside = hidden * (GELU_C + GELU_C * GELU_K * (hidden * hidden))
                half = 0.5 * hidden
                active = (half + half * jnp.tanh(inside)).astype(bf16)
                acc = acc + dot(active, down[j, k])
            y = acc.astype(bf16)
            y_rows[j, at, :] = y
            scaled[j, at, :] = (gate * y.astype(f32)).astype(bf16)
            return carry

        tiles = (end + MLP - 1) // MLP
        lax.fori_loop(0, tiles, tile_step, 0)
        scaled[j, pl.ds(pl.multiple_of(tiles * MLP, MLP), MLP), :] = jnp.zeros((MLP, scaled.shape[2]), bf16)
    scatter_rows(group, counts, places, scaled, outs, staged, leave_sems, offsets, total)


def expert_rows(group, capacity):
    return up_to(group * up_to(capacity, ROW), MLP) + MLP


def expert_forward(scalars, pos, places, sources, pieces, dense, smalls, ups, downs, group, experts, capacity, router_lane):
    shard, e_ids, counts = scalars
    n = len(dense)
    width = sources[0].shape[1]
    tokens = pos.shape[1]
    hidden = ups[0].shape[1]
    rows = expert_rows(group, capacity)
    flops = 2 * 2 * group * capacity * width * hidden * n
    return pl.pallas_call(
        functools.partial(expert_forward_kernel, n, group, experts, router_lane, pieces),
        name="expert_forward",
        out_shape=[jax.ShapeDtypeStruct((tokens, width), bf16)] * group
        + [jax.ShapeDtypeStruct((2, rows, width), bf16)] * 2,
        in_specs=[SMEM_SPEC] * 3
        + [VMEM_SPEC] * 2
        + [ANY_SPEC] * (len(sources) + n)
        + [VMEM_SPEC] * n
        + [ANY_SPEC] * (4 * n),
        out_specs=[ANY_SPEC] * group + [VMEM_SPEC] * 2,
        scratch_shapes=[
            pltpu.VMEM((group, tokens, width), bf16),
            pltpu.VMEM((2, n, width, hidden), bf16),
            pltpu.VMEM((2, n, hidden, width), bf16),
            pltpu.VMEM((width, LANES), bf16),
            pltpu.VMEM((8, width), f32),
            pltpu.VMEM((2, rows, width), bf16),
            pltpu.VMEM((tokens, width), f32),
            pltpu.VMEM((2, tokens, width), bf16),
            pltpu.SMEM((2, group), jnp.int32),
            pltpu.SemaphoreType.DMA((5 * n,)),
            pltpu.SemaphoreType.DMA((len(sources),)),
            pltpu.SemaphoreType.DMA((2,)),
        ],
        compiler_params=params(),
        cost_estimate=cost(flops, 16 * 2**20, group * capacity * hidden * n),
    )(shard, e_ids, counts, pos, places, *sources, *dense, *smalls, *ups, *downs)


def expert_backward_kernel(n, group, experts, router_lane, pieces, *refs):
    shard_ref, e_ref, counts, pos, places = refs[:5]
    refs = refs[5:]
    sources, refs = refs[: len(pieces)], refs[len(pieces) :]
    x_rows, y_rows, refs = refs[0], refs[1], refs[2:]
    dense, smalls, refs = refs[:n], refs[n : 2 * n], refs[2 * n :]
    ups, downs, refs = refs[: 2 * n], refs[2 * n : 4 * n], refs[4 * n :]
    outs, refs = refs[:group], refs[group:]
    pg_rows, act_out, hg_out, router_grad, inner_grad, outer_grad = refs[:6]
    blocks, up, down, router, outer, f_rows, b_rows, total, staged, act, hg = refs[6:17]
    offsets, sems, block_sems, out_sems, leave_sems = refs[17:]
    shard = shard_ref[0]
    hidden_width = up.shape[3]
    width = up.shape[2]
    weights = place_expert(
        shard, e_ref, dense, smalls, ups, downs, router, outer, up, down, sems, router_lane, hidden_width
    )
    arrivals = block_copies(pieces, sources, blocks, block_sems, 0)
    for copy in arrivals:
        copy.start()
    for copy in arrivals:
        copy.wait()
    for copy in weights:
        copy.wait()
    router_grad[...] = jnp.zeros(router_grad.shape, f32)
    inner_grad[...] = jnp.zeros(inner_grad.shape, f32)
    outer_grad[...] = jnp.zeros(outer_grad.shape, f32)

    def saves(j, i, slot):
        at = pl.ds(pl.multiple_of(i * MLP, MLP), MLP)
        return (
            pltpu.make_async_copy(act.at[slot], act_out.at[j, at], out_sems.at[0, slot]),
            pltpu.make_async_copy(hg.at[slot], hg_out.at[j, at], out_sems.at[1, slot]),
        )

    for j in range(2):
        end = gather_rows(j, group, counts, pos, blocks, f_rows, offsets)
        tiles = (end + MLP - 1) // MLP

        def tile_step(i, carry):
            slot = lax.rem(i, 2)

            @pl.when(i >= 2)
            def _():
                for copy in saves(j, i - 2, slot):
                    copy.wait()

            at = pl.ds(pl.multiple_of(i * MLP, MLP), MLP)
            x = x_rows[j, at, :]
            f = f_rows[j, at, :].astype(f32)
            probs, gate, mine = expert_gates(x, router[...], e_ref[j], experts)
            pg = (gate * f).astype(bf16)
            pg_rows[j, at, :] = pg
            gate_grad = jnp.sum(f * y_rows[j, at, :].astype(f32), axis=-1, keepdims=True)
            logit = gate_grad * gate * (jnp.where(mine, 1.0, 0.0) - probs)
            high = logit.astype(bf16)
            rest = (logit - high.astype(f32)).astype(bf16)
            acc = dot_last(high, router[...]) + dot_last(rest, router[...])
            router_grad[...] += dot_first(x, high) + dot_first(x, rest)
            outer_grad[j : j + 1] += jnp.sum(pg.astype(f32), axis=0, keepdims=True)
            for k in range(n):
                hidden = dot(x, up[j, k]) + smalls[k][j : j + 1, 0:hidden_width]
                active_grad = dot_last(pg, down[j, k])
                square = hidden * hidden
                tanh = jnp.tanh(hidden * (GELU_C + GELU_C * GELU_K * square))
                half = 0.5 * hidden
                columns = slice(k * hidden_width, (k + 1) * hidden_width)
                act[slot, :, columns] = (half + half * tanh).astype(bf16)
                slope = 0.5 + 0.5 * tanh + half * (1.0 - tanh * tanh) * (
                    GELU_C + 3.0 * GELU_C * GELU_K * square
                )
                grad = (active_grad * slope).astype(bf16)
                hg[slot, :, columns] = grad
                inner_grad[j : j + 1, columns] += jnp.sum(grad.astype(f32), axis=0, keepdims=True)
                acc = acc + dot_last(grad, up[j, k])
            for copy in saves(j, i, slot):
                copy.start()
            b_rows[j, at, :] = acc.astype(bf16)
            return carry

        lax.fori_loop(0, tiles, tile_step, 0)
        for back in (2, 1):

            @pl.when(tiles >= back)
            def _():
                for copy in saves(j, tiles - back, lax.rem(tiles - back, 2)):
                    copy.wait()

        b_rows[j, pl.ds(pl.multiple_of(tiles * MLP, MLP), MLP), :] = jnp.zeros((MLP, width), bf16)
    scatter_rows(group, counts, places, b_rows, outs, staged, leave_sems, offsets, total)


def expert_backward(scalars, pos, places, sources, pieces, x_rows, y_rows, dense, smalls, ups, downs, group, experts, capacity, router_lane):
    shard, e_ids, counts = scalars
    n = len(dense)
    width = sources[0].shape[1]
    tokens = pos.shape[1]
    hidden = ups[0].shape[1]
    rows = expert_rows(group, capacity)
    flops = 3 * 2 * group * capacity * width * hidden * n
    return pl.pallas_call(
        functools.partial(expert_backward_kernel, n, group, experts, router_lane, pieces),
        name="expert_backward",
        out_shape=[jax.ShapeDtypeStruct((tokens, width), bf16)] * group
        + [
            jax.ShapeDtypeStruct((2, rows, width), bf16),
            jax.ShapeDtypeStruct((2, rows, hidden * n), bf16),
            jax.ShapeDtypeStruct((2, rows, hidden * n), bf16),
            jax.ShapeDtypeStruct((width, LANES), f32),
            jax.ShapeDtypeStruct((8, hidden * n), f32),
            jax.ShapeDtypeStruct((8, width), f32),
        ],
        in_specs=[SMEM_SPEC] * 3
        + [VMEM_SPEC] * 2
        + [ANY_SPEC] * len(sources)
        + [VMEM_SPEC] * 2
        + [ANY_SPEC] * n
        + [VMEM_SPEC] * n
        + [ANY_SPEC] * (4 * n),
        out_specs=[ANY_SPEC] * group + [VMEM_SPEC, ANY_SPEC, ANY_SPEC] + [VMEM_SPEC] * 3,
        scratch_shapes=[
            pltpu.VMEM((group, tokens, width), bf16),
            pltpu.VMEM((2, n, width, hidden), bf16),
            pltpu.VMEM((2, n, hidden, width), bf16),
            pltpu.VMEM((width, LANES), bf16),
            pltpu.VMEM((8, width), f32),
            pltpu.VMEM((2, rows, width), bf16),
            pltpu.VMEM((2, rows, width), bf16),
            pltpu.VMEM((tokens, width), f32),
            pltpu.VMEM((2, tokens, width), bf16),
            pltpu.VMEM((2, MLP, hidden * n), bf16),
            pltpu.VMEM((2, MLP, hidden * n), bf16),
            pltpu.SMEM((2, group), jnp.int32),
            pltpu.SemaphoreType.DMA((5 * n,)),
            pltpu.SemaphoreType.DMA((len(sources),)),
            pltpu.SemaphoreType.DMA((2, 2)),
            pltpu.SemaphoreType.DMA((2,)),
        ],
        compiler_params=params(),
        cost_estimate=cost(flops, 40 * 2**20, group * capacity * hidden * n),
    )(shard, e_ids, counts, pos, places, *sources, x_rows, y_rows, *dense, *smalls, *ups, *downs)


def weight_grads_kernel(n, tiles_ref, x, pg, act, hg, up_grad, down_grad, up_total, down_total):
    tiles = tiles_ref[pl.program_id(0)]
    up_total[...] = jnp.zeros(up_total.shape, f32)
    down_total[...] = jnp.zeros(down_total.shape, f32)

    def tile_step(i, carry):
        at = pl.ds(pl.multiple_of(i * MLP, MLP), MLP)
        up_total[...] += dot_first(x[0, at, :], hg[0, at, :])
        down_total[...] += dot_first(act[0, at, :], pg[0, at, :])
        return carry

    lax.fori_loop(0, tiles, tile_step, 0)
    up_grad[0, 0] = up_total[...].astype(bf16)
    down_grad[0, 0] = down_total[...].astype(bf16)


def weight_grads(tiles, x_rows, pg_rows, act, hg, n):
    _, rows, width = x_rows.shape
    hidden = act.shape[2] // n
    wide = pl.BlockSpec((1, rows, width), lambda j, k, t: (j, 0, 0))
    narrow = pl.BlockSpec((1, rows, hidden), lambda j, k, t: (j, 0, k))
    return pl.pallas_call(
        functools.partial(weight_grads_kernel, n),
        name="weight_grads",
        grid_spec=pltpu.PrefetchScalarGridSpec(
            num_scalar_prefetch=1,
            grid=(2, n),
            in_specs=[wide, wide, narrow, narrow],
            out_specs=(
                pl.BlockSpec((1, 1, width, hidden), lambda j, k, t: (j, k, 0, 0)),
                pl.BlockSpec((1, 1, hidden, width), lambda j, k, t: (j, k, 0, 0)),
            ),
            scratch_shapes=[pltpu.VMEM((width, hidden), f32), pltpu.VMEM((hidden, width), f32)],
        ),
        out_shape=(
            jax.ShapeDtypeStruct((2, n, width, hidden), bf16),
            jax.ShapeDtypeStruct((2, n, hidden, width), bf16),
        ),
        compiler_params=params(),
        cost_estimate=cost(4 * 2 * rows * width * hidden * n, 40 * 2**20),
    )(tiles, x_rows, pg_rows, act, hg)


def norm_backward(rows, gain, grad):
    centered, rate = normalise(rows)
    unit = centered * rate
    scaled = grad * gain
    back = rate * (
        scaled
        - jnp.mean(scaled, axis=-1, keepdims=True)
        - unit * jnp.mean(scaled * unit, axis=-1, keepdims=True)
    )
    return (
        back,
        jnp.sum(grad * unit, axis=0, keepdims=True),
        jnp.sum(grad, axis=0, keepdims=True),
        unit,
    )


def attention_backward_kernel(n_tiles, group, images, norm_lane, *refs):
    shard_ref, own, others = refs[0], refs[1], refs[2 : 1 + group]
    fg, res, att, qkv, lse, tok = refs[1 + group : 7 + group]
    refs = refs[7 + group :]
    dense, smalls = refs[:n_tiles], refs[n_tiles : 2 * n_tiles]
    token_grad, mixer_grad, merge_grad, norm_grad = refs[2 * n_tiles : 2 * n_tiles + 4]
    mixer, merge, norms, dres, low, datt, normed, mg, sems = refs[2 * n_tiles + 4 :]
    shard = shard_ref[0]
    width = tok.shape[1]
    n_rows = tok.shape[0]
    copies = place_dense(shard, dense, mixer, merge, sems)
    for copy in copies:
        copy.start()
    place_columns(shard, smalls, norms, norm_lane)
    for copy in copies:
        copy.wait()
    norm_grad[...] = jnp.zeros(norm_grad.shape, f32)
    for t in range(n_rows // TILE):
        rows = slice(t * TILE, (t + 1) * TILE)
        grad = own[rows].astype(f32)
        for other in others:
            grad = grad + other[rows].astype(f32)
        back, gain, shift, _ = norm_backward(res[rows], norms[1:2], grad)
        norm_grad[1:2] += gain
        norm_grad[3:4] += shift
        total = fg[rows] + back
        dres[rows] = total
        low[rows] = total.astype(bf16)
        datt[rows] = dot_last(low[rows], merge[...]).astype(bf16)
        mg[rows] = jnp.zeros((TILE, 3 * width), bf16)
    merge_grad[...] = dot_first(att[...], low[...])
    lane = lax.broadcasted_iota(jnp.int32, (1, LANES), 1)

    def image_step(image, carry):
        start, row_in, column_in = image_window(image)
        inside = row_in & column_in
        window = pl.ds(start, WIN)
        for slab in range(width // LANES):
            q_at = slice(slab * LANES, (slab + 1) * LANES)
            k_at = slice(width + slab * LANES, width + (slab + 1) * LANES)
            v_at = slice(2 * width + slab * LANES, 2 * width + (slab + 1) * LANES)
            q, k, v = qkv[window, q_at], qkv[window, k_at], qkv[window, v_at]
            do = datt[window, q_at]
            parts = []
            for half in range(2):
                head = 2 * slab + half
                mine = (lane >= half * HEAD_DIM) & (lane < (half + 1) * HEAD_DIM)
                zero = jnp.zeros_like(q)
                scores = dot_last(jnp.where(mine, q, zero), k) * SCALING
                log_total = lse[window, head : head + 1]
                weights = jnp.where(inside, jnp.exp(jnp.where(inside, scores - log_total, 0.0)), 0.0)
                dv = dot_first(weights.astype(bf16), do)
                dw = dot_last(jnp.where(mine, do, zero), v)
                inner = jnp.sum(weights * dw, axis=-1, keepdims=True)
                ds = (weights * (dw - inner)).astype(bf16)
                parts.append((dot(ds, k) * SCALING, dot_first(ds, q) * SCALING, dv))
            for at, first, second in zip((q_at, k_at, v_at), parts[0], parts[1]):
                both = jnp.where(lane < HEAD_DIM, first, second).astype(bf16)
                mg[window, at] = mg[window, at] + both
        return carry

    lax.fori_loop(images[0], images[1], image_step, 0)
    for t in range(n_rows // TILE):
        rows = slice(t * TILE, (t + 1) * TILE)
        grad = dot_last(mg[rows], mixer[...])
        back, gain, shift, unit = norm_backward(tok[rows].astype(f32), norms[0:1], grad)
        norm_grad[0:1] += gain
        norm_grad[2:3] += shift
        token_grad[rows] = dres[rows] + back
        normed[rows] = (unit * norms[0:1] + norms[2:3]).astype(bf16)
    for c in range(3):
        columns = slice(c * width, (c + 1) * width)
        mixer_grad[:, columns] = dot_first(normed[...], mg[:, columns])


def attention_backward(shard, own, others, fg, res, att, qkv, lse, tok, dense, smalls, images, norm_lane):
    rows, width = tok.shape
    n = len(dense)
    group = len(others) + 1
    whole = lambda array: pl.BlockSpec(array.shape, lambda i: (0,) * array.ndim)
    shapes = (
        jax.ShapeDtypeStruct((rows, width), f32),
        jax.ShapeDtypeStruct((width, 3 * width), f32),
        jax.ShapeDtypeStruct((width, width), f32),
        jax.ShapeDtypeStruct((8, width), f32),
    )
    return pl.pallas_call(
        functools.partial(attention_backward_kernel, n, group, (0, images), norm_lane),
        name="attention_backward",
        grid=(1,),
        out_shape=shapes,
        in_specs=[SMEM_SPEC, whole(own)]
        + [whole(a) for a in others]
        + [whole(a) for a in (fg, res, att, qkv, lse, tok)]
        + [ANY_SPEC] * n
        + [whole(a) for a in smalls],
        out_specs=tuple(whole(s) for s in shapes),
        scratch_shapes=[
            pltpu.VMEM((width, 3 * width), bf16),
            pltpu.VMEM((width, width), bf16),
            pltpu.VMEM((8, width), f32),
            pltpu.VMEM((rows, width), f32),
            pltpu.VMEM((rows, width), bf16),
            pltpu.VMEM((rows, width), bf16),
            pltpu.VMEM((rows, width), bf16),
            pltpu.VMEM((rows, 3 * width), bf16),
            pltpu.SemaphoreType.DMA((2 * n,)),
        ],
        compiler_params=params(),
        cost_estimate=cost(2 * rows * width * width * 9.5, rows * width * 30, rows * SEQ * HEADS),
    )(shard, own, *others, fg, res, att, qkv, lse, tok, *dense, *smalls)


def bits_of(ways):
    bit = ways // 2
    while bit:
        yield bit
        bit //= 2


def gather_tiles(array, axis, ways):
    tiles = {0: array}
    for bit in bits_of(ways):
        for k in list(tiles):
            tiles[k | bit] = swap(tiles[k], axis, ways, bit)
    return [tiles[k] for k in range(ways)]


def scatter_sum(tiles, axis, ways, send_type):
    tiles = dict(enumerate(tiles))
    for bit in reversed(list(bits_of(ways))):
        for k in [k for k in tiles if k & bit]:
            arrived = swap(tiles.pop(k).astype(send_type), axis, ways, bit)
            tiles[k ^ bit] = tiles[k ^ bit].astype(f32) + arrived.astype(f32)
    return tiles[0]


def exchange(array, ways, group):
    rows = array.shape[0]
    arrays, pieces = [array], [(0, 0, rows)]
    if group == 4:
        half = rows // 2
        one, two = swap(array, "expert", ways, 1), swap(array, "expert", ways, 2)
        arrays += [one, two, swap(one[:half], "expert", ways, 2), swap(two[half:], "expert", ways, 1)]
        pieces += [(1, 0, rows), (2, 0, rows), (3, 0, half), (3, half, rows - half)]
    else:
        for b in range(1, group):
            arrays.append(swap(array, "expert", ways, b))
            pieces.append((b, 0, rows))
    return arrays, tuple(pieces)


def give_back(blocks, ways, group):
    return [swap(blocks[b], "expert", ways, b) for b in range(1, group)]


def per_device(
    tokens,
    teacher,
    valid_mask,
    routes,
    mixer_weight,
    merge_weight,
    router_weight,
    norm_gain,
    norm_shift,
    up_weight,
    inner_bias,
    down_weight,
    outer_bias,
):
    ways = lax.axis_size("expert")
    shards = lax.axis_size("shard")
    shard = lax.axis_index("shard").astype(jnp.int32)
    expert = lax.axis_index("expert").astype(jnp.int32)
    token_count, width = tokens.shape
    images = token_count // SEQ
    experts = router_weight.shape[1]
    group = ways // 2
    capacity = min(token_count, max(2, 4 * token_count // experts))
    rows = up_to(token_count, TILE)
    shard_rows = width // shards
    hidden = up_weight.shape[2]
    router_lane = 4 * width
    norm_lane = hidden + shard_rows

    dense_own = jnp.concatenate(
        [mixer_weight, merge_weight, jnp.pad(router_weight, ((0, 0), (0, LANES - experts)))], axis=1
    )
    bias = jnp.concatenate([inner_bias, outer_bias], axis=1).astype(f32)
    bias_other = swap(bias, "expert", ways, group)
    small_own = jnp.concatenate(
        [
            jnp.pad(jnp.concatenate([bias, bias_other], axis=0), ((0, 6), (0, 0))),
            jnp.pad(jnp.concatenate([norm_gain, norm_shift], axis=0).astype(f32), ((0, 4), (0, 0))),
        ],
        axis=1,
    )
    dense = gather_tiles(dense_own, "shard", shards)
    smalls = gather_tiles(small_own, "shard", shards)
    up_own, down_own = up_weight[0], down_weight[0]
    ups = gather_tiles(up_own, "shard", shards)
    downs = gather_tiles(down_own, "shard", shards)
    ups = ups + gather_tiles(swap(up_own, "expert", ways, group), "shard", shards)
    downs = downs + gather_tiles(swap(down_own, "expert", ways, group), "shard", shards)

    route_rows = jnp.pad(routes, ((0, rows - token_count), (0, 0)), constant_values=-1).T
    ids = jnp.arange(experts, dtype=jnp.int32)[:, None]
    named = (route_rows[0:1] == ids) | (route_rows[1:2] == ids)
    order = jnp.arange(rows, dtype=jnp.int32)
    earlier = (order[:, None] < order[None, :]).astype(bf16)
    slots = jnp.dot(named.astype(bf16), earlier, preferred_element_type=f32).astype(jnp.int32)
    slots = jnp.where(named, slots, -1)
    slot_blocks = jnp.stack([slots] + [swap(slots, "expert", ways, b) for b in range(1, group)])
    pos = jnp.concatenate(
        [
            lax.dynamic_slice_in_dim(slot_blocks, expert, 1, 1),
            lax.dynamic_slice_in_dim(slot_blocks, expert ^ group, 1, 1),
        ],
        axis=1,
    ).reshape(2 * group, rows)
    counts = jnp.max(pos, axis=1) + 1
    places = jnp.pad(pos.T, ((0, 0), (0, LANES - 2 * group)), constant_values=-1)
    ends = jnp.sum((counts.reshape(group, 2) + ROW - 1) // ROW * ROW, axis=0)
    tile_counts = (ends + MLP - 1) // MLP
    shard_id = shard[None]
    e_ids = jnp.stack([expert, expert ^ group])
    scalars = (shard_id, e_ids, counts)

    valid_rows = jnp.pad(valid_mask, ((0, rows - token_count),)).astype(f32)[:, None]
    valid_count = jnp.broadcast_to(jnp.sum(valid_rows), (8, LANES))
    for axis, size in (("shard", shards), ("expert", ways)):
        for bit in bits_of(size):
            valid_count = valid_count + swap(valid_count, axis, size, bit)
    valid_count = valid_count[0, 0]

    tok = jnp.pad(tokens, ((0, rows - token_count), (0, 0)))
    target = jnp.pad(teacher, ((0, rows - token_count), (0, 0)))
    qkv, att, lse, res, normed_two = attention_forward(
        shard_id, tok, dense, smalls, images, norm_lane
    )
    arrived, pieces = exchange(normed_two, ways, group)
    *parts, x_rows, y_rows = expert_forward(
        scalars, pos, places, arrived, pieces, dense, smalls, ups, downs, group, experts, capacity, router_lane
    )
    returned = give_back(parts, ways, group)
    block_out = res + parts[0].astype(f32)
    for part in returned:
        block_out = block_out + part.astype(f32)
    error = block_out - target.astype(f32)
    squared = jnp.sum(valid_rows * jnp.sum(error * error, axis=1, keepdims=True))
    all_tokens = token_count * ways * shards
    fg = all_tokens / valid_count * valid_rows * error
    grad_arrived, pieces = exchange(fg.astype(bf16), ways, group)
    *grad_parts, pg_rows, act, hg, router_part, inner_part, outer_part = expert_backward(
        scalars, pos, places, grad_arrived, pieces, x_rows, y_rows, dense, smalls, ups, downs, group, experts, capacity, router_lane
    )
    grad_returned = give_back(grad_parts, ways, group)
    up_part, down_part = weight_grads(tile_counts, x_rows, pg_rows, act, hg, shards)
    sums = {}
    for j in (1, 0):
        for name, part in (("up", up_part), ("down", down_part)):
            sums[name, j] = scatter_sum([part[j, k] for k in range(shards)], "shard", shards, bf16)
    up_grad = sums["up", 0] + swap(sums["up", 1].astype(bf16), "expert", ways, group).astype(f32)
    down_grad = sums["down", 0] + swap(sums["down", 1].astype(bf16), "expert", ways, group).astype(f32)

    token_grad, mixer_part, merge_part, norm_part = attention_backward(
        shard_id, grad_parts[0], grad_returned, fg, res, att, qkv, lse, tok, dense, smalls, images, norm_lane
    )

    def by_shard(array, axis):
        return [
            lax.dynamic_slice_in_dim(array, (shard ^ k) * shard_rows, shard_rows, axis)
            for k in range(shards)
        ]

    bias_tiles = [
        jnp.concatenate([inner_part[:, k * hidden : (k + 1) * hidden], outer_tile], axis=1)
        for k, outer_tile in enumerate(by_shard(outer_part, 1))
    ]
    bias_sum = scatter_sum(bias_tiles, "shard", shards, f32)
    bias_sum = bias_sum[0:1] + swap(bias_sum[1:2], "expert", ways, group)
    inner_grad, outer_grad = bias_sum[:, :hidden], bias_sum[:, hidden:]

    dense_part = jnp.concatenate([mixer_part, merge_part, router_part], axis=1)
    dense_sum = scatter_sum(by_shard(dense_part, 0), "shard", shards, bf16)
    norm_rows = norm_part.at[4].set(squared)
    norm_sum = scatter_sum(by_shard(norm_rows, 1), "shard", shards, f32)
    for bit in bits_of(ways):
        dense_low = dense_sum.astype(bf16)
        dense_sum = dense_low.astype(f32) + swap(dense_low, "expert", ways, bit).astype(f32)
        norm_sum = norm_sum + swap(norm_sum, "expert", ways, bit)
    loss_value = norm_sum[4, 0] / (2.0 * valid_count)
    return (
        block_out[:token_count].astype(bf16),
        loss_value,
        token_grad[:token_count],
        dense_sum[:, : 3 * width],
        dense_sum[:, 3 * width : 4 * width],
        dense_sum[:, 4 * width : 4 * width + experts],
        norm_sum[0:2],
        norm_sum[2:4],
        up_grad[None],
        inner_grad,
        down_grad[None],
        outer_grad,
    )


def solution(mesh):
    in_specs = (
        P(("expert", "shard"), None),
        P(("expert", "shard"), None),
        P(("expert", "shard")),
        P(("expert", "shard"), None),
        P("shard", None),
        P("shard", None),
        P("shard", None),
        P(None, "shard"),
        P(None, "shard"),
        P("expert", None, "shard"),
        P("expert", "shard"),
        P("expert", "shard", None),
        P("expert", "shard"),
    )
    out_specs = (
        P(("expert", "shard"), None),
        P(),
        P(("expert", "shard"), None),
        P("shard", None),
        P("shard", None),
        P("shard", None),
        P(None, "shard"),
        P(None, "shard"),
        P("expert", None, "shard"),
        P("expert", "shard"),
        P("expert", "shard", None),
        P("expert", "shard"),
    )
    return jax.shard_map(
        per_device, mesh=mesh, in_specs=in_specs, out_specs=out_specs, check_vma=False
    )
```

```python
import functools

import jax
import jax.numpy as jnp
from jax import lax
from jax.experimental import pallas as pl
from jax.experimental.pallas import tpu as pltpu
from jax.sharding import PartitionSpec as P

HEADS = 8
HEAD_DIM = 64
SEQ = 197
EPS = 1e-06
ROW = 16
WIN = 208
TILE = 160
GATHER = 208
MLP = 256
SCATTER = 256
LANES = 128
NEG = -1e30
SCALING = HEAD_DIM ** (-0.5)
GELU_C = 0.7978845608028654
GELU_K = 0.044715
f32 = jnp.float32
bf16 = jnp.bfloat16
VMEM_SPEC = pl.BlockSpec(memory_space=pltpu.VMEM)
SMEM_SPEC = pl.BlockSpec(memory_space=pltpu.SMEM)
ANY_SPEC = pl.BlockSpec(memory_space=pl.ANY)
VMEM_LIMIT = 60 * 1024 * 1024
FORWARD_US = 20
BACKWARD_US = 20


def up_to(value, step):
    return (value + step - 1) // step * step


def dot(left, right):
    return jnp.dot(left, right, preferred_element_type=f32)


def dot_last(left, right):
    return lax.dot_general(left, right, (((1,), (1,)), ((), ())), preferred_element_type=f32)


def dot_first(left, right):
    return lax.dot_general(left, right, (((0,), (0,)), ((), ())), preferred_element_type=f32)


def swap(array, axis, ways, bit):
    return lax.ppermute(array, axis, [(i, i ^ bit) for i in range(ways)])


def cost(microseconds):
    return pl.CostEstimate(
        flops=int(microseconds * 1.15e9), bytes_accessed=1 << 20, transcendentals=0
    )


def params():
    return pltpu.CompilerParams(vmem_limit_bytes=VMEM_LIMIT)


def normalise(rows):
    mean = jnp.mean(rows, axis=-1, keepdims=True)
    centered = rows - mean
    variance = jnp.mean(centered * centered, axis=-1, keepdims=True)
    return centered, lax.rsqrt(variance + EPS)


def place_dense(shard, tiles, mixer, merge, normt, sems):
    copies = []
    columns = mixer.shape[1]
    last = tiles[0].shape[1] - LANES
    for k, tile in enumerate(tiles):
        copies.append(
            pltpu.make_async_copy(
                tile.at[0:ROW, last : last + LANES], normt.at[k], sems.at[2 * len(tiles) + k]
            )
        )
    for k, tile in enumerate(tiles):
        rows = tile.shape[0]
        base = pl.multiple_of((shard ^ k) * rows, rows)
        copies.append(
            pltpu.make_async_copy(
                tile.at[:, 0:columns], mixer.at[pl.ds(base, rows)], sems.at[2 * k]
            )
        )
        copies.append(
            pltpu.make_async_copy(
                tile.at[:, columns : columns + merge.shape[1]],
                merge.at[pl.ds(base, rows)],
                sems.at[2 * k + 1],
            )
        )
    return copies


def place_columns(shard, smalls, into, first):
    width = into.shape[1] // len(smalls)
    for k, small in enumerate(smalls):
        if width % LANES == 0:
            base = pl.multiple_of((shard ^ k) * width, width)
            into[:, pl.ds(base, width)] = small[:, first : first + width]
            continue
        for place in range(len(smalls)):

            @pl.when((shard ^ k) == place)
            def _():
                into[:, place * width : (place + 1) * width] = small[:, first : first + width]


def place_norms(shard, normt, norms):
    tiles = [normt[k][0:8].astype(f32) for k in range(normt.shape[0])]
    place_columns(shard, tiles, norms, 0)


def pack_kernel(mixer, merge, router, gain, shift, up, inner, down, outer, dense, near, row, sems):
    columns, width = mixer.shape[1], merge.shape[1]
    own, hidden = gain.shape[1], up.shape[2]
    last = columns + width
    moves = [
        (mixer, dense.at[:, 0:columns]),
        (merge, dense.at[:, columns:last]),
        (down.at[0], near.at[hidden : 2 * hidden]),
    ]
    for fold in range(width // hidden):
        at = slice(fold * hidden, (fold + 1) * hidden)
        moves.append((up.at[0, at], near.at[0:hidden, at]))
    copies = [pltpu.make_async_copy(source, into, sems.at[i]) for i, (source, into) in enumerate(moves)]
    for copy in copies:
        copy.start()
    dense[:, last : last + 2 * LANES] = jnp.zeros((dense.shape[0], 2 * LANES), bf16)
    dense[:, last : last + router.shape[1]] = router[...]
    row[...] = jnp.zeros(row.shape, f32)
    row[0:2, 0:own] = gain[...].astype(f32)
    row[2:4, 0:own] = shift[...].astype(f32)
    dense[0:ROW, last + LANES : last + 2 * LANES] = row[:, 0:LANES].astype(bf16)
    row[...] = jnp.zeros(row.shape, f32)
    row[0:1, 0:hidden] = inner[...].astype(f32)
    row[1:2, 0:own] = outer[...].astype(f32)
    near[2 * hidden : 2 * hidden + ROW] = row[...].astype(bf16)
    for copy in copies:
        copy.wait()


def pack(mixer, merge, router, gain, shift, up, inner, down, outer):
    own, width = merge.shape
    hidden = up.shape[2]
    return pl.pallas_call(
        pack_kernel,
        name="pack",
        out_shape=(
            jax.ShapeDtypeStruct((own, mixer.shape[1] + width + 2 * LANES), bf16),
            jax.ShapeDtypeStruct((2 * hidden + ROW, width), bf16),
        ),
        in_specs=[ANY_SPEC] * 2 + [VMEM_SPEC] * 3 + [ANY_SPEC, VMEM_SPEC, ANY_SPEC, VMEM_SPEC],
        out_specs=(VMEM_SPEC, VMEM_SPEC),
        scratch_shapes=[
            pltpu.VMEM((ROW, width), f32),
            pltpu.SemaphoreType.DMA((3 + width // hidden,)),
        ],
        compiler_params=params(),
        cost_estimate=cost(2),
    )(mixer, merge, router, gain, shift, up, inner, down, outer)


def row_tiles(rows):
    return [slice(first, min(first + TILE, rows)) for first in range(0, rows, TILE)]


def image_window(base, image):
    first = base + image * SEQ
    start = pl.multiple_of(first // ROW * ROW, ROW)
    offset = first - start
    rows = lax.broadcasted_iota(jnp.int32, (WIN, 1), 0)
    columns = lax.broadcasted_iota(jnp.int32, (1, WIN), 1)
    row_in = (rows >= offset) & (rows < offset + SEQ)
    column_in = (columns >= offset) & (columns < offset + SEQ)
    return start, row_in, column_in


def attention_forward_kernel(n_tiles, base, images, *refs):
    shard_ref, tok = refs[0], refs[1]
    dense = refs[2 : 2 + n_tiles]
    qkv, att, weights, res, normed_two, mixer, merge, normt, norms, sems = refs[2 + n_tiles :]
    shard = shard_ref[0]
    width = tok.shape[1]
    copies = place_dense(shard, dense, mixer, merge, normt, sems)
    for copy in copies:
        copy.start()
    for copy in copies:
        copy.wait()
    place_norms(shard, normt, norms)
    for rows in row_tiles(tok.shape[0]):
        centered, rate = normalise(tok[rows].astype(f32))
        normed = (centered * rate * norms[0:1] + norms[2:3]).astype(bf16)
        qkv[rows] = dot(normed, mixer[...]).astype(bf16)
    att[...] = jnp.zeros(att.shape, bf16)
    lane = lax.broadcasted_iota(jnp.int32, (1, LANES), 1)

    def image_step(image, carry):
        start, row_in, column_in = image_window(base, image)
        window = pl.ds(start, WIN)
        for slab in range(width // LANES):
            q = qkv[window, slab * LANES : (slab + 1) * LANES]
            k = qkv[window, width + slab * LANES : width + (slab + 1) * LANES]
            v = qkv[window, 2 * width + slab * LANES : 2 * width + (slab + 1) * LANES]
            outs = []
            for half in range(2):
                mine = (lane >= half * HEAD_DIM) & (lane < (half + 1) * HEAD_DIM)
                scores = dot_last(jnp.where(mine, q, jnp.zeros_like(q)), k) * SCALING
                scores = jnp.where(column_in, scores, NEG)
                top = jnp.max(scores, axis=-1, keepdims=True)
                powers = jnp.exp(scores - top)
                total = jnp.sum(powers, axis=-1, keepdims=True)
                low = (powers * jnp.where(row_in, 1.0 / total, 0.0)).astype(bf16)
                weights[image, 2 * slab + half] = low
                outs.append(dot(low, v))
            out = jnp.where(lane < HEAD_DIM, outs[0], outs[1]).astype(bf16)
            columns = slice(slab * LANES, (slab + 1) * LANES)
            att[window, columns] = att[window, columns] + out
        return carry

    lax.fori_loop(0, images, image_step, 0)
    for rows in row_tiles(tok.shape[0]):
        residual = tok[rows].astype(f32) + dot(att[rows], merge[...])
        res[rows] = residual
        centered, rate = normalise(residual)
        normed_two[rows] = (centered * rate * norms[1:2] + norms[3:4]).astype(bf16)


def attention_forward(shard, tok, dense, base, images):
    rows, width = tok.shape
    n = len(dense)
    return pl.pallas_call(
        functools.partial(attention_forward_kernel, n, base, images),
        name="attention_forward",
        out_shape=(
            jax.ShapeDtypeStruct((rows, 3 * width), bf16),
            jax.ShapeDtypeStruct((rows, width), bf16),
            jax.ShapeDtypeStruct((images, HEADS, WIN, WIN), bf16),
            jax.ShapeDtypeStruct((rows, width), f32),
            jax.ShapeDtypeStruct((rows, width), bf16),
        ),
        in_specs=[SMEM_SPEC, VMEM_SPEC] + [ANY_SPEC] * n,
        out_specs=(VMEM_SPEC,) * 5,
        scratch_shapes=[
            pltpu.VMEM((width, 3 * width), bf16),
            pltpu.VMEM((width, width), bf16),
            pltpu.VMEM((n, ROW, LANES), bf16),
            pltpu.VMEM((8, width), f32),
            pltpu.SemaphoreType.DMA((3 * n,)),
        ],
        compiler_params=params(),
        cost_estimate=cost(7),
    )(shard, tok, *dense)


def weight_copies(shard, dense, tiles, router, up, down, bias, sems, router_lane):
    n = len(dense)
    width, hidden = up.shape[2], up.shape[3]
    folds = width // hidden
    routers, weights = [], [[], []]
    for k, tile in enumerate(dense):
        rows = tile.shape[0]
        base = pl.multiple_of((shard ^ k) * rows, rows)
        routers.append(
            pltpu.make_async_copy(
                tile.at[:, router_lane : router_lane + LANES], router.at[pl.ds(base, rows)], sems.at[0, 0, k]
            )
        )
    for j in range(2):
        for k in range(n):
            tile = tiles[j * n + k]
            for fold in range(folds):
                at = slice(fold * hidden, (fold + 1) * hidden)
                weights[j].append(
                    pltpu.make_async_copy(
                        tile.at[0:hidden, at], up.at[j, k, at], sems.at[1 + j, fold, k]
                    )
                )
            weights[j].append(
                pltpu.make_async_copy(
                    tile.at[hidden : 2 * hidden], down.at[j, k], sems.at[1 + j, folds, k]
                )
            )
            weights[j].append(
                pltpu.make_async_copy(
                    tile.at[2 * hidden : 2 * hidden + ROW], bias.at[j, k], sems.at[1 + j, folds + 1, k]
                )
            )
    return routers, weights


def block_starts(group, counts):
    starts = []
    for j in range(2):
        at, firsts = jnp.int32(0), []
        for b in range(group):
            firsts.append(pl.multiple_of(at, ROW))
            at = at + (counts[2 * b + j] + ROW - 1) // ROW * ROW
        starts.append((firsts, pl.multiple_of(at, ROW)))
    return starts


def gather_rows(group, counts, pos, blocks, into, starts):
    width = into.shape[2]
    row = lax.broadcasted_iota(jnp.int32, (GATHER, 1), 0)
    for b in range(group):
        hot = [
            jnp.where(pos[2 * b + j : 2 * b + j + 1, :] == row, 1.0, 0.0).astype(bf16) for j in range(2)
        ]
        both = dot(jnp.concatenate(hot, axis=0), blocks[b]).astype(bf16)
        for j in range(2):
            base = starts[j][0][b]
            into[j, pl.ds(base, GATHER), :] = both[j * GATHER : (j + 1) * GATHER]

            def more(i, carry, j=j, base=base):
                some = jnp.where(pos[2 * b + j : 2 * b + j + 1, :] == row + i * GATHER, 1.0, 0.0)
                at = pl.multiple_of(base + i * GATHER, ROW)
                into[j, pl.ds(at, GATHER), :] = dot(some.astype(bf16), blocks[b]).astype(bf16)
                return carry

            lax.fori_loop(1, (counts[2 * b + j] + GATHER - 1) // GATHER, more, 0)
    for j in range(2):
        into[j, pl.ds(starts[j][1], MLP), :] = jnp.zeros((MLP, width), bf16)


def scatter_rows(group, counts, places, source, outs, staged, sems, starts, total):
    column = lax.broadcasted_iota(jnp.int32, (1, SCATTER), 1)

    def leave(b):
        return pltpu.make_async_copy(staged.at[b % 2], outs[b], sems.at[b % 2])

    for b in range(group):
        mine = [places[:, 2 * b + j : 2 * b + j + 1] for j in range(2)]
        hot = jnp.concatenate(
            [jnp.where(mine[j] == column, 1.0, 0.0).astype(bf16) for j in range(2)], axis=1
        )
        rows = jnp.concatenate(
            [source[j, pl.ds(starts[j][0][b], SCATTER), :] for j in range(2)], axis=0
        )
        if b >= 2:
            leave(b - 2).wait()
        value = dot(hot, rows)
        staged[b % 2] = value.astype(bf16)

        @pl.when((counts[2 * b] > SCATTER) | (counts[2 * b + 1] > SCATTER))
        def _():
            total[...] = value
            for j in range(2):

                def more(i, carry, j=j):
                    some = jnp.where(mine[j] == column + i * SCATTER, 1.0, 0.0).astype(bf16)
                    at = pl.multiple_of(starts[j][0][b] + i * SCATTER, ROW)
                    total[...] += dot(some, source[j, pl.ds(at, SCATTER), :])
                    return carry

                lax.fori_loop(1, (counts[2 * b + j] + SCATTER - 1) // SCATTER, more, 0)
            staged[b % 2] = total[...].astype(bf16)

        leave(b).start()
    for b in range(max(0, group - 2), group):
        leave(b).wait()


def block_copies(refs, blocks, sems):
    return [pltpu.make_async_copy(ref, blocks.at[b], sems.at[b]) for b, ref in enumerate(refs)]


def tile_at(i):
    return pl.ds(pl.multiple_of(i * MLP, MLP), MLP)


def drain(copies, tiles):
    for back in (2, 1):

        @pl.when(tiles >= back)
        def _():
            for copy in copies(tiles - back):
                copy.wait()


def expert_forward_kernel(n, group, experts, router_lane, *refs):
    shard_ref, e_ref, counts, pos, places = refs[:5]
    refs = refs[5:]
    sources, dense, tiles_in, refs = refs[:group], refs[group : group + n], refs[group + n : group + 3 * n], refs[group + 3 * n :]
    outs, refs = refs[:group], refs[group:]
    x_out, y_out, probs_out, act_out, slope_out = refs[:5]
    blocks, up, down, bias, router, outer, x_rows, scaled, total, staged, act, slope, y, probs = refs[5:19]
    sems, block_sems, leave_sems, out_sems, x_sems = refs[19:]
    shard = shard_ref[0]
    hidden_width = up.shape[3]
    width = up.shape[2]
    arrivals = block_copies(sources, blocks, block_sems)
    routers, weights = weight_copies(shard, dense, tiles_in, router, up, down, bias, sems, router_lane)
    for copy in arrivals + routers + weights[0] + weights[1]:
        copy.start()
    for copy in arrivals:
        copy.wait()
    starts = block_starts(group, counts)
    gather_rows(group, counts, pos, blocks, x_rows, starts)
    for copy in routers:
        copy.wait()
    lane = lax.broadcasted_iota(jnp.int32, (1, LANES), 1)
    for j in range(2):
        tiles = (starts[j][1] + MLP - 1) // MLP

        def saves(i, j=j):
            slot = lax.rem(i, 2)
            return [
                pltpu.make_async_copy(source.at[slot], into.at[j, tile_at(i)], out_sems.at[m, slot])
                for m, (source, into) in enumerate(
                    ((act, act_out), (slope, slope_out), (y, y_out), (probs, probs_out))
                )
            ]

        def save_x(i, j=j):
            return pltpu.make_async_copy(x_rows.at[j, tile_at(i)], x_out.at[j, tile_at(i)], x_sems.at[j, i])

        for copy in weights[j]:
            copy.wait()
        place_columns(shard, [bias[j, k][0:8].astype(f32) for k in range(n)], outer.at[j], 0)

        def tile_step(i, carry):
            slot = lax.rem(i, 2)

            @pl.when(i >= 2)
            def _():
                for copy in saves(i - 2):
                    copy.wait()

            save_x(i).start()
            x = x_rows[j, tile_at(i), :]
            logits = jnp.where(lane < experts, dot(x, router[...]), NEG)
            powers = jnp.exp(logits - jnp.max(logits, axis=-1, keepdims=True))
            shares = powers * (1.0 / jnp.sum(powers, axis=-1, keepdims=True))
            probs[slot] = shares
            gate = jnp.sum(jnp.where(lane == e_ref[j], shares, 0.0), axis=-1, keepdims=True)
            for k in range(n):
                hidden = dot(x, up[j, k]) + bias[j, k, 0:1, 0:hidden_width].astype(f32)
                square = hidden * hidden
                share = 0.5 * jnp.tanh(hidden * (GELU_C + GELU_C * GELU_K * square)) + 0.5
                active = hidden * share
                columns = slice(k * hidden_width, (k + 1) * hidden_width)
                act[slot, :, columns] = active.astype(bf16)
                slope[slot, :, columns] = (
                    share
                    + (active - active * share) * (2.0 * GELU_C + 6.0 * GELU_C * GELU_K * square)
                ).astype(bf16)
            acc = jnp.broadcast_to(outer[j, 1:2], (MLP, width))
            for k in range(n):
                acc = acc + dot(act[slot, :, k * hidden_width : (k + 1) * hidden_width], down[j, k])
            low = acc.astype(bf16)
            y[slot] = low
            for copy in saves(i):
                copy.start()
            scaled[j, tile_at(i), :] = (gate * low.astype(f32)).astype(bf16)
            return carry

        lax.fori_loop(0, tiles, tile_step, 0)
        drain(saves, tiles)

        def wait_x(i, carry):
            save_x(i).wait()
            return carry

        lax.fori_loop(0, tiles, wait_x, 0)
        scaled[j, tile_at(tiles), :] = jnp.zeros((MLP, width), bf16)
    scatter_rows(group, counts, places, scaled, outs, staged, leave_sems, starts, total)


def expert_rows(group, capacity):
    return up_to(group * up_to(capacity, ROW), MLP) + MLP


def expert_forward(scalars, pos, places, sources, dense, tiles, group, experts, capacity, router_lane):
    n = len(dense)
    width = sources[0].shape[1]
    tokens = pos.shape[1]
    hidden = (tiles[0].shape[0] - ROW) // 2
    rows = expert_rows(group, capacity)
    return pl.pallas_call(
        functools.partial(expert_forward_kernel, n, group, experts, router_lane),
        name="expert_forward",
        out_shape=[jax.ShapeDtypeStruct((tokens, width), bf16)] * group
        + [jax.ShapeDtypeStruct((2, rows, width), bf16)] * 2
        + [jax.ShapeDtypeStruct((2, rows, LANES), f32)]
        + [jax.ShapeDtypeStruct((2, rows, hidden * n), bf16)] * 2,
        in_specs=[SMEM_SPEC] * 3 + [VMEM_SPEC] * 2 + [ANY_SPEC] * (group + 3 * n),
        out_specs=[ANY_SPEC] * (group + 5),
        scratch_shapes=[
            pltpu.VMEM((group, tokens, width), bf16),
            pltpu.VMEM((2, n, width, hidden), bf16),
            pltpu.VMEM((2, n, hidden, width), bf16),
            pltpu.VMEM((2, n, ROW, width), bf16),
            pltpu.VMEM((width, LANES), bf16),
            pltpu.VMEM((2, 8, width), f32),
            pltpu.VMEM((2, rows, width), bf16),
            pltpu.VMEM((2, rows, width), bf16),
            pltpu.VMEM((tokens, width), f32),
            pltpu.VMEM((2, tokens, width), bf16),
            pltpu.VMEM((2, MLP, hidden * n), bf16),
            pltpu.VMEM((2, MLP, hidden * n), bf16),
            pltpu.VMEM((2, MLP, width), bf16),
            pltpu.VMEM((2, MLP, LANES), f32),
            pltpu.SemaphoreType.DMA((3, width // hidden + 2, n)),
            pltpu.SemaphoreType.DMA((group,)),
            pltpu.SemaphoreType.DMA((2,)),
            pltpu.SemaphoreType.DMA((4, 2)),
            pltpu.SemaphoreType.DMA((2, rows // MLP)),
        ],
        compiler_params=params(),
        cost_estimate=cost(FORWARD_US),
    )(*scalars, pos, places, *sources, *dense, *tiles)


def expert_backward_kernel(n, group, router_lane, *refs):
    shard_ref, e_ref, counts, pos, places = refs[:5]
    refs = refs[5:]
    sources, dense, tiles_in, refs = refs[:group], refs[group : group + n], refs[group + n : group + 3 * n], refs[group + 3 * n :]
    x_in, y_in, probs_in, slope_in, refs = refs[0], refs[1], refs[2], refs[3], refs[4:]
    outs, refs = refs[:group], refs[group:]
    pg_out, hg_out, router_grad, inner_grad, outer_grad = refs[:5]
    blocks, up, down, bias, router, f_rows, b_rows, total, staged, hg, pg, slope, x, y, probs = refs[5:20]
    sems, block_sems, leave_sems, out_sems, in_sems = refs[20:]
    shard = shard_ref[0]
    hidden_width = up.shape[3]
    width = up.shape[2]
    arrivals = block_copies(sources, blocks, block_sems)
    routers, weights = weight_copies(shard, dense, tiles_in, router, up, down, bias, sems, router_lane)
    for copy in arrivals + routers + weights[0] + weights[1]:
        copy.start()
    router_grad[...] = jnp.zeros(router_grad.shape, f32)
    inner_grad[...] = jnp.zeros(inner_grad.shape, f32)
    outer_grad[...] = jnp.zeros(outer_grad.shape, f32)
    for copy in arrivals:
        copy.wait()
    starts = block_starts(group, counts)
    gather_rows(group, counts, pos, blocks, f_rows, starts)
    for copy in routers:
        copy.wait()
    lane = lax.broadcasted_iota(jnp.int32, (1, LANES), 1)
    for j in range(2):
        tiles = (starts[j][1] + MLP - 1) // MLP

        def saves(i, j=j):
            slot = lax.rem(i, 2)
            return (
                pltpu.make_async_copy(hg.at[slot], hg_out.at[j, tile_at(i)], out_sems.at[0, slot]),
                pltpu.make_async_copy(pg.at[slot], pg_out.at[j, tile_at(i)], out_sems.at[1, slot]),
            )

        def loads(i, j=j):
            slot = lax.rem(i, 2)
            return [
                pltpu.make_async_copy(source.at[j, tile_at(i)], into.at[slot], in_sems.at[m, slot])
                for m, (source, into) in enumerate(
                    ((x_in, x), (y_in, y), (probs_in, probs), (slope_in, slope))
                )
            ]

        @pl.when(tiles >= 1)
        def _():
            for copy in loads(0):
                copy.start()

        for copy in weights[j]:
            copy.wait()

        def tile_step(i, carry):
            slot = lax.rem(i, 2)

            @pl.when(i + 1 < tiles)
            def _():
                for copy in loads(i + 1):
                    copy.start()

            @pl.when(i >= 2)
            def _():
                for copy in saves(i - 2):
                    copy.wait()

            for copy in loads(i):
                copy.wait()
            f = f_rows[j, tile_at(i), :].astype(f32)
            shares = probs[slot]
            mine = lane == e_ref[j]
            gate = jnp.sum(jnp.where(mine, shares, 0.0), axis=-1, keepdims=True)
            wide = gate * f
            pg[slot] = wide.astype(bf16)
            gate_grad = jnp.sum(f * y[slot].astype(f32), axis=-1, keepdims=True)
            logit = gate_grad * gate * (jnp.where(mine, 1.0, 0.0) - shares)
            high = logit.astype(bf16)
            rest = (logit - high.astype(f32)).astype(bf16)
            outer_grad[j : j + 1] += jnp.sum(wide, axis=0, keepdims=True)
            for k in range(n):
                columns = slice(k * hidden_width, (k + 1) * hidden_width)
                grad = dot_last(pg[slot], down[j, k]) * slope[slot, :, columns].astype(f32)
                hg[slot, :, columns] = grad.astype(bf16)
                inner_grad[j : j + 1, columns] += jnp.sum(grad, axis=0, keepdims=True)
            for copy in saves(i):
                copy.start()
            turned = x[slot].T
            router_grad[...] += dot(turned, high) + dot(turned, rest)
            acc = dot_last(high, router[...]) + dot_last(rest, router[...])
            for k in range(n):
                acc = acc + dot_last(hg[slot, :, k * hidden_width : (k + 1) * hidden_width], up[j, k])
            b_rows[j, tile_at(i), :] = acc.astype(bf16)
            return carry

        lax.fori_loop(0, tiles, tile_step, 0)
        drain(saves, tiles)
        b_rows[j, tile_at(tiles), :] = jnp.zeros((MLP, width), bf16)
    scatter_rows(group, counts, places, b_rows, outs, staged, leave_sems, starts, total)


def expert_backward(scalars, pos, places, sources, dense, tiles, saved, group, capacity, router_lane):
    n = len(dense)
    width = sources[0].shape[1]
    tokens = pos.shape[1]
    hidden = (tiles[0].shape[0] - ROW) // 2
    rows = expert_rows(group, capacity)
    return pl.pallas_call(
        functools.partial(expert_backward_kernel, n, group, router_lane),
        name="expert_backward",
        out_shape=[jax.ShapeDtypeStruct((tokens, width), bf16)] * group
        + [
            jax.ShapeDtypeStruct((2, rows, width), bf16),
            jax.ShapeDtypeStruct((2, rows, hidden * n), bf16),
            jax.ShapeDtypeStruct((width, LANES), f32),
            jax.ShapeDtypeStruct((8, hidden * n), f32),
            jax.ShapeDtypeStruct((8, width), f32),
        ],
        in_specs=[SMEM_SPEC] * 3 + [VMEM_SPEC] * 2 + [ANY_SPEC] * (group + 3 * n + 4),
        out_specs=[ANY_SPEC] * (group + 2) + [VMEM_SPEC] * 3,
        scratch_shapes=[
            pltpu.VMEM((group, tokens, width), bf16),
            pltpu.VMEM((2, n, width, hidden), bf16),
            pltpu.VMEM((2, n, hidden, width), bf16),
            pltpu.VMEM((2, n, ROW, width), bf16),
            pltpu.VMEM((width, LANES), bf16),
            pltpu.VMEM((2, rows, width), bf16),
            pltpu.VMEM((2, rows, width), bf16),
            pltpu.VMEM((tokens, width), f32),
            pltpu.VMEM((2, tokens, width), bf16),
            pltpu.VMEM((2, MLP, hidden * n), bf16),
            pltpu.VMEM((2, MLP, width), bf16),
            pltpu.VMEM((2, MLP, hidden * n), bf16),
            pltpu.VMEM((2, MLP, width), bf16),
            pltpu.VMEM((2, MLP, width), bf16),
            pltpu.VMEM((2, MLP, LANES), f32),
            pltpu.SemaphoreType.DMA((3, width // hidden + 2, n)),
            pltpu.SemaphoreType.DMA((group,)),
            pltpu.SemaphoreType.DMA((2,)),
            pltpu.SemaphoreType.DMA((2, 2)),
            pltpu.SemaphoreType.DMA((4, 2)),
        ],
        compiler_params=params(),
        cost_estimate=cost(BACKWARD_US),
    )(*scalars, pos, places, *sources, *dense, *tiles, *saved)


def put_columns(shard, k, n, source, row, into):
    width = source.shape[1] // n
    if width % LANES == 0:
        base = pl.multiple_of((shard ^ k) * width, width)
        into[:, 0:width] = source[row : row + 1, pl.ds(base, width)].astype(into.dtype)
        return
    for place in range(n):

        @pl.when((shard ^ k) == place)
        def _():
            into[:, 0:width] = source[row : row + 1, place * width : (place + 1) * width].astype(into.dtype)


def weight_grads_kernel(n, experts, added, shard_ref, tiles_ref, *refs):
    saved, inner_part, outer_part, refs = refs[:4], refs[4], refs[5], refs[6:]
    before, refs = refs[:added], refs[added:]
    results, refs = refs[: 2 * len(experts)], refs[2 * len(experts) :]
    x, pg, act, hg, up_total, down_total, row, sems = refs
    width, hidden = up_total.shape[1:]
    folds = width // hidden
    shard = shard_ref[0]
    for turn, j in enumerate(experts):
        tiles = tiles_ref[j]
        for k in range(n):
            up_total[k] = jnp.zeros((width, hidden), f32)
            down_total[k] = jnp.zeros((width, hidden), f32)

        def loads(i, j=j):
            slot = lax.rem(i, 2)
            return [
                pltpu.make_async_copy(source.at[j, tile_at(i)], into.at[slot], sems.at[m, slot])
                for m, (source, into) in enumerate(zip(saved, (x, pg, act, hg)))
            ]

        @pl.when(tiles >= 1)
        def _():
            for copy in loads(0):
                copy.start()

        def tile_step(i, carry):
            slot = lax.rem(i, 2)

            @pl.when(i + 1 < tiles)
            def _():
                for copy in loads(i + 1):
                    copy.start()

            for copy in loads(i):
                copy.wait()
            turned = x[slot].T
            turned_grad = pg[slot].T
            for k in range(n):
                columns = slice(k * hidden, (k + 1) * hidden)
                up_total[k] += dot(turned, hg[slot, :, columns])
                down_total[k] += dot(turned_grad, act[slot, :, columns])
            return carry

        lax.fori_loop(0, tiles, tile_step, 0)
        row[8:16] = outer_part[...]
        for k in range(n):
            into = results[2 * turn + 1 - k % 2].at[k // 2]
            base = before[2 * turn + 1 - k % 2].at[k // 2] if added else None

            def put(rows, columns, value):
                if added:
                    value = value + base[rows, columns].astype(f32)
                into[rows, columns] = value.astype(bf16)

            for fold in range(folds):
                at = slice(fold * hidden, (fold + 1) * hidden)
                put(slice(0, hidden), at, up_total[k, at])
            put(slice(hidden, 2 * hidden), slice(0, width), down_total[k].T)
            row[0:8] = jnp.zeros((8, width), f32)
            row[0:1, 0:hidden] = inner_part[j : j + 1, k * hidden : (k + 1) * hidden]
            put_columns(shard, k, n, row, 8 + j, row.at[1:2])
            row[8:16] = outer_part[...]
            put(slice(2 * hidden, 2 * hidden + 8), slice(0, width), row[0:8])
            into[2 * hidden + 8 : 2 * hidden + ROW] = jnp.zeros((ROW - 8, width), bf16)


def weight_grads(experts, shard, tiles, saved, biases, n, before=()):
    _, rows, width = saved[0].shape
    hidden = saved[2].shape[2] // n
    shape = jax.ShapeDtypeStruct((n // 2, 2 * hidden + ROW, width), bf16)
    return pl.pallas_call(
        functools.partial(weight_grads_kernel, n, experts, len(before)),
        name="weight_grads",
        out_shape=(shape,) * (2 * len(experts)),
        in_specs=[SMEM_SPEC] * 2 + [ANY_SPEC] * 4 + [VMEM_SPEC] * (2 + len(before)),
        out_specs=(VMEM_SPEC,) * (2 * len(experts)),
        scratch_shapes=[
            pltpu.VMEM((2, MLP, width), bf16),
            pltpu.VMEM((2, MLP, width), bf16),
            pltpu.VMEM((2, MLP, hidden * n), bf16),
            pltpu.VMEM((2, MLP, hidden * n), bf16),
            pltpu.VMEM((n, width, hidden), f32),
            pltpu.VMEM((n, width, hidden), f32),
            pltpu.VMEM((ROW, width), f32),
            pltpu.SemaphoreType.DMA((4, 2)),
        ],
        compiler_params=params(),
        cost_estimate=cost(8 * len(experts)),
    )(shard, tiles, *saved, *biases, *before)


def norm_backward(rows, gain, grad):
    centered, rate = normalise(rows)
    unit = centered * rate
    scaled = grad * gain
    back = rate * (
        scaled
        - jnp.mean(scaled, axis=-1, keepdims=True)
        - unit * jnp.mean(scaled * unit, axis=-1, keepdims=True)
    )
    return (
        back,
        jnp.sum(grad * unit, axis=0, keepdims=True),
        jnp.sum(grad, axis=0, keepdims=True),
        unit,
    )


def attention_backward_kernel(n_tiles, parts, base, images, overlap, last, *refs):
    shard_ref, refs = refs[0], refs[1:]
    grads, refs = refs[:parts], refs[parts:]
    fg, res, att, qkv, weights, tok = refs[:6]
    dense, refs = refs[6 : 6 + n_tiles], refs[6 + n_tiles :]
    before = None
    if overlap:
        before, refs = refs[:4], refs[4:]
    if last:
        router_parts, refs = refs[:last], refs[last:]
        token_grad, norm_grad, send, keep = refs[:4]
        mixer_grad, merge_grad = refs[-2:]
        refs = refs[:-2]
    else:
        token_grad, mixer_grad, merge_grad, norm_grad = refs[:4]
    mixer, merge, normt, norms, dres, low, datt, normed, mg, sems = refs[4:]
    shard = shard_ref[0]
    width = tok.shape[1]
    n_rows = tok.shape[0]
    copies = place_dense(shard, dense, mixer, merge, normt, sems)
    for copy in copies:
        copy.start()
    for copy in copies:
        copy.wait()
    place_norms(shard, normt, norms)
    norm_grad[...] = before[3][...] if overlap else jnp.zeros(norm_grad.shape, f32)
    for rows in row_tiles(n_rows):
        grad = grads[0][rows].astype(f32)
        for other in grads[1:]:
            grad = grad + other[rows].astype(f32)
        back, gain, shift, _ = norm_backward(res[rows], norms[1:2], grad)
        norm_grad[1:2] += gain
        norm_grad[3:4] += shift
        total = fg[rows] + back
        dres[rows] = total
        low[rows] = total.astype(bf16)
        datt[rows] = dot_last(low[rows], merge[...]).astype(bf16)
    mg[...] = jnp.zeros(mg.shape, bf16)
    merge_term = dot_first(att[...], low[...])
    merge_grad[...] = before[2][...] + merge_term if overlap else merge_term
    lane = lax.broadcasted_iota(jnp.int32, (1, LANES), 1)

    def image_step(image, carry):
        start, _, _ = image_window(base, image)
        window = pl.ds(start, WIN)
        for slab in range(width // LANES):
            q_at = slice(slab * LANES, (slab + 1) * LANES)
            k_at = slice(width + slab * LANES, width + (slab + 1) * LANES)
            v_at = slice(2 * width + slab * LANES, 2 * width + (slab + 1) * LANES)
            q, k, v = qkv[window, q_at], qkv[window, k_at], qkv[window, v_at]
            do = datt[window, q_at]
            parts = []
            for half in range(2):
                head = 2 * slab + half
                mine = (lane >= half * HEAD_DIM) & (lane < (half + 1) * HEAD_DIM)
                zero = jnp.zeros_like(q)
                low = weights[image, head]
                dv = dot_first(low, do)
                dw = dot_last(jnp.where(mine, do, zero), v)
                wide = low.astype(f32)
                inner = jnp.sum(wide * dw, axis=-1, keepdims=True)
                ds = (wide * (dw - inner)).astype(bf16)
                parts.append((dot(ds, k) * SCALING, dot_first(ds, q) * SCALING, dv))
            for at, first, second in zip((q_at, k_at, v_at), parts[0], parts[1]):
                both = jnp.where(lane < HEAD_DIM, first, second).astype(bf16)
                mg[window, at] = mg[window, at] + both
        return carry

    lax.fori_loop(0, images, image_step, 0)
    shift_rows = token_grad.shape[0] - n_rows if overlap else 0
    if overlap:
        token_grad[0:shift_rows] = before[0][0:shift_rows]
    for rows in row_tiles(n_rows):
        grad = dot_last(mg[rows], mixer[...])
        back, gain, shift, unit = norm_backward(tok[rows].astype(f32), norms[0:1], grad)
        norm_grad[0:1] += gain
        norm_grad[2:3] += shift
        total = dres[rows] + back
        if overlap and rows.start < overlap:
            both = before[0][shift_rows : shift_rows + overlap]
            token_grad[shift_rows : shift_rows + overlap] = total[0:overlap] + both
            token_grad[shift_rows + overlap : shift_rows + rows.stop] = total[overlap:]
        else:
            token_grad[shift_rows + rows.start : shift_rows + rows.stop] = total
        normed[rows] = (unit * norms[0:1] + norms[2:3]).astype(bf16)
    for c in range(3):
        columns = slice(c * width, (c + 1) * width)
        term = dot_first(normed[...], mg[:, columns])
        mixer_grad[:, columns] = before[1][:, columns] + term if overlap else term
    if last:
        for k in range(n_tiles):
            own = width // n_tiles
            at = pl.ds(pl.multiple_of((shard ^ k) * own, own), own)
            into = (send if k % 2 else keep).at[k // 2]
            into[:, 0 : 3 * width] = mixer_grad[at].astype(bf16)
            into[:, 3 * width : 4 * width] = merge_grad[at].astype(bf16)
            into[:, 4 * width : 4 * width + LANES] = sum(part[at] for part in router_parts).astype(bf16)


def attention_backward(shard, grads, fg, res, att, qkv, weights, tok, dense, base, images, before, start, router_parts):
    rows, width = tok.shape
    n = len(dense)
    overlap = before[0].shape[0] - start if before else 0
    token_shape = jax.ShapeDtypeStruct((start + rows if before else rows, width), f32)
    norm_shape = jax.ShapeDtypeStruct((8, width), f32)
    totals = [pltpu.VMEM((width, 3 * width), f32), pltpu.VMEM((width, width), f32)]
    if router_parts:
        tile = jax.ShapeDtypeStruct((n // 2, width // n, 4 * width + LANES), bf16)
        shapes = (token_shape, norm_shape, tile, tile)
    else:
        shapes = (
            token_shape,
            jax.ShapeDtypeStruct((width, 3 * width), f32),
            jax.ShapeDtypeStruct((width, width), f32),
            norm_shape,
        )
    held = (*grads, fg, res, att, qkv, weights, tok)
    more = (*(before or ()), *router_parts)
    return pl.pallas_call(
        functools.partial(
            attention_backward_kernel, n, len(grads), base, images, overlap, len(router_parts)
        ),
        name="attention_backward",
        out_shape=shapes,
        in_specs=[SMEM_SPEC] + [VMEM_SPEC] * len(held) + [ANY_SPEC] * n + [VMEM_SPEC] * len(more),
        out_specs=(VMEM_SPEC,) * 4,
        scratch_shapes=[
            pltpu.VMEM((width, 3 * width), bf16),
            pltpu.VMEM((width, width), bf16),
            pltpu.VMEM((n, ROW, LANES), bf16),
            pltpu.VMEM((8, width), f32),
            pltpu.VMEM((rows, width), f32),
            pltpu.VMEM((rows, width), bf16),
            pltpu.VMEM((rows, width), bf16),
            pltpu.VMEM((rows, width), bf16),
            pltpu.VMEM((rows, 3 * width), bf16),
            pltpu.SemaphoreType.DMA((3 * n,)),
        ]
        + (totals if router_parts else []),
        compiler_params=params(),
        cost_estimate=cost(17),
    )(shard, *held, *dense, *more)


def bits_of(ways):
    bit = ways // 2
    while bit:
        yield bit
        bit //= 2


def gather_tiles(array, axis, ways, gate=None):
    tiles = {0: array}
    for step, bit in enumerate(bits_of(ways)):
        for k in list(tiles):
            sent = after(tiles[k], *gate) if gate is not None and step else tiles[k]
            tiles[k | bit] = swap(sent, axis, ways, bit)
    return [tiles[k] for k in range(ways)]


def fold_tiles(send, keep, axis, ways):
    sums = (keep.astype(f32) + swap(send, axis, ways, 1).astype(f32)).astype(bf16)

    def rest():
        tiles = sums
        for bit in [bit for bit in reversed(list(bits_of(ways))) if bit > 1]:
            tiles = (tiles[0::2].astype(f32) + swap(tiles[1::2], axis, ways, bit).astype(f32)).astype(bf16)
        return tiles[0]

    return sums, rest


def sum_over(array, axis, ways):
    for bit in bits_of(ways):
        array = array + swap(array, axis, ways, bit)
    return array


def sum_split(array, axis, ways, index, gate, last_gate):
    half = array.shape[0] // 2
    mine = index & 1
    kept = lax.dynamic_slice_in_dim(array, mine * half, half, 0)
    sent = lax.dynamic_slice_in_dim(array, (1 - mine) * half, half, 0)
    part = after(kept.astype(f32) + swap(sent, axis, ways, 1).astype(f32), gate)
    for bit in [bit for bit in reversed(list(bits_of(ways))) if bit > 1]:
        low = part.astype(bf16)
        part = low.astype(f32) + swap(low, axis, ways, bit).astype(f32)
    low = after(part.astype(bf16), last_gate)
    other = swap(low, axis, ways, 1)
    first = jnp.where(mine == 0, low, other)
    second = jnp.where(mine == 0, other, low)
    return jnp.concatenate([first, second], axis=0).astype(f32)


def exchange(array, ways, group):
    return [array] + [swap(array, "expert", ways, b) for b in range(1, group)]


def give_back(blocks, ways, group):
    return [blocks[0]] + [swap(blocks[b], "expert", ways, b) for b in range(1, group)]


def after(value, *others):
    return lax.optimization_barrier((value, *others))[0]


def per_device(
    tokens,
    teacher,
    valid_mask,
    routes,
    mixer_weight,
    merge_weight,
    router_weight,
    norm_gain,
    norm_shift,
    up_weight,
    inner_bias,
    down_weight,
    outer_bias,
):
    ways = lax.axis_size("expert")
    shards = lax.axis_size("shard")
    shard = lax.axis_index("shard").astype(jnp.int32)
    expert = lax.axis_index("expert").astype(jnp.int32)
    token_count, width = tokens.shape
    images = token_count // SEQ
    experts = router_weight.shape[1]
    group = ways // 2
    chunks = 2 if images % 2 == 0 else 1
    chunk_images = images // chunks
    chunk_tokens = chunk_images * SEQ
    capacity = min(chunk_tokens, max(2, 4 * token_count // experts))
    firsts = [c * chunk_tokens for c in range(chunks)]
    starts = [first // 8 * 8 for first in firsts]
    last = max(first - start + (chunk_images - 1) * SEQ for first, start in zip(firsts, starts))
    rows = up_to(last // ROW * ROW + WIN, ROW)
    all_rows = starts[-1] + rows
    shard_rows = width // shards
    hidden = up_weight.shape[2]
    router_lane = 4 * width
    folds = width // hidden

    dense_own, near = pack(
        mixer_weight, merge_weight, router_weight, norm_gain, norm_shift, up_weight, inner_bias, down_weight, outer_bias
    )
    dense = gather_tiles(dense_own, "shard", shards)
    far = swap(near, "expert", ways, group)

    route_rows = jnp.pad(routes, ((0, all_rows - token_count), (0, 0)), constant_values=-1).T
    ids = jnp.arange(experts, dtype=jnp.int32)[:, None]
    named = (route_rows[0:1] == ids) | (route_rows[1:2] == ids)
    order = jnp.arange(all_rows, dtype=jnp.int32)
    in_chunk = (order[None, :] // chunk_tokens) == jnp.arange(chunks, dtype=jnp.int32)[:, None]
    named = (named[None] & in_chunk[:, None, :]).reshape(chunks * experts, all_rows)
    earlier = (order[:, None] < order[None, :]).astype(bf16)
    slots = jnp.dot(named.astype(bf16), earlier, preferred_element_type=f32).astype(jnp.int32)
    slots = jnp.where(named, slots, -1)
    slots = jnp.pad(slots, ((0, 8), (0, 0)), constant_values=jnp.sum(valid_mask))
    slot_blocks = jnp.stack([slots] + [swap(slots, "expert", ways, b) for b in range(1, group)])
    group_count = jnp.sum(slot_blocks[:, -8:, 0:LANES], axis=0).astype(f32)
    slot_blocks = slot_blocks[:, :-8].reshape(group, chunks, experts, all_rows)
    chosen = jnp.concatenate(
        [
            lax.dynamic_slice_in_dim(slot_blocks, expert, 1, 2),
            lax.dynamic_slice_in_dim(slot_blocks, expert ^ group, 1, 2),
        ],
        axis=2,
    )
    shard_id = shard[None]
    e_ids = jnp.stack([expert, expert ^ group])
    routing, tile_counts = [], []
    for c in range(chunks):
        pos = chosen[:, c, :, starts[c] : starts[c] + rows].reshape(2 * group, rows)
        counts = jnp.max(pos, axis=1) + 1
        places = jnp.pad(pos.T, ((0, 0), (0, LANES - 2 * group)), constant_values=-1)
        ends = jnp.sum((counts.reshape(group, 2) + ROW - 1) // ROW * ROW, axis=0)
        tile_counts.append((ends + MLP - 1) // MLP)
        routing.append(((shard_id, e_ids, counts), pos, places))

    def chunk_rows(array, c):
        part = array[starts[c] : min(starts[c] + rows, token_count)]
        return jnp.pad(part, ((0, rows - part.shape[0]),) + ((0, 0),) * (part.ndim - 1))

    toks = [chunk_rows(tokens, c) for c in range(chunks)]
    local = jnp.arange(rows, dtype=jnp.int32)[:, None]
    kept, valids = [], []
    for c in range(chunks):
        base = firsts[c] - starts[c]
        mask = (local >= base) & (local < base + chunk_tokens)
        kept.append(mask)
        valids.append(jnp.where(mask, chunk_rows(valid_mask, c).astype(f32)[:, None], 0.0))

    forward = []
    for c in range(chunks):
        gates = (forward[-1][4],) if c else (chosen,)
        forward.append(
            attention_forward(shard_id, after(toks[c], *gates), dense, firsts[c] - starts[c], chunk_images)
        )
    attended = forward[-1][4]
    given, experts_saved = [], []
    for c in range(chunks):
        arrived = exchange(forward[c][4] if c == 0 else after(forward[c][4], tiles[-2]), ways, group)
        if c == 0:
            near_tiles = gather_tiles(after(near, dense[-1]), "shard", shards, (attended, *arrived[1:]))
            far_tiles = gather_tiles(
                after(far, *arrived[1:], *near_tiles[1:]), "shard", shards
            )
            tiles = near_tiles + far_tiles
            group_count = after(group_count, far)
            valid_count = group_count + swap(group_count, "expert", ways, group)
            valid_count = sum_over(valid_count, "shard", shards)[0, 0]
            scale = token_count * ways * shards / valid_count
        if c:
            arrived[0] = after(arrived[0], given[-1][0])
        results = expert_forward(*routing[c], arrived, dense, tiles, group, experts, capacity, router_lane)
        given.append(results[:group])
        experts_saved.append(results[group:])

    blocks_out, squared, final_grads, input_grads = [], 0.0, [], []
    router_parts, biases, saved, early = [], [], [], ()
    arrived = None
    for c in range(chunks):
        parts = given[c] if c == 0 else [given[c][0]] + [after(part, *arrived) for part in given[c][1:]]
        block_out = forward[c][3]
        if c == 0:
            block_out = after(block_out, given[-1][0])
        for part in give_back(parts, ways, group):
            block_out = block_out + part.astype(f32)
        error = block_out - chunk_rows(teacher, c).astype(f32)
        squared = squared + jnp.sum(valids[c] * jnp.sum(error * error, axis=1, keepdims=True))
        fg = scale * valids[c] * error
        final_grads.append(fg)
        blocks_out.append(jnp.where(kept[c], block_out, 0.0).astype(bf16))
        arrived = exchange(fg.astype(bf16), ways, group)
        if c:
            early = weight_grads(
                (0, 1), shard_id, after(tile_counts[c - 1], fg), saved[c - 1], biases[c - 1], shards, early
            )
            arrived[0] = after(arrived[0], early[0])
            input_grads[c - 1] = [input_grads[c - 1][0]] + [
                after(part, *arrived[1:]) for part in input_grads[c - 1][1:]
            ]
            input_grads[c - 1] = give_back(input_grads[c - 1], ways, group)
        x_rows, y_rows, probs_rows, act, slope = experts_saved[c]
        results = expert_backward(
            *routing[c],
            arrived,
            dense,
            tiles,
            (x_rows, y_rows, probs_rows, slope),
            group,
            capacity,
            router_lane,
        )
        input_grads.append(results[:group])
        pg_rows, hg, router_part, inner_part, outer_part = results[group:]
        router_parts.append(router_part)
        biases.append((inner_part, outer_part))
        saved.append((x_rows, pg_rows, act, hg))
    last = chunks - 1
    far_tiles = weight_grads(
        (1,), shard_id, after(tile_counts[last], *input_grads[0][1:]), saved[last], biases[last], shards, early[2:]
    )
    input_grads[last] = give_back(input_grads[last], ways, group)
    far_sums, far_rest = fold_tiles(*far_tiles, "shard", shards)
    before = None
    for c in range(chunks):
        qkv, att, weights, res, _ = forward[c]
        gate = far_sums if c == 0 else far_grad
        before = attention_backward(
            after(shard_id, gate),
            input_grads[c],
            final_grads[c],
            res,
            att,
            qkv,
            weights,
            toks[c],
            dense,
            firsts[c] - starts[c],
            chunk_images,
            before,
            starts[c],
            router_parts if c == last else (),
        )
        if c == 0:
            far_grad = far_rest()
            far_arrived = [
                swap(half, "expert", ways, group) for half in (far_grad[:hidden], far_grad[hidden:])
            ]
    token_grad, norm_part, *dense_parts = before
    dense_parts[0] = after(dense_parts[0], far_arrived[0])
    dense_sums, dense_rest = fold_tiles(*dense_parts, "shard", shards)
    near_tiles = weight_grads(
        (0,), shard_id, after(tile_counts[last], dense_sums), saved[last], biases[last], shards, early[:2]
    )
    dense_grad = dense_rest()
    near_tiles = (after(near_tiles[0], dense_grad, far_arrived[1]), near_tiles[1])
    near_sums, near_rest = fold_tiles(*near_tiles, "shard", shards)
    near_grad = near_rest()
    up_sum = near_grad[:hidden].astype(f32) + far_arrived[0].astype(f32)
    up_grad = jnp.concatenate(
        [up_sum[:, fold * hidden : (fold + 1) * hidden] for fold in range(folds)], axis=0
    )
    rest_sum = near_grad[hidden:].astype(f32) + far_arrived[1].astype(f32)
    down_grad = rest_sum[:hidden]
    inner_grad = rest_sum[hidden : hidden + 1, 0:hidden]
    outer_grad = rest_sum[hidden + 1 : hidden + 2, 0:shard_rows]
    dense_sum = sum_split(dense_grad, "expert", ways, expert, near_sums, near_grad)
    output = jnp.zeros((all_rows, width), bf16)
    for c in range(chunks):
        output = output + jnp.pad(blocks_out[c], ((starts[c], all_rows - starts[c] - rows), (0, 0)))

    norm_sum = sum_over(sum_over(norm_part.at[4].set(squared), "shard", shards), "expert", ways)
    norm_sum = lax.dynamic_slice_in_dim(norm_sum, shard * shard_rows, shard_rows, 1)
    loss_value = norm_sum[4, 0] / (2.0 * valid_count)
    return (
        output[:token_count],
        loss_value,
        token_grad[:token_count],
        dense_sum[:, : 3 * width],
        dense_sum[:, 3 * width : 4 * width],
        dense_sum[:, 4 * width : 4 * width + experts],
        norm_sum[0:2],
        norm_sum[2:4],
        up_grad[None],
        inner_grad,
        down_grad[None],
        outer_grad,
    )


def solution(mesh):
    in_specs = (
        P(("expert", "shard"), None),
        P(("expert", "shard"), None),
        P(("expert", "shard")),
        P(("expert", "shard"), None),
        P("shard", None),
        P("shard", None),
        P("shard", None),
        P(None, "shard"),
        P(None, "shard"),
        P("expert", None, "shard"),
        P("expert", "shard"),
        P("expert", "shard", None),
        P("expert", "shard"),
    )
    out_specs = (
        P(("expert", "shard"), None),
        P(),
        P(("expert", "shard"), None),
        P("shard", None),
        P("shard", None),
        P("shard", None),
        P(None, "shard"),
        P(None, "shard"),
        P("expert", None, "shard"),
        P("expert", "shard"),
        P("expert", "shard", None),
        P("expert", "shard"),
    )
    return jax.shard_map(
        per_device, mesh=mesh, in_specs=in_specs, out_specs=out_specs, check_vma=False
    )
```

```python
import functools

import jax
import jax.numpy as jnp
from jax import lax
from jax.experimental import pallas as pl
from jax.experimental.pallas import tpu as pltpu
from jax.sharding import PartitionSpec as P

HEADS = 8
HEAD_DIM = 64
SEQ = 197
EPS = 1e-06
ROW = 16
WIN = 208
TILE = 160
GATHER = 208
MLP = 256
SCATTER = 256
LANES = 128
NEG = -1e30
SCALING = HEAD_DIM ** (-0.5)
GELU_C = 0.7978845608028654
GELU_K = 0.044715
f32 = jnp.float32
bf16 = jnp.bfloat16
VMEM_SPEC = pl.BlockSpec(memory_space=pltpu.VMEM)
SMEM_SPEC = pl.BlockSpec(memory_space=pltpu.SMEM)
ANY_SPEC = pl.BlockSpec(memory_space=pl.ANY)
VMEM_LIMIT = 60 * 1024 * 1024
FORWARD_US = 20
BACKWARD_US = 20


def up_to(value, step):
    return (value + step - 1) // step * step


def dot(left, right):
    return jnp.dot(left, right, preferred_element_type=f32)


def dot_last(left, right):
    return lax.dot_general(left, right, (((1,), (1,)), ((), ())), preferred_element_type=f32)


def dot_first(left, right):
    return lax.dot_general(left, right, (((0,), (0,)), ((), ())), preferred_element_type=f32)


def swap(array, axis, ways, bit):
    return lax.ppermute(array, axis, [(i, i ^ bit) for i in range(ways)])


def cost(microseconds):
    return pl.CostEstimate(
        flops=int(microseconds * 1.15e9), bytes_accessed=1 << 20, transcendentals=0
    )


def params():
    return pltpu.CompilerParams(vmem_limit_bytes=VMEM_LIMIT)


def normalise(rows):
    mean = jnp.mean(rows, axis=-1, keepdims=True)
    centered = rows - mean
    variance = jnp.mean(centered * centered, axis=-1, keepdims=True)
    return centered, lax.rsqrt(variance + EPS)


def place_dense(shard, tiles, mixer, merge, normt, sems):
    copies = []
    columns = mixer.shape[1]
    last = tiles[0].shape[1] - LANES
    for k, tile in enumerate(tiles):
        copies.append(
            pltpu.make_async_copy(
                tile.at[0:ROW, last : last + LANES], normt.at[k], sems.at[2 * len(tiles) + k]
            )
        )
    for k, tile in enumerate(tiles):
        rows = tile.shape[0]
        base = pl.multiple_of((shard ^ k) * rows, rows)
        copies.append(
            pltpu.make_async_copy(
                tile.at[:, 0:columns], mixer.at[pl.ds(base, rows)], sems.at[2 * k]
            )
        )
        copies.append(
            pltpu.make_async_copy(
                tile.at[:, columns : columns + merge.shape[1]],
                merge.at[pl.ds(base, rows)],
                sems.at[2 * k + 1],
            )
        )
    return copies


def place_columns(shard, smalls, into, first):
    width = into.shape[1] // len(smalls)
    for k, small in enumerate(smalls):
        if width % LANES == 0:
            base = pl.multiple_of((shard ^ k) * width, width)
            into[:, pl.ds(base, width)] = small[:, first : first + width]
            continue
        for place in range(len(smalls)):

            @pl.when((shard ^ k) == place)
            def _():
                into[:, place * width : (place + 1) * width] = small[:, first : first + width]


def place_norms(shard, normt, norms):
    tiles = [normt[k][0:8].astype(f32) for k in range(normt.shape[0])]
    place_columns(shard, tiles, norms, 0)


def pack_kernel(mixer, merge, router, gain, shift, up, inner, down, outer, dense, near, row, sems):
    columns, width = mixer.shape[1], merge.shape[1]
    own, hidden = gain.shape[1], up.shape[2]
    last = columns + width
    moves = [
        (mixer, dense.at[:, 0:columns]),
        (merge, dense.at[:, columns:last]),
        (down.at[0], near.at[hidden : 2 * hidden]),
    ]
    for fold in range(width // hidden):
        at = slice(fold * hidden, (fold + 1) * hidden)
        moves.append((up.at[0, at], near.at[0:hidden, at]))
    copies = [pltpu.make_async_copy(source, into, sems.at[i]) for i, (source, into) in enumerate(moves)]
    for copy in copies:
        copy.start()
    dense[:, last : last + 2 * LANES] = jnp.zeros((dense.shape[0], 2 * LANES), bf16)
    dense[:, last : last + router.shape[1]] = router[...]
    row[...] = jnp.zeros(row.shape, f32)
    row[0:2, 0:own] = gain[...].astype(f32)
    row[2:4, 0:own] = shift[...].astype(f32)
    dense[0:ROW, last + LANES : last + 2 * LANES] = row[:, 0:LANES].astype(bf16)
    row[...] = jnp.zeros(row.shape, f32)
    row[0:1, 0:hidden] = inner[...].astype(f32)
    row[1:2, 0:own] = outer[...].astype(f32)
    near[2 * hidden : 2 * hidden + ROW] = row[...].astype(bf16)
    for copy in copies:
        copy.wait()


def pack(mixer, merge, router, gain, shift, up, inner, down, outer):
    own, width = merge.shape
    hidden = up.shape[2]
    return pl.pallas_call(
        pack_kernel,
        name="pack",
        out_shape=(
            jax.ShapeDtypeStruct((own, mixer.shape[1] + width + 2 * LANES), bf16),
            jax.ShapeDtypeStruct((2 * hidden + ROW, width), bf16),
        ),
        in_specs=[ANY_SPEC] * 2 + [VMEM_SPEC] * 3 + [ANY_SPEC, VMEM_SPEC, ANY_SPEC, VMEM_SPEC],
        out_specs=(VMEM_SPEC, VMEM_SPEC),
        scratch_shapes=[
            pltpu.VMEM((ROW, width), f32),
            pltpu.SemaphoreType.DMA((3 + width // hidden,)),
        ],
        compiler_params=params(),
        cost_estimate=cost(2),
    )(mixer, merge, router, gain, shift, up, inner, down, outer)


def row_tiles(rows):
    return [slice(first, min(first + TILE, rows)) for first in range(0, rows, TILE)]


def image_window(base, image):
    first = base + image * SEQ
    start = pl.multiple_of(first // ROW * ROW, ROW)
    offset = first - start
    rows = lax.broadcasted_iota(jnp.int32, (WIN, 1), 0)
    columns = lax.broadcasted_iota(jnp.int32, (1, WIN), 1)
    row_in = (rows >= offset) & (rows < offset + SEQ)
    column_in = (columns >= offset) & (columns < offset + SEQ)
    return start, row_in, column_in


def attention_forward_kernel(n_tiles, base, images, *refs):
    shard_ref, tok = refs[0], refs[1]
    dense = refs[2 : 2 + n_tiles]
    qkv, att, weights, res, normed_two, mixer, merge, normt, norms, sems = refs[2 + n_tiles :]
    shard = shard_ref[0]
    width = tok.shape[1]
    copies = place_dense(shard, dense, mixer, merge, normt, sems)
    for copy in copies:
        copy.start()
    for copy in copies:
        copy.wait()
    place_norms(shard, normt, norms)
    for rows in row_tiles(tok.shape[0]):
        centered, rate = normalise(tok[rows].astype(f32))
        normed = (centered * rate * norms[0:1] + norms[2:3]).astype(bf16)
        qkv[rows] = dot(normed, mixer[...]).astype(bf16)
    att[...] = jnp.zeros(att.shape, bf16)
    lane = lax.broadcasted_iota(jnp.int32, (1, LANES), 1)

    def image_step(image, carry):
        start, row_in, column_in = image_window(base, image)
        window = pl.ds(start, WIN)
        for slab in range(width // LANES):
            q = qkv[window, slab * LANES : (slab + 1) * LANES]
            k = qkv[window, width + slab * LANES : width + (slab + 1) * LANES]
            v = qkv[window, 2 * width + slab * LANES : 2 * width + (slab + 1) * LANES]
            outs = []
            for half in range(2):
                mine = (lane >= half * HEAD_DIM) & (lane < (half + 1) * HEAD_DIM)
                scores = dot_last(jnp.where(mine, q, jnp.zeros_like(q)), k) * SCALING
                scores = jnp.where(column_in, scores, NEG)
                top = jnp.max(scores, axis=-1, keepdims=True)
                powers = jnp.exp(scores - top)
                total = jnp.sum(powers, axis=-1, keepdims=True)
                low = (powers * jnp.where(row_in, 1.0 / total, 0.0)).astype(bf16)
                weights[image, 2 * slab + half] = low
                outs.append(dot(low, v))
            out = jnp.where(lane < HEAD_DIM, outs[0], outs[1]).astype(bf16)
            columns = slice(slab * LANES, (slab + 1) * LANES)
            att[window, columns] = att[window, columns] + out
        return carry

    lax.fori_loop(0, images, image_step, 0)
    for rows in row_tiles(tok.shape[0]):
        residual = tok[rows].astype(f32) + dot(att[rows], merge[...])
        res[rows] = residual
        centered, rate = normalise(residual)
        normed_two[rows] = (centered * rate * norms[1:2] + norms[3:4]).astype(bf16)


def attention_forward(shard, tok, dense, base, images):
    rows, width = tok.shape
    n = len(dense)
    return pl.pallas_call(
        functools.partial(attention_forward_kernel, n, base, images),
        name="attention_forward",
        out_shape=(
            jax.ShapeDtypeStruct((rows, 3 * width), bf16),
            jax.ShapeDtypeStruct((rows, width), bf16),
            jax.ShapeDtypeStruct((images, HEADS, WIN, WIN), bf16),
            jax.ShapeDtypeStruct((rows, width), f32),
            jax.ShapeDtypeStruct((rows, width), bf16),
        ),
        in_specs=[SMEM_SPEC, VMEM_SPEC] + [ANY_SPEC] * n,
        out_specs=(VMEM_SPEC,) * 5,
        scratch_shapes=[
            pltpu.VMEM((width, 3 * width), bf16),
            pltpu.VMEM((width, width), bf16),
            pltpu.VMEM((n, ROW, LANES), bf16),
            pltpu.VMEM((8, width), f32),
            pltpu.SemaphoreType.DMA((3 * n,)),
        ],
        compiler_params=params(),
        cost_estimate=cost(7),
    )(shard, tok, *dense)


def weight_copies(shard, dense, tiles, router, up, down, bias, sems, router_lane):
    n = len(dense)
    width, hidden = up.shape[2], up.shape[3]
    folds = width // hidden
    routers, weights = [], [[], []]
    for k, tile in enumerate(dense):
        rows = tile.shape[0]
        base = pl.multiple_of((shard ^ k) * rows, rows)
        routers.append(
            pltpu.make_async_copy(
                tile.at[:, router_lane : router_lane + LANES], router.at[pl.ds(base, rows)], sems.at[0, 0, k]
            )
        )
    for j in range(2):
        for k in range(n):
            tile = tiles[j * n + k]
            for fold in range(folds):
                at = slice(fold * hidden, (fold + 1) * hidden)
                weights[j].append(
                    pltpu.make_async_copy(
                        tile.at[0:hidden, at], up.at[j, k, at], sems.at[1 + j, fold, k]
                    )
                )
            weights[j].append(
                pltpu.make_async_copy(
                    tile.at[hidden : 2 * hidden], down.at[j, k], sems.at[1 + j, folds, k]
                )
            )
            weights[j].append(
                pltpu.make_async_copy(
                    tile.at[2 * hidden : 2 * hidden + ROW], bias.at[j, k], sems.at[1 + j, folds + 1, k]
                )
            )
    return routers, weights


def block_starts(group, counts):
    starts = []
    for j in range(2):
        at, firsts = jnp.int32(0), []
        for b in range(group):
            firsts.append(pl.multiple_of(at, ROW))
            at = at + (counts[2 * b + j] + ROW - 1) // ROW * ROW
        starts.append((firsts, pl.multiple_of(at, ROW)))
    return starts


def gather_rows(group, counts, pos, blocks, into, starts):
    width = into.shape[2]
    row = lax.broadcasted_iota(jnp.int32, (GATHER, 1), 0)
    for b in range(group):
        hot = [
            jnp.where(pos[2 * b + j : 2 * b + j + 1, :] == row, 1.0, 0.0).astype(bf16) for j in range(2)
        ]
        both = dot(jnp.concatenate(hot, axis=0), blocks[b]).astype(bf16)
        for j in range(2):
            base = starts[j][0][b]
            into[j, pl.ds(base, GATHER), :] = both[j * GATHER : (j + 1) * GATHER]

            def more(i, carry, j=j, base=base):
                some = jnp.where(pos[2 * b + j : 2 * b + j + 1, :] == row + i * GATHER, 1.0, 0.0)
                at = pl.multiple_of(base + i * GATHER, ROW)
                into[j, pl.ds(at, GATHER), :] = dot(some.astype(bf16), blocks[b]).astype(bf16)
                return carry

            lax.fori_loop(1, (counts[2 * b + j] + GATHER - 1) // GATHER, more, 0)
    for j in range(2):
        into[j, pl.ds(starts[j][1], MLP), :] = jnp.zeros((MLP, width), bf16)


def scatter_rows(group, counts, places, source, outs, staged, sems, starts, total):
    column = lax.broadcasted_iota(jnp.int32, (1, SCATTER), 1)

    def leave(b):
        return pltpu.make_async_copy(staged.at[b % 2], outs[b], sems.at[b % 2])

    for b in range(group):
        mine = [places[:, 2 * b + j : 2 * b + j + 1] for j in range(2)]
        hot = jnp.concatenate(
            [jnp.where(mine[j] == column, 1.0, 0.0).astype(bf16) for j in range(2)], axis=1
        )
        rows = jnp.concatenate(
            [source[j, pl.ds(starts[j][0][b], SCATTER), :] for j in range(2)], axis=0
        )
        if b >= 2:
            leave(b - 2).wait()
        value = dot(hot, rows)
        staged[b % 2] = value.astype(bf16)

        @pl.when((counts[2 * b] > SCATTER) | (counts[2 * b + 1] > SCATTER))
        def _():
            total[...] = value
            for j in range(2):

                def more(i, carry, j=j):
                    some = jnp.where(mine[j] == column + i * SCATTER, 1.0, 0.0).astype(bf16)
                    at = pl.multiple_of(starts[j][0][b] + i * SCATTER, ROW)
                    total[...] += dot(some, source[j, pl.ds(at, SCATTER), :])
                    return carry

                lax.fori_loop(1, (counts[2 * b + j] + SCATTER - 1) // SCATTER, more, 0)
            staged[b % 2] = total[...].astype(bf16)

        leave(b).start()
    for b in range(max(0, group - 2), group):
        leave(b).wait()


def block_copies(refs, blocks, sems):
    return [pltpu.make_async_copy(ref, blocks.at[b], sems.at[b]) for b, ref in enumerate(refs)]


def tile_at(i):
    return pl.ds(pl.multiple_of(i * MLP, MLP), MLP)


def drain(copies, tiles):
    for back in (2, 1):

        @pl.when(tiles >= back)
        def _():
            for copy in copies(tiles - back):
                copy.wait()


def expert_forward_kernel(n, group, experts, router_lane, *refs):
    shard_ref, e_ref, counts, pos, places = refs[:5]
    refs = refs[5:]
    sources, dense, tiles_in, refs = refs[:group], refs[group : group + n], refs[group + n : group + 3 * n], refs[group + 3 * n :]
    outs, refs = refs[:group], refs[group:]
    x_out, y_out, probs_out, act_out, slope_out = refs[:5]
    blocks, up, down, bias, router, outer, x_rows, scaled, total, staged, act, slope, y, probs = refs[5:19]
    sems, block_sems, leave_sems, out_sems, x_sems = refs[19:]
    shard = shard_ref[0]
    hidden_width = up.shape[3]
    width = up.shape[2]
    arrivals = block_copies(sources, blocks, block_sems)
    routers, weights = weight_copies(shard, dense, tiles_in, router, up, down, bias, sems, router_lane)
    for copy in arrivals + routers + weights[0] + weights[1]:
        copy.start()
    for copy in arrivals:
        copy.wait()
    starts = block_starts(group, counts)
    gather_rows(group, counts, pos, blocks, x_rows, starts)
    for copy in routers:
        copy.wait()
    lane = lax.broadcasted_iota(jnp.int32, (1, LANES), 1)
    for j in range(2):
        tiles = (starts[j][1] + MLP - 1) // MLP

        def saves(i, j=j):
            slot = lax.rem(i, 2)
            return [
                pltpu.make_async_copy(source.at[slot], into.at[j, tile_at(i)], out_sems.at[m, slot])
                for m, (source, into) in enumerate(
                    ((act, act_out), (slope, slope_out), (y, y_out), (probs, probs_out))
                )
            ]

        def save_x(i, j=j):
            return pltpu.make_async_copy(x_rows.at[j, tile_at(i)], x_out.at[j, tile_at(i)], x_sems.at[j, i])

        for copy in weights[j]:
            copy.wait()
        place_columns(shard, [bias[j, k][0:8].astype(f32) for k in range(n)], outer.at[j], 0)

        def tile_step(i, carry):
            slot = lax.rem(i, 2)

            @pl.when(i >= 2)
            def _():
                for copy in saves(i - 2):
                    copy.wait()

            save_x(i).start()
            x = x_rows[j, tile_at(i), :]
            logits = jnp.where(lane < experts, dot(x, router[...]), NEG)
            powers = jnp.exp(logits - jnp.max(logits, axis=-1, keepdims=True))
            shares = powers * (1.0 / jnp.sum(powers, axis=-1, keepdims=True))
            probs[slot] = shares
            gate = jnp.sum(jnp.where(lane == e_ref[j], shares, 0.0), axis=-1, keepdims=True)
            for k in range(n):
                hidden = dot(x, up[j, k]) + bias[j, k, 0:1, 0:hidden_width].astype(f32)
                square = hidden * hidden
                share = 0.5 * jnp.tanh(hidden * (GELU_C + GELU_C * GELU_K * square)) + 0.5
                active = hidden * share
                columns = slice(k * hidden_width, (k + 1) * hidden_width)
                act[slot, :, columns] = active.astype(bf16)
                slope[slot, :, columns] = (
                    share
                    + (active - active * share) * (2.0 * GELU_C + 6.0 * GELU_C * GELU_K * square)
                ).astype(bf16)
            acc = jnp.broadcast_to(outer[j, 1:2], (MLP, width))
            for k in range(n):
                acc = acc + dot(act[slot, :, k * hidden_width : (k + 1) * hidden_width], down[j, k])
            low = acc.astype(bf16)
            y[slot] = low
            for copy in saves(i):
                copy.start()
            scaled[j, tile_at(i), :] = (gate * low.astype(f32)).astype(bf16)
            return carry

        lax.fori_loop(0, tiles, tile_step, 0)
        drain(saves, tiles)

        def wait_x(i, carry):
            save_x(i).wait()
            return carry

        lax.fori_loop(0, tiles, wait_x, 0)
        scaled[j, tile_at(tiles), :] = jnp.zeros((MLP, width), bf16)
    scatter_rows(group, counts, places, scaled, outs, staged, leave_sems, starts, total)


def expert_rows(group, capacity):
    return up_to(group * up_to(capacity, ROW), MLP) + MLP


def expert_forward(scalars, pos, places, sources, dense, tiles, group, experts, capacity, router_lane):
    n = len(dense)
    width = sources[0].shape[1]
    tokens = pos.shape[1]
    hidden = (tiles[0].shape[0] - ROW) // 2
    rows = expert_rows(group, capacity)
    return pl.pallas_call(
        functools.partial(expert_forward_kernel, n, group, experts, router_lane),
        name="expert_forward",
        out_shape=[jax.ShapeDtypeStruct((tokens, width), bf16)] * group
        + [jax.ShapeDtypeStruct((2, rows, width), bf16)] * 2
        + [jax.ShapeDtypeStruct((2, rows, LANES), f32)]
        + [jax.ShapeDtypeStruct((2, rows, hidden * n), bf16)] * 2,
        in_specs=[SMEM_SPEC] * 3 + [VMEM_SPEC] * 2 + [ANY_SPEC] * (group + 3 * n),
        out_specs=[ANY_SPEC] * (group + 5),
        scratch_shapes=[
            pltpu.VMEM((group, tokens, width), bf16),
            pltpu.VMEM((2, n, width, hidden), bf16),
            pltpu.VMEM((2, n, hidden, width), bf16),
            pltpu.VMEM((2, n, ROW, width), bf16),
            pltpu.VMEM((width, LANES), bf16),
            pltpu.VMEM((2, 8, width), f32),
            pltpu.VMEM((2, rows, width), bf16),
            pltpu.VMEM((2, rows, width), bf16),
            pltpu.VMEM((tokens, width), f32),
            pltpu.VMEM((2, tokens, width), bf16),
            pltpu.VMEM((2, MLP, hidden * n), bf16),
            pltpu.VMEM((2, MLP, hidden * n), bf16),
            pltpu.VMEM((2, MLP, width), bf16),
            pltpu.VMEM((2, MLP, LANES), f32),
            pltpu.SemaphoreType.DMA((3, width // hidden + 2, n)),
            pltpu.SemaphoreType.DMA((group,)),
            pltpu.SemaphoreType.DMA((2,)),
            pltpu.SemaphoreType.DMA((4, 2)),
            pltpu.SemaphoreType.DMA((2, rows // MLP)),
        ],
        compiler_params=params(),
        cost_estimate=cost(FORWARD_US),
    )(*scalars, pos, places, *sources, *dense, *tiles)


def expert_backward_kernel(n, group, router_lane, *refs):
    shard_ref, e_ref, counts, pos, places = refs[:5]
    refs = refs[5:]
    sources, dense, tiles_in, refs = refs[:group], refs[group : group + n], refs[group + n : group + 3 * n], refs[group + 3 * n :]
    x_in, y_in, probs_in, slope_in, refs = refs[0], refs[1], refs[2], refs[3], refs[4:]
    outs, refs = refs[:group], refs[group:]
    pg_out, hg_out, router_grad, inner_grad, outer_grad = refs[:5]
    blocks, up, down, bias, router, f_rows, b_rows, total, staged, hg, pg, slope, x, y, probs = refs[5:20]
    sems, block_sems, leave_sems, out_sems, in_sems = refs[20:]
    shard = shard_ref[0]
    hidden_width = up.shape[3]
    width = up.shape[2]
    arrivals = block_copies(sources, blocks, block_sems)
    routers, weights = weight_copies(shard, dense, tiles_in, router, up, down, bias, sems, router_lane)
    for copy in arrivals + routers + weights[0] + weights[1]:
        copy.start()
    router_grad[...] = jnp.zeros(router_grad.shape, f32)
    inner_grad[...] = jnp.zeros(inner_grad.shape, f32)
    outer_grad[...] = jnp.zeros(outer_grad.shape, f32)
    for copy in arrivals:
        copy.wait()
    starts = block_starts(group, counts)
    gather_rows(group, counts, pos, blocks, f_rows, starts)
    for copy in routers:
        copy.wait()
    lane = lax.broadcasted_iota(jnp.int32, (1, LANES), 1)
    for j in range(2):
        tiles = (starts[j][1] + MLP - 1) // MLP

        def saves(i, j=j):
            slot = lax.rem(i, 2)
            return (
                pltpu.make_async_copy(hg.at[slot], hg_out.at[j, tile_at(i)], out_sems.at[0, slot]),
                pltpu.make_async_copy(pg.at[slot], pg_out.at[j, tile_at(i)], out_sems.at[1, slot]),
            )

        def loads(i, j=j):
            slot = lax.rem(i, 2)
            return [
                pltpu.make_async_copy(source.at[j, tile_at(i)], into.at[slot], in_sems.at[m, slot])
                for m, (source, into) in enumerate(
                    ((x_in, x), (y_in, y), (probs_in, probs), (slope_in, slope))
                )
            ]

        @pl.when(tiles >= 1)
        def _():
            for copy in loads(0):
                copy.start()

        for copy in weights[j]:
            copy.wait()

        def tile_step(i, carry):
            slot = lax.rem(i, 2)

            @pl.when(i + 1 < tiles)
            def _():
                for copy in loads(i + 1):
                    copy.start()

            @pl.when(i >= 2)
            def _():
                for copy in saves(i - 2):
                    copy.wait()

            for copy in loads(i):
                copy.wait()
            f = f_rows[j, tile_at(i), :].astype(f32)
            shares = probs[slot]
            mine = lane == e_ref[j]
            gate = jnp.sum(jnp.where(mine, shares, 0.0), axis=-1, keepdims=True)
            wide = gate * f
            pg[slot] = wide.astype(bf16)
            gate_grad = jnp.sum(f * y[slot].astype(f32), axis=-1, keepdims=True)
            logit = gate_grad * gate * (jnp.where(mine, 1.0, 0.0) - shares)
            high = logit.astype(bf16)
            rest = (logit - high.astype(f32)).astype(bf16)
            outer_grad[j : j + 1] += jnp.sum(wide, axis=0, keepdims=True)
            for k in range(n):
                columns = slice(k * hidden_width, (k + 1) * hidden_width)
                grad = dot_last(pg[slot], down[j, k]) * slope[slot, :, columns].astype(f32)
                hg[slot, :, columns] = grad.astype(bf16)
                inner_grad[j : j + 1, columns] += jnp.sum(grad, axis=0, keepdims=True)
            for copy in saves(i):
                copy.start()
            turned = x[slot].T
            router_grad[...] += dot(turned, high) + dot(turned, rest)
            acc = dot_last(high, router[...]) + dot_last(rest, router[...])
            for k in range(n):
                acc = acc + dot_last(hg[slot, :, k * hidden_width : (k + 1) * hidden_width], up[j, k])
            b_rows[j, tile_at(i), :] = acc.astype(bf16)
            return carry

        lax.fori_loop(0, tiles, tile_step, 0)
        drain(saves, tiles)
        b_rows[j, tile_at(tiles), :] = jnp.zeros((MLP, width), bf16)
    scatter_rows(group, counts, places, b_rows, outs, staged, leave_sems, starts, total)


def expert_backward(scalars, pos, places, sources, dense, tiles, saved, group, capacity, router_lane):
    n = len(dense)
    width = sources[0].shape[1]
    tokens = pos.shape[1]
    hidden = (tiles[0].shape[0] - ROW) // 2
    rows = expert_rows(group, capacity)
    return pl.pallas_call(
        functools.partial(expert_backward_kernel, n, group, router_lane),
        name="expert_backward",
        out_shape=[jax.ShapeDtypeStruct((tokens, width), bf16)] * group
        + [
            jax.ShapeDtypeStruct((2, rows, width), bf16),
            jax.ShapeDtypeStruct((2, rows, hidden * n), bf16),
            jax.ShapeDtypeStruct((width, LANES), f32),
            jax.ShapeDtypeStruct((8, hidden * n), f32),
            jax.ShapeDtypeStruct((8, width), f32),
        ],
        in_specs=[SMEM_SPEC] * 3 + [VMEM_SPEC] * 2 + [ANY_SPEC] * (group + 3 * n + 4),
        out_specs=[ANY_SPEC] * (group + 2) + [VMEM_SPEC] * 3,
        scratch_shapes=[
            pltpu.VMEM((group, tokens, width), bf16),
            pltpu.VMEM((2, n, width, hidden), bf16),
            pltpu.VMEM((2, n, hidden, width), bf16),
            pltpu.VMEM((2, n, ROW, width), bf16),
            pltpu.VMEM((width, LANES), bf16),
            pltpu.VMEM((2, rows, width), bf16),
            pltpu.VMEM((2, rows, width), bf16),
            pltpu.VMEM((tokens, width), f32),
            pltpu.VMEM((2, tokens, width), bf16),
            pltpu.VMEM((2, MLP, hidden * n), bf16),
            pltpu.VMEM((2, MLP, width), bf16),
            pltpu.VMEM((2, MLP, hidden * n), bf16),
            pltpu.VMEM((2, MLP, width), bf16),
            pltpu.VMEM((2, MLP, width), bf16),
            pltpu.VMEM((2, MLP, LANES), f32),
            pltpu.SemaphoreType.DMA((3, width // hidden + 2, n)),
            pltpu.SemaphoreType.DMA((group,)),
            pltpu.SemaphoreType.DMA((2,)),
            pltpu.SemaphoreType.DMA((2, 2)),
            pltpu.SemaphoreType.DMA((4, 2)),
        ],
        compiler_params=params(),
        cost_estimate=cost(BACKWARD_US),
    )(*scalars, pos, places, *sources, *dense, *tiles, *saved)


def put_columns(shard, k, n, source, row, into):
    width = source.shape[1] // n
    if width % LANES == 0:
        base = pl.multiple_of((shard ^ k) * width, width)
        into[:, 0:width] = source[row : row + 1, pl.ds(base, width)].astype(into.dtype)
        return
    for place in range(n):

        @pl.when((shard ^ k) == place)
        def _():
            into[:, 0:width] = source[row : row + 1, place * width : (place + 1) * width].astype(into.dtype)


def weight_grads_kernel(n, experts, added, shard_ref, tiles_ref, *refs):
    saved, inner_part, outer_part, refs = refs[:4], refs[4], refs[5], refs[6:]
    before, refs = refs[:added], refs[added:]
    results, refs = refs[: 2 * len(experts)], refs[2 * len(experts) :]
    x, pg, act, hg, up_total, down_total, row, sems = refs
    width, hidden = up_total.shape[1:]
    folds = width // hidden
    shard = shard_ref[0]
    for turn, j in enumerate(experts):
        tiles = tiles_ref[j]
        for k in range(n):
            up_total[k] = jnp.zeros((width, hidden), f32)
            down_total[k] = jnp.zeros((width, hidden), f32)

        def loads(i, j=j):
            slot = lax.rem(i, 2)
            return [
                pltpu.make_async_copy(source.at[j, tile_at(i)], into.at[slot], sems.at[m, slot])
                for m, (source, into) in enumerate(zip(saved, (x, pg, act, hg)))
            ]

        @pl.when(tiles >= 1)
        def _():
            for copy in loads(0):
                copy.start()

        def tile_step(i, carry):
            slot = lax.rem(i, 2)

            @pl.when(i + 1 < tiles)
            def _():
                for copy in loads(i + 1):
                    copy.start()

            for copy in loads(i):
                copy.wait()
            turned = x[slot].T
            turned_grad = pg[slot].T
            for k in range(n):
                columns = slice(k * hidden, (k + 1) * hidden)
                up_total[k] += dot(turned, hg[slot, :, columns])
                down_total[k] += dot(turned_grad, act[slot, :, columns])
            return carry

        lax.fori_loop(0, tiles, tile_step, 0)
        row[8:16] = outer_part[...]
        for k in range(n):
            into = results[2 * turn + 1 - k % 2].at[k // 2]
            base = before[2 * turn + 1 - k % 2].at[k // 2] if added else None

            def put(rows, columns, value):
                if added:
                    value = value + base[rows, columns].astype(f32)
                into[rows, columns] = value.astype(bf16)

            for fold in range(folds):
                at = slice(fold * hidden, (fold + 1) * hidden)
                put(slice(0, hidden), at, up_total[k, at])
            put(slice(hidden, 2 * hidden), slice(0, width), down_total[k].T)
            row[0:8] = jnp.zeros((8, width), f32)
            row[0:1, 0:hidden] = inner_part[j : j + 1, k * hidden : (k + 1) * hidden]
            put_columns(shard, k, n, row, 8 + j, row.at[1:2])
            row[8:16] = outer_part[...]
            put(slice(2 * hidden, 2 * hidden + 8), slice(0, width), row[0:8])
            into[2 * hidden + 8 : 2 * hidden + ROW] = jnp.zeros((ROW - 8, width), bf16)


def weight_grads(experts, shard, tiles, saved, biases, n, before=()):
    _, rows, width = saved[0].shape
    hidden = saved[2].shape[2] // n
    shape = jax.ShapeDtypeStruct((n // 2, 2 * hidden + ROW, width), bf16)
    return pl.pallas_call(
        functools.partial(weight_grads_kernel, n, experts, len(before)),
        name="weight_grads",
        out_shape=(shape,) * (2 * len(experts)),
        in_specs=[SMEM_SPEC] * 2 + [ANY_SPEC] * 4 + [VMEM_SPEC] * (2 + len(before)),
        out_specs=(VMEM_SPEC,) * (2 * len(experts)),
        scratch_shapes=[
            pltpu.VMEM((2, MLP, width), bf16),
            pltpu.VMEM((2, MLP, width), bf16),
            pltpu.VMEM((2, MLP, hidden * n), bf16),
            pltpu.VMEM((2, MLP, hidden * n), bf16),
            pltpu.VMEM((n, width, hidden), f32),
            pltpu.VMEM((n, width, hidden), f32),
            pltpu.VMEM((ROW, width), f32),
            pltpu.SemaphoreType.DMA((4, 2)),
        ],
        compiler_params=params(),
        cost_estimate=cost(8 * len(experts)),
    )(shard, tiles, *saved, *biases, *before)


def norm_backward(rows, gain, grad):
    centered, rate = normalise(rows)
    unit = centered * rate
    scaled = grad * gain
    back = rate * (
        scaled
        - jnp.mean(scaled, axis=-1, keepdims=True)
        - unit * jnp.mean(scaled * unit, axis=-1, keepdims=True)
    )
    return (
        back,
        jnp.sum(grad * unit, axis=0, keepdims=True),
        jnp.sum(grad, axis=0, keepdims=True),
        unit,
    )


def attention_backward_kernel(n_tiles, parts, base, images, overlap, last, *refs):
    shard_ref, refs = refs[0], refs[1:]
    grads, refs = refs[:parts], refs[parts:]
    fg, res, att, qkv, weights, tok = refs[:6]
    dense, refs = refs[6 : 6 + n_tiles], refs[6 + n_tiles :]
    before = None
    if overlap:
        before, refs = refs[:4], refs[4:]
    if last:
        router_parts, refs = refs[:last], refs[last:]
        token_grad, norm_grad, send, keep = refs[:4]
        mixer_grad, merge_grad = refs[-2:]
        refs = refs[:-2]
    else:
        token_grad, mixer_grad, merge_grad, norm_grad = refs[:4]
    mixer, merge, normt, norms, dres, low, datt, normed, mg, sems = refs[4:]
    shard = shard_ref[0]
    width = tok.shape[1]
    n_rows = tok.shape[0]
    copies = place_dense(shard, dense, mixer, merge, normt, sems)
    for copy in copies:
        copy.start()
    for copy in copies:
        copy.wait()
    place_norms(shard, normt, norms)
    norm_grad[...] = before[3][...] if overlap else jnp.zeros(norm_grad.shape, f32)
    for rows in row_tiles(n_rows):
        grad = grads[0][rows].astype(f32)
        for other in grads[1:]:
            grad = grad + other[rows].astype(f32)
        back, gain, shift, _ = norm_backward(res[rows], norms[1:2], grad)
        norm_grad[1:2] += gain
        norm_grad[3:4] += shift
        total = fg[rows] + back
        dres[rows] = total
        low[rows] = total.astype(bf16)
        datt[rows] = dot_last(low[rows], merge[...]).astype(bf16)
    mg[...] = jnp.zeros(mg.shape, bf16)
    merge_term = dot_first(att[...], low[...])
    merge_grad[...] = before[2][...] + merge_term if overlap else merge_term
    lane = lax.broadcasted_iota(jnp.int32, (1, LANES), 1)

    def image_step(image, carry):
        start, _, _ = image_window(base, image)
        window = pl.ds(start, WIN)
        for slab in range(width // LANES):
            q_at = slice(slab * LANES, (slab + 1) * LANES)
            k_at = slice(width + slab * LANES, width + (slab + 1) * LANES)
            v_at = slice(2 * width + slab * LANES, 2 * width + (slab + 1) * LANES)
            q, k, v = qkv[window, q_at], qkv[window, k_at], qkv[window, v_at]
            do = datt[window, q_at]
            parts = []
            for half in range(2):
                head = 2 * slab + half
                mine = (lane >= half * HEAD_DIM) & (lane < (half + 1) * HEAD_DIM)
                zero = jnp.zeros_like(q)
                low = weights[image, head]
                dv = dot_first(low, do)
                dw = dot_last(jnp.where(mine, do, zero), v)
                wide = low.astype(f32)
                inner = jnp.sum(wide * dw, axis=-1, keepdims=True)
                ds = (wide * (dw - inner)).astype(bf16)
                parts.append((dot(ds, k) * SCALING, dot_first(ds, q) * SCALING, dv))
            for at, first, second in zip((q_at, k_at, v_at), parts[0], parts[1]):
                both = jnp.where(lane < HEAD_DIM, first, second).astype(bf16)
                mg[window, at] = mg[window, at] + both
        return carry

    lax.fori_loop(0, images, image_step, 0)
    shift_rows = token_grad.shape[0] - n_rows if overlap else 0
    if overlap:
        token_grad[0:shift_rows] = before[0][0:shift_rows]
    for rows in row_tiles(n_rows):
        grad = dot_last(mg[rows], mixer[...])
        back, gain, shift, unit = norm_backward(tok[rows].astype(f32), norms[0:1], grad)
        norm_grad[0:1] += gain
        norm_grad[2:3] += shift
        total = dres[rows] + back
        if overlap and rows.start < overlap:
            both = before[0][shift_rows : shift_rows + overlap]
            token_grad[shift_rows : shift_rows + overlap] = total[0:overlap] + both
            token_grad[shift_rows + overlap : shift_rows + rows.stop] = total[overlap:]
        else:
            token_grad[shift_rows + rows.start : shift_rows + rows.stop] = total
        normed[rows] = (unit * norms[0:1] + norms[2:3]).astype(bf16)
    for c in range(3):
        columns = slice(c * width, (c + 1) * width)
        term = dot_first(normed[...], mg[:, columns])
        mixer_grad[:, columns] = before[1][:, columns] + term if overlap else term
    if last:
        for k in range(n_tiles):
            own = width // n_tiles
            at = pl.ds(pl.multiple_of((shard ^ k) * own, own), own)
            into = (send if k % 2 else keep).at[k // 2]
            into[:, 0 : 3 * width] = mixer_grad[at].astype(bf16)
            into[:, 3 * width : 4 * width] = merge_grad[at].astype(bf16)
            into[:, 4 * width : 4 * width + LANES] = sum(part[at] for part in router_parts).astype(bf16)


def attention_backward(shard, grads, fg, res, att, qkv, weights, tok, dense, base, images, before, start, router_parts):
    rows, width = tok.shape
    n = len(dense)
    overlap = before[0].shape[0] - start if before else 0
    token_shape = jax.ShapeDtypeStruct((start + rows if before else rows, width), f32)
    norm_shape = jax.ShapeDtypeStruct((8, width), f32)
    totals = [pltpu.VMEM((width, 3 * width), f32), pltpu.VMEM((width, width), f32)]
    if router_parts:
        tile = jax.ShapeDtypeStruct((n // 2, width // n, 4 * width + LANES), bf16)
        shapes = (token_shape, norm_shape, tile, tile)
    else:
        shapes = (
            token_shape,
            jax.ShapeDtypeStruct((width, 3 * width), f32),
            jax.ShapeDtypeStruct((width, width), f32),
            norm_shape,
        )
    held = (*grads, fg, res, att, qkv, weights, tok)
    more = (*(before or ()), *router_parts)
    return pl.pallas_call(
        functools.partial(
            attention_backward_kernel, n, len(grads), base, images, overlap, len(router_parts)
        ),
        name="attention_backward",
        out_shape=shapes,
        in_specs=[SMEM_SPEC] + [VMEM_SPEC] * len(held) + [ANY_SPEC] * n + [VMEM_SPEC] * len(more),
        out_specs=(VMEM_SPEC,) * 4,
        scratch_shapes=[
            pltpu.VMEM((width, 3 * width), bf16),
            pltpu.VMEM((width, width), bf16),
            pltpu.VMEM((n, ROW, LANES), bf16),
            pltpu.VMEM((8, width), f32),
            pltpu.VMEM((rows, width), f32),
            pltpu.VMEM((rows, width), bf16),
            pltpu.VMEM((rows, width), bf16),
            pltpu.VMEM((rows, width), bf16),
            pltpu.VMEM((rows, 3 * width), bf16),
            pltpu.SemaphoreType.DMA((3 * n,)),
        ]
        + (totals if router_parts else []),
        compiler_params=params(),
        cost_estimate=cost(17),
    )(shard, *held, *dense, *more)


def bits_of(ways):
    bit = ways // 2
    while bit:
        yield bit
        bit //= 2


def gather_tiles(array, axis, ways, gate=None):
    tiles = {0: array}
    for step, bit in enumerate(bits_of(ways)):
        for k in list(tiles):
            sent = after(tiles[k], *gate) if gate is not None and step else tiles[k]
            tiles[k | bit] = swap(sent, axis, ways, bit)
    return [tiles[k] for k in range(ways)]


def fold_tiles(send, keep, axis, ways):
    sums = (keep.astype(f32) + swap(send, axis, ways, 1).astype(f32)).astype(bf16)

    def rest():
        tiles = sums
        for bit in [bit for bit in reversed(list(bits_of(ways))) if bit > 1]:
            tiles = (tiles[0::2].astype(f32) + swap(tiles[1::2], axis, ways, bit).astype(f32)).astype(bf16)
        return tiles

    return sums, rest


def sum_over(array, axis, ways):
    for bit in bits_of(ways):
        array = array + swap(array, axis, ways, bit)
    return array


def sum_split(array, axis, ways, index, gate, last_gate):
    half = array.shape[0] // 2
    mine = index & 1
    kept = lax.dynamic_slice_in_dim(array, mine * half, half, 0)
    sent = lax.dynamic_slice_in_dim(array, (1 - mine) * half, half, 0)
    part = after(kept.astype(f32) + swap(sent, axis, ways, 1).astype(f32), gate)
    for bit in [bit for bit in reversed(list(bits_of(ways))) if bit > 1]:
        low = part.astype(bf16)
        part = low.astype(f32) + swap(low, axis, ways, bit).astype(f32)
    low = after(part.astype(bf16), last_gate)
    other = swap(low, axis, ways, 1)
    first = jnp.where(mine == 0, low, other)
    second = jnp.where(mine == 0, other, low)
    return jnp.concatenate([first, second], axis=0).astype(f32)


def exchange(array, ways, group):
    return [array] + [swap(array, "expert", ways, b) for b in range(1, group)]


def give_back(blocks, ways, group):
    return [blocks[0]] + [swap(blocks[b], "expert", ways, b) for b in range(1, group)]


def after(value, *others):
    return lax.optimization_barrier((value, *others))[0]


def per_device(
    tokens,
    teacher,
    valid_mask,
    routes,
    mixer_weight,
    merge_weight,
    router_weight,
    norm_gain,
    norm_shift,
    up_weight,
    inner_bias,
    down_weight,
    outer_bias,
):
    ways = lax.axis_size("expert")
    shards = lax.axis_size("shard")
    shard = lax.axis_index("shard").astype(jnp.int32)
    expert = lax.axis_index("expert").astype(jnp.int32)
    token_count, width = tokens.shape
    images = token_count // SEQ
    experts = router_weight.shape[1]
    group = ways // 2
    chunks = 2 if images % 2 == 0 else 1
    chunk_images = images // chunks
    chunk_tokens = chunk_images * SEQ
    capacity = min(chunk_tokens, max(2, 4 * token_count // experts))
    firsts = [c * chunk_tokens for c in range(chunks)]
    starts = [first // 8 * 8 for first in firsts]
    last = max(first - start + (chunk_images - 1) * SEQ for first, start in zip(firsts, starts))
    rows = up_to(last // ROW * ROW + WIN, ROW)
    all_rows = starts[-1] + rows
    shard_rows = width // shards
    hidden = up_weight.shape[2]
    router_lane = 4 * width
    folds = width // hidden

    dense_own, near = pack(
        mixer_weight, merge_weight, router_weight, norm_gain, norm_shift, up_weight, inner_bias, down_weight, outer_bias
    )
    dense = gather_tiles(dense_own, "shard", shards)
    far = swap(near, "expert", ways, group)

    route_rows = jnp.pad(routes, ((0, all_rows - token_count), (0, 0)), constant_values=-1).T
    ids = jnp.arange(experts, dtype=jnp.int32)[:, None]
    named = (route_rows[0:1] == ids) | (route_rows[1:2] == ids)
    order = jnp.arange(all_rows, dtype=jnp.int32)
    in_chunk = (order[None, :] // chunk_tokens) == jnp.arange(chunks, dtype=jnp.int32)[:, None]
    named = (named[None] & in_chunk[:, None, :]).reshape(chunks * experts, all_rows)
    earlier = (order[:, None] < order[None, :]).astype(bf16)
    slots = jnp.dot(named.astype(bf16), earlier, preferred_element_type=f32).astype(jnp.int32)
    slots = jnp.where(named, slots, -1)
    slots = jnp.pad(slots, ((0, 8), (0, 0)), constant_values=jnp.sum(valid_mask))
    slots = after(slots, dense[1])
    slot_blocks = jnp.stack([slots] + [swap(slots, "expert", ways, b) for b in range(1, group)])
    group_count = jnp.sum(slot_blocks[:, -8:, 0:LANES], axis=0).astype(f32)
    shard_count = sum_over(group_count, "shard", shards)
    slot_blocks = slot_blocks[:, :-8].reshape(group, chunks, experts, all_rows)
    chosen = jnp.concatenate(
        [
            lax.dynamic_slice_in_dim(slot_blocks, expert, 1, 2),
            lax.dynamic_slice_in_dim(slot_blocks, expert ^ group, 1, 2),
        ],
        axis=2,
    )
    shard_id = shard[None]
    e_ids = jnp.stack([expert, expert ^ group])
    routing, tile_counts = [], []
    for c in range(chunks):
        pos = chosen[:, c, :, starts[c] : starts[c] + rows].reshape(2 * group, rows)
        counts = jnp.max(pos, axis=1) + 1
        places = jnp.pad(pos.T, ((0, 0), (0, LANES - 2 * group)), constant_values=-1)
        ends = jnp.sum((counts.reshape(group, 2) + ROW - 1) // ROW * ROW, axis=0)
        tile_counts.append((ends + MLP - 1) // MLP)
        routing.append(((shard_id, e_ids, counts), pos, places))

    def chunk_rows(array, c):
        part = array[starts[c] : min(starts[c] + rows, token_count)]
        return jnp.pad(part, ((0, rows - part.shape[0]),) + ((0, 0),) * (part.ndim - 1))

    toks = [chunk_rows(tokens, c) for c in range(chunks)]
    local = jnp.arange(rows, dtype=jnp.int32)[:, None]
    kept, valids = [], []
    for c in range(chunks):
        base = firsts[c] - starts[c]
        mask = (local >= base) & (local < base + chunk_tokens)
        kept.append(mask)
        valids.append(jnp.where(mask, chunk_rows(valid_mask, c).astype(f32)[:, None], 0.0))

    forward = []
    for c in range(chunks):
        gates = (forward[-1][4],) if c else ()
        forward.append(
            attention_forward(shard_id, after(toks[c], *gates), dense, firsts[c] - starts[c], chunk_images)
        )
    attended = forward[-1][4]
    given, experts_saved = [], []
    for c in range(chunks):
        arrived = exchange(forward[c][4] if c == 0 else after(forward[c][4], tiles[-2]), ways, group)
        if c == 0:
            near_tiles = gather_tiles(
                after(near, dense[-1], shard_count, chosen), "shard", shards, (attended, *arrived[1:])
            )
            far_tiles = gather_tiles(
                after(far, attended), "shard", shards
            )
            tiles = near_tiles + far_tiles
        if c:
            arrived[0] = after(arrived[0], given[-1][0])
        results = expert_forward(*routing[c], arrived, dense, tiles, group, experts, capacity, router_lane)
        given.append(results[:group])
        if c == 0:
            valid_count = shard_count + swap(after(shard_count, given[0][0]), "expert", ways, group)
            valid_count = valid_count[0, 0]
            scale = token_count * ways * shards / valid_count
        experts_saved.append(results[group:])

    blocks_out, squared, final_grads, input_grads = [], 0.0, [], []
    router_parts, biases, saved, early = [], [], [], ()
    arrived = None
    for c in range(chunks):
        parts = given[c] if c == 0 else [given[c][0]] + [after(part, *arrived) for part in given[c][1:]]
        block_out = forward[c][3]
        if c == 0:
            block_out = after(block_out, given[-1][0])
        for part in give_back(parts, ways, group):
            block_out = block_out + part.astype(f32)
        error = block_out - chunk_rows(teacher, c).astype(f32)
        squared = squared + jnp.sum(valids[c] * jnp.sum(error * error, axis=1, keepdims=True))
        fg = scale * valids[c] * error
        final_grads.append(fg)
        blocks_out.append(jnp.where(kept[c], block_out, 0.0).astype(bf16))
        arrived = exchange(fg.astype(bf16), ways, group)
        if c:
            early = weight_grads(
                (0, 1), shard_id, after(tile_counts[c - 1], fg), saved[c - 1], biases[c - 1], shards, early
            )
            arrived[0] = after(arrived[0], early[0])
            input_grads[c - 1] = [input_grads[c - 1][0]] + [
                after(part, *arrived[1:]) for part in input_grads[c - 1][1:]
            ]
            input_grads[c - 1] = give_back(input_grads[c - 1], ways, group)
        x_rows, y_rows, probs_rows, act, slope = experts_saved[c]
        results = expert_backward(
            *routing[c],
            arrived,
            dense,
            tiles,
            (x_rows, y_rows, probs_rows, slope),
            group,
            capacity,
            router_lane,
        )
        input_grads.append(results[:group])
        pg_rows, hg, router_part, inner_part, outer_part = results[group:]
        router_parts.append(router_part)
        biases.append((inner_part, outer_part))
        saved.append((x_rows, pg_rows, act, hg))
    last = chunks - 1
    far_tiles = weight_grads(
        (1,), shard_id, after(tile_counts[last], *input_grads[0][1:]), saved[last], biases[last], shards, early[2:]
    )
    input_grads[last] = give_back(input_grads[last], ways, group)
    far_sums, far_rest = fold_tiles(*far_tiles, "shard", shards)
    before = None
    for c in range(chunks):
        qkv, att, weights, res, _ = forward[c]
        gate = far_sums if c == 0 else far_grad
        before = attention_backward(
            after(shard_id, gate),
            input_grads[c],
            final_grads[c],
            res,
            att,
            qkv,
            weights,
            toks[c],
            dense,
            firsts[c] - starts[c],
            chunk_images,
            before,
            starts[c],
            router_parts if c == last else (),
        )
        if c == 0:
            far_grad = far_rest()
            far_arrived = [
                swap(half, "expert", ways, group) for half in (far_grad[0, :hidden], far_grad[0, hidden:])
            ]
    token_grad, norm_part, *dense_parts = before
    dense_parts[0] = after(dense_parts[0], far_arrived[0])
    dense_sums, dense_rest = fold_tiles(*dense_parts, "shard", shards)
    near_tiles = weight_grads(
        (0,), shard_id, after(tile_counts[last], dense_sums), saved[last], biases[last], shards, early[:2]
    )
    dense_grad = dense_rest()
    near_tiles = (after(near_tiles[0], dense_grad, far_arrived[1]), near_tiles[1])
    near_sums, near_rest = fold_tiles(*near_tiles, "shard", shards)
    near_grad = near_rest()
    up_sum = near_grad[0, :hidden].astype(f32) + far_arrived[0].astype(f32)
    up_grad = jnp.concatenate(
        [up_sum[:, fold * hidden : (fold + 1) * hidden] for fold in range(folds)], axis=0
    )
    rest_sum = near_grad[0, hidden:].astype(f32) + far_arrived[1].astype(f32)
    down_grad = rest_sum[:hidden]
    inner_grad = rest_sum[hidden : hidden + 1, 0:hidden]
    outer_grad = rest_sum[hidden + 1 : hidden + 2, 0:shard_rows]
    dense_sum = sum_split(dense_grad[0], "expert", ways, expert, near_sums, near_grad)
    output = jnp.zeros((all_rows, width), bf16)
    for c in range(chunks):
        output = output + jnp.pad(blocks_out[c], ((starts[c], all_rows - starts[c] - rows), (0, 0)))

    norm_sum = sum_over(sum_over(norm_part.at[4].set(squared), "shard", shards), "expert", ways)
    norm_sum = lax.dynamic_slice_in_dim(norm_sum, shard * shard_rows, shard_rows, 1)
    loss_value = norm_sum[4, 0] / (2.0 * valid_count)
    return (
        output[:token_count],
        loss_value,
        token_grad[:token_count],
        dense_sum[:, : 3 * width],
        dense_sum[:, 3 * width : 4 * width],
        dense_sum[:, 4 * width : 4 * width + experts],
        norm_sum[0:2],
        norm_sum[2:4],
        up_grad[None],
        inner_grad,
        down_grad[None],
        outer_grad,
    )


def solution(mesh):
    in_specs = (
        P(("expert", "shard"), None),
        P(("expert", "shard"), None),
        P(("expert", "shard")),
        P(("expert", "shard"), None),
        P("shard", None),
        P("shard", None),
        P("shard", None),
        P(None, "shard"),
        P(None, "shard"),
        P("expert", None, "shard"),
        P("expert", "shard"),
        P("expert", "shard", None),
        P("expert", "shard"),
    )
    out_specs = (
        P(("expert", "shard"), None),
        P(),
        P(("expert", "shard"), None),
        P("shard", None),
        P("shard", None),
        P("shard", None),
        P(None, "shard"),
        P(None, "shard"),
        P("expert", None, "shard"),
        P("expert", "shard"),
        P("expert", "shard", None),
        P("expert", "shard"),
    )
    return jax.shard_map(
        per_device, mesh=mesh, in_specs=in_specs, out_specs=out_specs, check_vma=False
    )
```

```python
import functools

import jax
import jax.numpy as jnp
from jax import lax
from jax.experimental import pallas as pl
from jax.experimental.pallas import tpu as pltpu
from jax.sharding import PartitionSpec as P

HEADS = 8
HEAD_DIM = 64
SEQ = 197
EPS = 1e-06
ROW = 16
WIN = 208
TILE = 160
GATHER = 208
MLP = 256
SCATTER = 256
LANES = 128
NEG = -1e30
SCALING = HEAD_DIM ** (-0.5)
GELU_C = 0.7978845608028654
GELU_K = 0.044715
f32 = jnp.float32
bf16 = jnp.bfloat16
VMEM_SPEC = pl.BlockSpec(memory_space=pltpu.VMEM)
SMEM_SPEC = pl.BlockSpec(memory_space=pltpu.SMEM)
ANY_SPEC = pl.BlockSpec(memory_space=pl.ANY)
VMEM_LIMIT = 60 * 1024 * 1024
FORWARD_US = 12
BACKWARD_US = 20


def up_to(value, step):
    return (value + step - 1) // step * step


def dot(left, right):
    return jnp.dot(left, right, preferred_element_type=f32)


def dot_last(left, right):
    return lax.dot_general(left, right, (((1,), (1,)), ((), ())), preferred_element_type=f32)


def dot_first(left, right):
    return lax.dot_general(left, right, (((0,), (0,)), ((), ())), preferred_element_type=f32)


def swap(array, axis, ways, bit):
    return lax.ppermute(array, axis, [(i, i ^ bit) for i in range(ways)])


def cost(microseconds):
    return pl.CostEstimate(
        flops=int(microseconds * 1.15e9), bytes_accessed=1 << 20, transcendentals=0
    )


def params():
    return pltpu.CompilerParams(vmem_limit_bytes=VMEM_LIMIT)


def normalise(rows):
    mean = jnp.mean(rows, axis=-1, keepdims=True)
    centered = rows - mean
    variance = jnp.mean(centered * centered, axis=-1, keepdims=True)
    return centered, lax.rsqrt(variance + EPS)


def place_dense(shard, tiles, mixer, merge, normt, sems):
    copies = []
    columns = mixer.shape[1]
    last = tiles[0].shape[1] - LANES
    for k, tile in enumerate(tiles):
        copies.append(
            pltpu.make_async_copy(
                tile.at[0:ROW, last : last + LANES], normt.at[k], sems.at[2 * len(tiles) + k]
            )
        )
    for k, tile in enumerate(tiles):
        rows = tile.shape[0]
        base = pl.multiple_of((shard ^ k) * rows, rows)
        copies.append(
            pltpu.make_async_copy(
                tile.at[:, 0:columns], mixer.at[pl.ds(base, rows)], sems.at[2 * k]
            )
        )
        copies.append(
            pltpu.make_async_copy(
                tile.at[:, columns : columns + merge.shape[1]],
                merge.at[pl.ds(base, rows)],
                sems.at[2 * k + 1],
            )
        )
    return copies


def place_columns(shard, smalls, into, first):
    width = into.shape[1] // len(smalls)
    for k, small in enumerate(smalls):
        if width % LANES == 0:
            base = pl.multiple_of((shard ^ k) * width, width)
            into[:, pl.ds(base, width)] = small[:, first : first + width]
            continue
        for place in range(len(smalls)):

            @pl.when((shard ^ k) == place)
            def _():
                into[:, place * width : (place + 1) * width] = small[:, first : first + width]


def place_norms(shard, normt, norms):
    tiles = [normt[k][0:8].astype(f32) for k in range(normt.shape[0])]
    place_columns(shard, tiles, norms, 0)


def pack_kernel(mixer, merge, router, gain, shift, up, inner, down, outer, dense, near, row, sems):
    columns, width = mixer.shape[1], merge.shape[1]
    own, hidden = gain.shape[1], up.shape[2]
    last = columns + width
    moves = [
        (mixer, dense.at[:, 0:columns]),
        (merge, dense.at[:, columns:last]),
        (down.at[0], near.at[hidden : 2 * hidden]),
    ]
    for fold in range(width // hidden):
        at = slice(fold * hidden, (fold + 1) * hidden)
        moves.append((up.at[0, at], near.at[0:hidden, at]))
    copies = [pltpu.make_async_copy(source, into, sems.at[i]) for i, (source, into) in enumerate(moves)]
    for copy in copies:
        copy.start()
    dense[:, last : last + 2 * LANES] = jnp.zeros((dense.shape[0], 2 * LANES), bf16)
    dense[:, last : last + router.shape[1]] = router[...]
    row[...] = jnp.zeros(row.shape, f32)
    row[0:2, 0:own] = gain[...].astype(f32)
    row[2:4, 0:own] = shift[...].astype(f32)
    dense[0:ROW, last + LANES : last + 2 * LANES] = row[:, 0:LANES].astype(bf16)
    row[...] = jnp.zeros(row.shape, f32)
    row[0:1, 0:hidden] = inner[...].astype(f32)
    row[1:2, 0:own] = outer[...].astype(f32)
    near[2 * hidden : 2 * hidden + ROW] = row[...].astype(bf16)
    for copy in copies:
        copy.wait()


def pack(mixer, merge, router, gain, shift, up, inner, down, outer):
    own, width = merge.shape
    hidden = up.shape[2]
    return pl.pallas_call(
        pack_kernel,
        name="pack",
        out_shape=(
            jax.ShapeDtypeStruct((own, mixer.shape[1] + width + 2 * LANES), bf16),
            jax.ShapeDtypeStruct((2 * hidden + ROW, width), bf16),
        ),
        in_specs=[ANY_SPEC] * 2 + [VMEM_SPEC] * 3 + [ANY_SPEC, VMEM_SPEC, ANY_SPEC, VMEM_SPEC],
        out_specs=(VMEM_SPEC, VMEM_SPEC),
        scratch_shapes=[
            pltpu.VMEM((ROW, width), f32),
            pltpu.SemaphoreType.DMA((3 + width // hidden,)),
        ],
        compiler_params=params(),
        cost_estimate=cost(2),
    )(mixer, merge, router, gain, shift, up, inner, down, outer)


def row_tiles(rows):
    return [slice(first, min(first + TILE, rows)) for first in range(0, rows, TILE)]


def image_window(base, image):
    first = base + image * SEQ
    start = pl.multiple_of(first // ROW * ROW, ROW)
    offset = first - start
    rows = lax.broadcasted_iota(jnp.int32, (WIN, 1), 0)
    columns = lax.broadcasted_iota(jnp.int32, (1, WIN), 1)
    row_in = (rows >= offset) & (rows < offset + SEQ)
    column_in = (columns >= offset) & (columns < offset + SEQ)
    return start, row_in, column_in


def attention_forward_kernel(n_tiles, base, images, *refs):
    shard_ref, tok = refs[0], refs[1]
    dense = refs[2 : 2 + n_tiles]
    qkv, att, weights, res, normed_two, mixer, merge, normt, norms, sems = refs[2 + n_tiles :]
    shard = shard_ref[0]
    width = tok.shape[1]
    copies = place_dense(shard, dense, mixer, merge, normt, sems)
    for copy in copies:
        copy.start()
    for copy in copies:
        copy.wait()
    place_norms(shard, normt, norms)
    for rows in row_tiles(tok.shape[0]):
        centered, rate = normalise(tok[rows].astype(f32))
        normed = (centered * rate * norms[0:1] + norms[2:3]).astype(bf16)
        qkv[rows] = dot(normed, mixer[...]).astype(bf16)
    att[...] = jnp.zeros(att.shape, bf16)
    lane = lax.broadcasted_iota(jnp.int32, (1, LANES), 1)

    def image_step(image, carry):
        start, row_in, column_in = image_window(base, image)
        window = pl.ds(start, WIN)
        for slab in range(width // LANES):
            q = qkv[window, slab * LANES : (slab + 1) * LANES]
            k = qkv[window, width + slab * LANES : width + (slab + 1) * LANES]
            v = qkv[window, 2 * width + slab * LANES : 2 * width + (slab + 1) * LANES]
            outs = []
            for half in range(2):
                mine = (lane >= half * HEAD_DIM) & (lane < (half + 1) * HEAD_DIM)
                scores = dot_last(jnp.where(mine, q, jnp.zeros_like(q)), k) * SCALING
                scores = jnp.where(column_in, scores, NEG)
                top = jnp.max(scores, axis=-1, keepdims=True)
                powers = jnp.exp(scores - top)
                total = jnp.sum(powers, axis=-1, keepdims=True)
                low = (powers * jnp.where(row_in, 1.0 / total, 0.0)).astype(bf16)
                weights[image, 2 * slab + half] = low
                outs.append(dot(low, v))
            out = jnp.where(lane < HEAD_DIM, outs[0], outs[1]).astype(bf16)
            columns = slice(slab * LANES, (slab + 1) * LANES)
            att[window, columns] = att[window, columns] + out
        return carry

    lax.fori_loop(0, images, image_step, 0)
    for rows in row_tiles(tok.shape[0]):
        residual = tok[rows].astype(f32) + dot(att[rows], merge[...])
        res[rows] = residual
        centered, rate = normalise(residual)
        normed_two[rows] = (centered * rate * norms[1:2] + norms[3:4]).astype(bf16)


def attention_forward(shard, tok, dense, base, images):
    rows, width = tok.shape
    n = len(dense)
    return pl.pallas_call(
        functools.partial(attention_forward_kernel, n, base, images),
        name="attention_forward",
        out_shape=(
            jax.ShapeDtypeStruct((rows, 3 * width), bf16),
            jax.ShapeDtypeStruct((rows, width), bf16),
            jax.ShapeDtypeStruct((images, HEADS, WIN, WIN), bf16),
            jax.ShapeDtypeStruct((rows, width), f32),
            jax.ShapeDtypeStruct((rows, width), bf16),
        ),
        in_specs=[SMEM_SPEC, VMEM_SPEC] + [ANY_SPEC] * n,
        out_specs=(VMEM_SPEC,) * 5,
        scratch_shapes=[
            pltpu.VMEM((width, 3 * width), bf16),
            pltpu.VMEM((width, width), bf16),
            pltpu.VMEM((n, ROW, LANES), bf16),
            pltpu.VMEM((8, width), f32),
            pltpu.SemaphoreType.DMA((3 * n,)),
        ],
        compiler_params=params(),
        cost_estimate=cost(7),
    )(shard, tok, *dense)


def weight_copies(shard, dense, tiles, router, up, down, bias, sems, router_lane):
    n = len(dense)
    width, hidden = up.shape[2], up.shape[3]
    folds = width // hidden
    routers, weights = [], [[] for _ in range(len(tiles) // n)]
    for k, tile in enumerate(dense):
        rows = tile.shape[0]
        base = pl.multiple_of((shard ^ k) * rows, rows)
        routers.append(
            pltpu.make_async_copy(
                tile.at[:, router_lane : router_lane + LANES], router.at[pl.ds(base, rows)], sems.at[0, 0, k]
            )
        )
    for j in range(len(weights)):
        for k in range(n):
            tile = tiles[j * n + k]
            for fold in range(folds):
                at = slice(fold * hidden, (fold + 1) * hidden)
                weights[j].append(
                    pltpu.make_async_copy(
                        tile.at[0:hidden, at], up.at[j, k, at], sems.at[1 + j, fold, k]
                    )
                )
            weights[j].append(
                pltpu.make_async_copy(
                    tile.at[hidden : 2 * hidden], down.at[j, k], sems.at[1 + j, folds, k]
                )
            )
            weights[j].append(
                pltpu.make_async_copy(
                    tile.at[2 * hidden : 2 * hidden + ROW], bias.at[j, k], sems.at[1 + j, folds + 1, k]
                )
            )
    return routers, weights


def block_starts(group, counts, js):
    starts = []
    for j in js:
        at, firsts = jnp.int32(0), []
        for b in range(group):
            firsts.append(pl.multiple_of(at, ROW))
            at = at + (counts[2 * b + j] + ROW - 1) // ROW * ROW
        starts.append((firsts, pl.multiple_of(at, ROW)))
    return starts


def gather_rows(js, group, counts, pos, blocks, into, starts):
    width = into.shape[2]
    row = lax.broadcasted_iota(jnp.int32, (GATHER, 1), 0)
    for b in range(group):
        hot = [
            jnp.where(pos[2 * b + j : 2 * b + j + 1, :] == row, 1.0, 0.0).astype(bf16) for j in js
        ]
        rows = dot(jnp.concatenate(hot, axis=0), blocks[b]).astype(bf16)
        for i, j in enumerate(js):
            base = starts[i][0][b]
            into[i, pl.ds(base, GATHER), :] = rows[i * GATHER : (i + 1) * GATHER]

            def more(step, carry, i=i, j=j, base=base):
                some = jnp.where(pos[2 * b + j : 2 * b + j + 1, :] == row + step * GATHER, 1.0, 0.0)
                at = pl.multiple_of(base + step * GATHER, ROW)
                into[i, pl.ds(at, GATHER), :] = dot(some.astype(bf16), blocks[b]).astype(bf16)
                return carry

            lax.fori_loop(1, (counts[2 * b + j] + GATHER - 1) // GATHER, more, 0)
    for i in range(len(js)):
        into[i, pl.ds(starts[i][1], MLP), :] = jnp.zeros((MLP, width), bf16)


def scatter_rows(js, group, counts, places, source, outs, staged, sems, starts, total, before=()):
    column = lax.broadcasted_iota(jnp.int32, (1, SCATTER), 1)

    def leave(b):
        return pltpu.make_async_copy(staged.at[b % 2], outs[b], sems.at[b % 2])

    for b in range(group):
        mine = [places[:, 2 * b + j : 2 * b + j + 1] for j in js]
        hot = jnp.concatenate(
            [jnp.where(place == column, 1.0, 0.0).astype(bf16) for place in mine], axis=1
        )
        rows = jnp.concatenate(
            [source[i, pl.ds(starts[i][0][b], SCATTER), :] for i in range(len(js))], axis=0
        )
        if b >= 2:
            leave(b - 2).wait()
        value = dot(hot, rows)
        if before:
            value = value + before[b][...].astype(f32)
        staged[b % 2] = value.astype(bf16)
        most = counts[2 * b + js[0]]
        for j in js[1:]:
            most = jnp.maximum(most, counts[2 * b + j])

        @pl.when(most > SCATTER)
        def _():
            total[...] = value
            for i, j in enumerate(js):

                def more(step, carry, i=i):
                    some = jnp.where(mine[i] == column + step * SCATTER, 1.0, 0.0).astype(bf16)
                    at = pl.multiple_of(starts[i][0][b] + step * SCATTER, ROW)
                    total[...] += dot(some, source[i, pl.ds(at, SCATTER), :])
                    return carry

                lax.fori_loop(1, (counts[2 * b + j] + SCATTER - 1) // SCATTER, more, 0)
            staged[b % 2] = total[...].astype(bf16)

        leave(b).start()
    for b in range(max(0, group - 2), group):
        leave(b).wait()


def block_copies(refs, blocks, sems):
    return [pltpu.make_async_copy(ref, blocks.at[b], sems.at[b]) for b, ref in enumerate(refs)]


def tile_at(i):
    return pl.ds(pl.multiple_of(i * MLP, MLP), MLP)


def drain(copies, tiles):
    for back in (2, 1):

        @pl.when(tiles >= back)
        def _():
            for copy in copies(tiles - back):
                copy.wait()


def expert_forward_kernel(n, group, experts, router_lane, j, *refs):
    shard_ref, e_ref, counts, pos, places = refs[:5]
    refs = refs[5:]
    sources, dense, tiles_in, refs = refs[:group], refs[group : group + n], refs[group + n : group + 2 * n], refs[group + 2 * n :]
    before, refs = refs[: group * j], refs[group * j :]
    outs, refs = refs[:group], refs[group:]
    x_out, y_out, probs_out, act_out, slope_out = refs[:5]
    blocks, up, down, bias, router, outer, x_rows, scaled, total, staged, act, slope, y, probs = refs[5:19]
    sems, block_sems, leave_sems, out_sems, x_sems = refs[19:]
    shard = shard_ref[0]
    hidden_width = up.shape[3]
    width = up.shape[2]
    arrivals = block_copies(sources, blocks, block_sems)
    routers, weights = weight_copies(shard, dense, tiles_in, router, up, down, bias, sems, router_lane)
    for copy in arrivals:
        copy.start()
    for copy in arrivals:
        copy.wait()
    for copy in routers + weights[0]:
        copy.start()
    starts = block_starts(group, counts, (j,))
    gather_rows((j,), group, counts, pos, blocks, x_rows, starts)
    for copy in routers:
        copy.wait()
    lane = lax.broadcasted_iota(jnp.int32, (1, LANES), 1)
    tiles = (starts[0][1] + MLP - 1) // MLP

    def saves(i):
        slot = lax.rem(i, 2)
        return [
            pltpu.make_async_copy(source.at[slot], into.at[0, tile_at(i)], out_sems.at[m, slot])
            for m, (source, into) in enumerate(
                ((act, act_out), (slope, slope_out), (y, y_out), (probs, probs_out))
            )
        ]

    def save_x(i):
        return pltpu.make_async_copy(x_rows.at[0, tile_at(i)], x_out.at[0, tile_at(i)], x_sems.at[0, i])

    for copy in weights[0]:
        copy.wait()
    place_columns(shard, [bias[0, k][0:8].astype(f32) for k in range(n)], outer.at[0], 0)

    def tile_step(i, carry):
        slot = lax.rem(i, 2)

        @pl.when(i >= 2)
        def _():
            for copy in saves(i - 2):
                copy.wait()

        save_x(i).start()
        x = x_rows[0, tile_at(i), :]
        logits = jnp.where(lane < experts, dot(x, router[...]), NEG)
        powers = jnp.exp(logits - jnp.max(logits, axis=-1, keepdims=True))
        shares = powers * (1.0 / jnp.sum(powers, axis=-1, keepdims=True))
        probs[slot] = shares
        gate = jnp.sum(jnp.where(lane == e_ref[j], shares, 0.0), axis=-1, keepdims=True)
        for k in range(n):
            hidden = dot(x, up[0, k]) + bias[0, k, 0:1, 0:hidden_width].astype(f32)
            square = hidden * hidden
            share = 0.5 * jnp.tanh(hidden * (GELU_C + GELU_C * GELU_K * square)) + 0.5
            active = hidden * share
            columns = slice(k * hidden_width, (k + 1) * hidden_width)
            act[slot, :, columns] = active.astype(bf16)
            slope[slot, :, columns] = (
                share
                + (active - active * share) * (2.0 * GELU_C + 6.0 * GELU_C * GELU_K * square)
            ).astype(bf16)
        acc = jnp.broadcast_to(outer[0, 1:2], (MLP, width))
        for k in range(n):
            acc = acc + dot(act[slot, :, k * hidden_width : (k + 1) * hidden_width], down[0, k])
        low = acc.astype(bf16)
        y[slot] = low
        for copy in saves(i):
            copy.start()
        scaled[0, tile_at(i), :] = (gate * low.astype(f32)).astype(bf16)
        return carry

    lax.fori_loop(0, tiles, tile_step, 0)
    drain(saves, tiles)

    def wait_x(i, carry):
        save_x(i).wait()
        return carry

    lax.fori_loop(0, tiles, wait_x, 0)
    scaled[0, tile_at(tiles), :] = jnp.zeros((MLP, width), bf16)
    scatter_rows((j,), group, counts, places, scaled, outs, staged, leave_sems, starts, total, before)


def expert_rows(group, capacity):
    return up_to(group * up_to(capacity, ROW), MLP) + MLP


def expert_forward(j, scalars, pos, places, sources, dense, tiles, group, experts, capacity, router_lane, before=()):
    n = len(dense)
    width = sources[0].shape[1]
    tokens = pos.shape[1]
    hidden = (tiles[0].shape[0] - ROW) // 2
    rows = expert_rows(group, capacity)
    return pl.pallas_call(
        functools.partial(expert_forward_kernel, n, group, experts, router_lane, j),
        name="expert_forward",
        out_shape=[jax.ShapeDtypeStruct((tokens, width), bf16)] * group
        + [jax.ShapeDtypeStruct((1, rows, width), bf16)] * 2
        + [jax.ShapeDtypeStruct((1, rows, LANES), f32)]
        + [jax.ShapeDtypeStruct((1, rows, hidden * n), bf16)] * 2,
        in_specs=[SMEM_SPEC] * 3
        + [VMEM_SPEC] * 2
        + [ANY_SPEC] * (group + 2 * n)
        + [VMEM_SPEC] * len(before),
        out_specs=[ANY_SPEC] * (group + 5),
        scratch_shapes=[
            pltpu.VMEM((group, tokens, width), bf16),
            pltpu.VMEM((1, n, width, hidden), bf16),
            pltpu.VMEM((1, n, hidden, width), bf16),
            pltpu.VMEM((1, n, ROW, width), bf16),
            pltpu.VMEM((width, LANES), bf16),
            pltpu.VMEM((1, 8, width), f32),
            pltpu.VMEM((1, rows, width), bf16),
            pltpu.VMEM((1, rows, width), bf16),
            pltpu.VMEM((tokens, width), f32),
            pltpu.VMEM((2, tokens, width), bf16),
            pltpu.VMEM((2, MLP, hidden * n), bf16),
            pltpu.VMEM((2, MLP, hidden * n), bf16),
            pltpu.VMEM((2, MLP, width), bf16),
            pltpu.VMEM((2, MLP, LANES), f32),
            pltpu.SemaphoreType.DMA((2, width // hidden + 2, n)),
            pltpu.SemaphoreType.DMA((group,)),
            pltpu.SemaphoreType.DMA((2,)),
            pltpu.SemaphoreType.DMA((4, 2)),
            pltpu.SemaphoreType.DMA((1, rows // MLP)),
        ],
        compiler_params=params(),
        cost_estimate=cost(FORWARD_US),
    )(*scalars, pos, places, *sources, *dense, *tiles, *before)


def expert_backward_kernel(n, group, router_lane, *refs):
    shard_ref, e_ref, counts, pos, places = refs[:5]
    refs = refs[5:]
    sources, dense, tiles_in, refs = refs[:group], refs[group : group + n], refs[group + n : group + 3 * n], refs[group + 3 * n :]
    saved_in, refs = (refs[0:4], refs[4:8]), refs[8:]
    outs, refs = refs[:group], refs[group:]
    pg_out, hg_out, router_grad, inner_grad, outer_grad = refs[:5]
    blocks, up, down, bias, router, f_rows, b_rows, total, staged, hg, pg, slope, x, y, probs = refs[5:20]
    sems, block_sems, leave_sems, out_sems, in_sems = refs[20:]
    shard = shard_ref[0]
    hidden_width = up.shape[3]
    width = up.shape[2]
    arrivals = block_copies(sources, blocks, block_sems)
    routers, weights = weight_copies(shard, dense, tiles_in, router, up, down, bias, sems, router_lane)
    for copy in arrivals:
        copy.start()
    router_grad[...] = jnp.zeros(router_grad.shape, f32)
    inner_grad[...] = jnp.zeros(inner_grad.shape, f32)
    outer_grad[...] = jnp.zeros(outer_grad.shape, f32)
    for copy in arrivals:
        copy.wait()
    for copy in routers + weights[0]:
        copy.start()
    starts = block_starts(group, counts, (0, 1))
    gather_rows((0, 1), group, counts, pos, blocks, f_rows, starts)
    for copy in routers:
        copy.wait()
    lane = lax.broadcasted_iota(jnp.int32, (1, LANES), 1)
    for j in range(2):
        tiles = (starts[j][1] + MLP - 1) // MLP

        def saves(i, j=j):
            slot = lax.rem(i, 2)
            return (
                pltpu.make_async_copy(hg.at[slot], hg_out.at[j, tile_at(i)], out_sems.at[0, slot]),
                pltpu.make_async_copy(pg.at[slot], pg_out.at[j, tile_at(i)], out_sems.at[1, slot]),
            )

        def loads(i, j=j):
            slot = lax.rem(i, 2)
            return [
                pltpu.make_async_copy(source.at[0, tile_at(i)], into.at[slot], in_sems.at[m, slot])
                for m, (source, into) in enumerate(zip(saved_in[j], (x, y, probs, slope)))
            ]

        @pl.when(tiles >= 1)
        def _():
            for copy in loads(0):
                copy.start()

        for copy in weights[j]:
            copy.wait()
        if j == 0:
            for copy in weights[1]:
                copy.start()

        def tile_step(i, carry):
            slot = lax.rem(i, 2)

            @pl.when(i + 1 < tiles)
            def _():
                for copy in loads(i + 1):
                    copy.start()

            @pl.when(i >= 2)
            def _():
                for copy in saves(i - 2):
                    copy.wait()

            for copy in loads(i):
                copy.wait()
            f = f_rows[j, tile_at(i), :].astype(f32)
            shares = probs[slot]
            mine = lane == e_ref[j]
            gate = jnp.sum(jnp.where(mine, shares, 0.0), axis=-1, keepdims=True)
            wide = gate * f
            pg[slot] = wide.astype(bf16)
            gate_grad = jnp.sum(f * y[slot].astype(f32), axis=-1, keepdims=True)
            logit = gate_grad * gate * (jnp.where(mine, 1.0, 0.0) - shares)
            high = logit.astype(bf16)
            rest = (logit - high.astype(f32)).astype(bf16)
            outer_grad[j : j + 1] += jnp.sum(wide, axis=0, keepdims=True)
            for k in range(n):
                columns = slice(k * hidden_width, (k + 1) * hidden_width)
                grad = dot_last(pg[slot], down[j, k]) * slope[slot, :, columns].astype(f32)
                hg[slot, :, columns] = grad.astype(bf16)
                inner_grad[j : j + 1, columns] += jnp.sum(grad, axis=0, keepdims=True)
            for copy in saves(i):
                copy.start()
            turned = x[slot].T
            router_grad[...] += dot(turned, high) + dot(turned, rest)
            acc = dot_last(high, router[...]) + dot_last(rest, router[...])
            for k in range(n):
                acc = acc + dot_last(hg[slot, :, k * hidden_width : (k + 1) * hidden_width], up[j, k])
            b_rows[j, tile_at(i), :] = acc.astype(bf16)
            return carry

        lax.fori_loop(0, tiles, tile_step, 0)
        drain(saves, tiles)
        b_rows[j, tile_at(tiles), :] = jnp.zeros((MLP, width), bf16)
    scatter_rows((0, 1), group, counts, places, b_rows, outs, staged, leave_sems, starts, total)


def expert_backward(scalars, pos, places, sources, dense, tiles, saved, group, capacity, router_lane):
    n = len(dense)
    width = sources[0].shape[1]
    tokens = pos.shape[1]
    hidden = (tiles[0].shape[0] - ROW) // 2
    rows = expert_rows(group, capacity)
    return pl.pallas_call(
        functools.partial(expert_backward_kernel, n, group, router_lane),
        name="expert_backward",
        out_shape=[jax.ShapeDtypeStruct((tokens, width), bf16)] * group
        + [
            jax.ShapeDtypeStruct((2, rows, width), bf16),
            jax.ShapeDtypeStruct((2, rows, hidden * n), bf16),
            jax.ShapeDtypeStruct((width, LANES), f32),
            jax.ShapeDtypeStruct((8, hidden * n), f32),
            jax.ShapeDtypeStruct((8, width), f32),
        ],
        in_specs=[SMEM_SPEC] * 3 + [VMEM_SPEC] * 2 + [ANY_SPEC] * (group + 3 * n + 8),
        out_specs=[ANY_SPEC] * (group + 2) + [VMEM_SPEC] * 3,
        scratch_shapes=[
            pltpu.VMEM((group, tokens, width), bf16),
            pltpu.VMEM((2, n, width, hidden), bf16),
            pltpu.VMEM((2, n, hidden, width), bf16),
            pltpu.VMEM((2, n, ROW, width), bf16),
            pltpu.VMEM((width, LANES), bf16),
            pltpu.VMEM((2, rows, width), bf16),
            pltpu.VMEM((2, rows, width), bf16),
            pltpu.VMEM((tokens, width), f32),
            pltpu.VMEM((2, tokens, width), bf16),
            pltpu.VMEM((2, MLP, hidden * n), bf16),
            pltpu.VMEM((2, MLP, width), bf16),
            pltpu.VMEM((2, MLP, hidden * n), bf16),
            pltpu.VMEM((2, MLP, width), bf16),
            pltpu.VMEM((2, MLP, width), bf16),
            pltpu.VMEM((2, MLP, LANES), f32),
            pltpu.SemaphoreType.DMA((3, width // hidden + 2, n)),
            pltpu.SemaphoreType.DMA((group,)),
            pltpu.SemaphoreType.DMA((2,)),
            pltpu.SemaphoreType.DMA((2, 2)),
            pltpu.SemaphoreType.DMA((4, 2)),
        ],
        compiler_params=params(),
        cost_estimate=cost(BACKWARD_US),
    )(*scalars, pos, places, *sources, *dense, *tiles, *saved)


def put_columns(shard, k, n, source, row, into):
    width = source.shape[1] // n
    if width % LANES == 0:
        base = pl.multiple_of((shard ^ k) * width, width)
        into[:, 0:width] = source[row : row + 1, pl.ds(base, width)].astype(into.dtype)
        return
    for place in range(n):

        @pl.when((shard ^ k) == place)
        def _():
            into[:, 0:width] = source[row : row + 1, place * width : (place + 1) * width].astype(into.dtype)


def weight_grads_kernel(n, experts, added, shard_ref, tiles_ref, *refs):
    saved, refs = refs[: 2 * len(experts) + 2], refs[2 * len(experts) + 2 :]
    inner_part, outer_part, refs = refs[0], refs[1], refs[2:]
    before, refs = refs[:added], refs[added:]
    results, refs = refs[: 2 * len(experts)], refs[2 * len(experts) :]
    x, pg, act, hg, up_total, down_total, row, sems = refs
    width, hidden = up_total.shape[1:]
    folds = width // hidden
    shard = shard_ref[0]
    for turn, j in enumerate(experts):
        tiles = tiles_ref[j]
        for k in range(n):
            up_total[k] = jnp.zeros((width, hidden), f32)
            down_total[k] = jnp.zeros((width, hidden), f32)

        def loads(i, j=j, turn=turn):
            slot = lax.rem(i, 2)
            sources = (
                saved[2 * turn].at[0, tile_at(i)],
                saved[-2].at[j, tile_at(i)],
                saved[2 * turn + 1].at[0, tile_at(i)],
                saved[-1].at[j, tile_at(i)],
            )
            return [
                pltpu.make_async_copy(source, into.at[slot], sems.at[m, slot])
                for m, (source, into) in enumerate(zip(sources, (x, pg, act, hg)))
            ]

        @pl.when(tiles >= 1)
        def _():
            for copy in loads(0):
                copy.start()

        def tile_step(i, carry):
            slot = lax.rem(i, 2)

            @pl.when(i + 1 < tiles)
            def _():
                for copy in loads(i + 1):
                    copy.start()

            for copy in loads(i):
                copy.wait()
            turned = x[slot].T
            turned_grad = pg[slot].T
            for k in range(n):
                columns = slice(k * hidden, (k + 1) * hidden)
                up_total[k] += dot(turned, hg[slot, :, columns])
                down_total[k] += dot(turned_grad, act[slot, :, columns])
            return carry

        lax.fori_loop(0, tiles, tile_step, 0)
        row[8:16] = outer_part[...]
        for k in range(n):
            into = results[2 * turn + 1 - k % 2].at[k // 2]
            base = before[2 * turn + 1 - k % 2].at[k // 2] if added else None

            def put(rows, columns, value):
                if added:
                    value = value + base[rows, columns].astype(f32)
                into[rows, columns] = value.astype(bf16)

            for fold in range(folds):
                at = slice(fold * hidden, (fold + 1) * hidden)
                put(slice(0, hidden), at, up_total[k, at])
            put(slice(hidden, 2 * hidden), slice(0, width), down_total[k].T)
            row[0:8] = jnp.zeros((8, width), f32)
            row[0:1, 0:hidden] = inner_part[j : j + 1, k * hidden : (k + 1) * hidden]
            put_columns(shard, k, n, row, 8 + j, row.at[1:2])
            row[8:16] = outer_part[...]
            put(slice(2 * hidden, 2 * hidden + 8), slice(0, width), row[0:8])
            into[2 * hidden + 8 : 2 * hidden + ROW] = jnp.zeros((ROW - 8, width), bf16)


def weight_grads(experts, shard, tiles, saved, biases, n, before=()):
    rows_in, grads = saved
    _, rows, width = grads[0].shape
    hidden = grads[1].shape[2] // n
    held = [array for j in experts for array in rows_in[j]] + list(grads)
    shape = jax.ShapeDtypeStruct((n // 2, 2 * hidden + ROW, width), bf16)
    return pl.pallas_call(
        functools.partial(weight_grads_kernel, n, experts, len(before)),
        name="weight_grads",
        out_shape=(shape,) * (2 * len(experts)),
        in_specs=[SMEM_SPEC] * 2 + [ANY_SPEC] * len(held) + [VMEM_SPEC] * (2 + len(before)),
        out_specs=(VMEM_SPEC,) * (2 * len(experts)),
        scratch_shapes=[
            pltpu.VMEM((2, MLP, width), bf16),
            pltpu.VMEM((2, MLP, width), bf16),
            pltpu.VMEM((2, MLP, hidden * n), bf16),
            pltpu.VMEM((2, MLP, hidden * n), bf16),
            pltpu.VMEM((n, width, hidden), f32),
            pltpu.VMEM((n, width, hidden), f32),
            pltpu.VMEM((ROW, width), f32),
            pltpu.SemaphoreType.DMA((4, 2)),
        ],
        compiler_params=params(),
        cost_estimate=cost(8 * len(experts)),
    )(shard, tiles, *held, *biases, *before)


def norm_backward(rows, gain, grad):
    centered, rate = normalise(rows)
    unit = centered * rate
    scaled = grad * gain
    back = rate * (
        scaled
        - jnp.mean(scaled, axis=-1, keepdims=True)
        - unit * jnp.mean(scaled * unit, axis=-1, keepdims=True)
    )
    return (
        back,
        jnp.sum(grad * unit, axis=0, keepdims=True),
        jnp.sum(grad, axis=0, keepdims=True),
        unit,
    )


def attention_backward_kernel(n_tiles, parts, base, images, overlap, last, *refs):
    shard_ref, refs = refs[0], refs[1:]
    grads, refs = refs[:parts], refs[parts:]
    fg, res, att, qkv, weights, tok = refs[:6]
    dense, refs = refs[6 : 6 + n_tiles], refs[6 + n_tiles :]
    before = None
    if overlap:
        before, refs = refs[:4], refs[4:]
    if last:
        router_parts, refs = refs[:last], refs[last:]
        token_grad, norm_grad, send, keep = refs[:4]
        mixer_grad, merge_grad = refs[-2:]
        refs = refs[:-2]
    else:
        token_grad, mixer_grad, merge_grad, norm_grad = refs[:4]
    mixer, merge, normt, norms, dres, low, datt, normed, mg, sems = refs[4:]
    shard = shard_ref[0]
    width = tok.shape[1]
    n_rows = tok.shape[0]
    copies = place_dense(shard, dense, mixer, merge, normt, sems)
    for copy in copies:
        copy.start()
    for copy in copies:
        copy.wait()
    place_norms(shard, normt, norms)
    norm_grad[...] = before[3][...] if overlap else jnp.zeros(norm_grad.shape, f32)
    for rows in row_tiles(n_rows):
        grad = grads[0][rows].astype(f32)
        for other in grads[1:]:
            grad = grad + other[rows].astype(f32)
        back, gain, shift, _ = norm_backward(res[rows], norms[1:2], grad)
        norm_grad[1:2] += gain
        norm_grad[3:4] += shift
        total = fg[rows] + back
        dres[rows] = total
        low[rows] = total.astype(bf16)
        datt[rows] = dot_last(low[rows], merge[...]).astype(bf16)
    mg[...] = jnp.zeros(mg.shape, bf16)
    merge_term = dot_first(att[...], low[...])
    merge_grad[...] = before[2][...] + merge_term if overlap else merge_term
    lane = lax.broadcasted_iota(jnp.int32, (1, LANES), 1)

    def image_step(image, carry):
        start, _, _ = image_window(base, image)
        window = pl.ds(start, WIN)
        for slab in range(width // LANES):
            q_at = slice(slab * LANES, (slab + 1) * LANES)
            k_at = slice(width + slab * LANES, width + (slab + 1) * LANES)
            v_at = slice(2 * width + slab * LANES, 2 * width + (slab + 1) * LANES)
            q, k, v = qkv[window, q_at], qkv[window, k_at], qkv[window, v_at]
            do = datt[window, q_at]
            parts = []
            for half in range(2):
                head = 2 * slab + half
                mine = (lane >= half * HEAD_DIM) & (lane < (half + 1) * HEAD_DIM)
                zero = jnp.zeros_like(q)
                low = weights[image, head]
                dv = dot_first(low, do)
                dw = dot_last(jnp.where(mine, do, zero), v)
                wide = low.astype(f32)
                inner = jnp.sum(wide * dw, axis=-1, keepdims=True)
                ds = (wide * (dw - inner)).astype(bf16)
                parts.append((dot(ds, k) * SCALING, dot_first(ds, q) * SCALING, dv))
            for at, first, second in zip((q_at, k_at, v_at), parts[0], parts[1]):
                both = jnp.where(lane < HEAD_DIM, first, second).astype(bf16)
                mg[window, at] = mg[window, at] + both
        return carry

    lax.fori_loop(0, images, image_step, 0)
    shift_rows = token_grad.shape[0] - n_rows if overlap else 0
    if overlap:
        token_grad[0:shift_rows] = before[0][0:shift_rows]
    for rows in row_tiles(n_rows):
        grad = dot_last(mg[rows], mixer[...])
        back, gain, shift, unit = norm_backward(tok[rows].astype(f32), norms[0:1], grad)
        norm_grad[0:1] += gain
        norm_grad[2:3] += shift
        total = dres[rows] + back
        if overlap and rows.start < overlap:
            both = before[0][shift_rows : shift_rows + overlap]
            token_grad[shift_rows : shift_rows + overlap] = total[0:overlap] + both
            token_grad[shift_rows + overlap : shift_rows + rows.stop] = total[overlap:]
        else:
            token_grad[shift_rows + rows.start : shift_rows + rows.stop] = total
        normed[rows] = (unit * norms[0:1] + norms[2:3]).astype(bf16)
    for c in range(3):
        columns = slice(c * width, (c + 1) * width)
        term = dot_first(normed[...], mg[:, columns])
        mixer_grad[:, columns] = before[1][:, columns] + term if overlap else term
    if last:
        for k in range(n_tiles):
            own = width // n_tiles
            at = pl.ds(pl.multiple_of((shard ^ k) * own, own), own)
            into = (send if k % 2 else keep).at[k // 2]
            into[:, 0 : 3 * width] = mixer_grad[at].astype(bf16)
            into[:, 3 * width : 4 * width] = merge_grad[at].astype(bf16)
            into[:, 4 * width : 4 * width + LANES] = sum(part[at] for part in router_parts).astype(bf16)


def attention_backward(shard, grads, fg, res, att, qkv, weights, tok, dense, base, images, before, start, router_parts):
    rows, width = tok.shape
    n = len(dense)
    overlap = before[0].shape[0] - start if before else 0
    token_shape = jax.ShapeDtypeStruct((start + rows if before else rows, width), f32)
    norm_shape = jax.ShapeDtypeStruct((8, width), f32)
    totals = [pltpu.VMEM((width, 3 * width), f32), pltpu.VMEM((width, width), f32)]
    if router_parts:
        tile = jax.ShapeDtypeStruct((n // 2, width // n, 4 * width + LANES), bf16)
        shapes = (token_shape, norm_shape, tile, tile)
    else:
        shapes = (
            token_shape,
            jax.ShapeDtypeStruct((width, 3 * width), f32),
            jax.ShapeDtypeStruct((width, width), f32),
            norm_shape,
        )
    held = (*grads, fg, res, att, qkv, weights, tok)
    more = (*(before or ()), *router_parts)
    return pl.pallas_call(
        functools.partial(
            attention_backward_kernel, n, len(grads), base, images, overlap, len(router_parts)
        ),
        name="attention_backward",
        out_shape=shapes,
        in_specs=[SMEM_SPEC] + [VMEM_SPEC] * len(held) + [ANY_SPEC] * n + [VMEM_SPEC] * len(more),
        out_specs=(VMEM_SPEC,) * 4,
        scratch_shapes=[
            pltpu.VMEM((width, 3 * width), bf16),
            pltpu.VMEM((width, width), bf16),
            pltpu.VMEM((n, ROW, LANES), bf16),
            pltpu.VMEM((8, width), f32),
            pltpu.VMEM((rows, width), f32),
            pltpu.VMEM((rows, width), bf16),
            pltpu.VMEM((rows, width), bf16),
            pltpu.VMEM((rows, width), bf16),
            pltpu.VMEM((rows, 3 * width), bf16),
            pltpu.SemaphoreType.DMA((3 * n,)),
        ]
        + (totals if router_parts else []),
        compiler_params=params(),
        cost_estimate=cost(17),
    )(shard, *held, *dense, *more)


def bits_of(ways):
    bit = ways // 2
    while bit:
        yield bit
        bit //= 2


def gather_tiles(array, axis, ways, gate=None):
    tiles = {0: array}
    for step, bit in enumerate(bits_of(ways)):
        for k in list(tiles):
            sent = after(tiles[k], *gate) if gate is not None and step else tiles[k]
            tiles[k | bit] = swap(sent, axis, ways, bit)
    return [tiles[k] for k in range(ways)]


def fold_tiles(send, keep, axis, ways):
    sums = (keep.astype(f32) + swap(send, axis, ways, 1).astype(f32)).astype(bf16)

    def rest():
        tiles = sums
        for bit in [bit for bit in reversed(list(bits_of(ways))) if bit > 1]:
            tiles = (tiles[0::2].astype(f32) + swap(tiles[1::2], axis, ways, bit).astype(f32)).astype(bf16)
        return tiles

    return sums, rest


def sum_over(array, axis, ways):
    for bit in bits_of(ways):
        array = array + swap(array, axis, ways, bit)
    return array


def sum_split(array, axis, ways, index, gate, last_gate):
    half = array.shape[0] // 2
    mine = index & 1
    kept = lax.dynamic_slice_in_dim(array, mine * half, half, 0)
    sent = lax.dynamic_slice_in_dim(array, (1 - mine) * half, half, 0)
    part = after(kept.astype(f32) + swap(sent, axis, ways, 1).astype(f32), gate)
    for bit in [bit for bit in reversed(list(bits_of(ways))) if bit > 1]:
        low = part.astype(bf16)
        part = low.astype(f32) + swap(low, axis, ways, bit).astype(f32)
    low = after(part.astype(bf16), last_gate)
    other = swap(low, axis, ways, 1)
    first = jnp.where(mine == 0, low, other)
    second = jnp.where(mine == 0, other, low)
    return jnp.concatenate([first, second], axis=0).astype(f32)


def exchange(array, ways, group):
    return [array] + [swap(array, "expert", ways, b) for b in range(1, group)]


def give_back(blocks, ways, group):
    return [blocks[0]] + [swap(blocks[b], "expert", ways, b) for b in range(1, group)]


def after(value, *others):
    return lax.optimization_barrier((value, *others))[0]


def per_device(
    tokens,
    teacher,
    valid_mask,
    routes,
    mixer_weight,
    merge_weight,
    router_weight,
    norm_gain,
    norm_shift,
    up_weight,
    inner_bias,
    down_weight,
    outer_bias,
):
    ways = lax.axis_size("expert")
    shards = lax.axis_size("shard")
    shard = lax.axis_index("shard").astype(jnp.int32)
    expert = lax.axis_index("expert").astype(jnp.int32)
    token_count, width = tokens.shape
    images = token_count // SEQ
    experts = router_weight.shape[1]
    group = ways // 2
    chunks = 2 if images % 2 == 0 else 1
    chunk_images = images // chunks
    chunk_tokens = chunk_images * SEQ
    capacity = min(chunk_tokens, max(2, 4 * token_count // experts))
    firsts = [c * chunk_tokens for c in range(chunks)]
    starts = [first // 8 * 8 for first in firsts]
    last = max(first - start + (chunk_images - 1) * SEQ for first, start in zip(firsts, starts))
    rows = up_to(last // ROW * ROW + WIN, ROW)
    all_rows = starts[-1] + rows
    shard_rows = width // shards
    hidden = up_weight.shape[2]
    router_lane = 4 * width
    folds = width // hidden

    dense_own, near = pack(
        mixer_weight, merge_weight, router_weight, norm_gain, norm_shift, up_weight, inner_bias, down_weight, outer_bias
    )
    dense = gather_tiles(dense_own, "shard", shards)
    far = swap(near, "expert", ways, group)

    route_rows = jnp.pad(routes, ((0, all_rows - token_count), (0, 0)), constant_values=-1).T
    ids = jnp.arange(experts, dtype=jnp.int32)[:, None]
    named = (route_rows[0:1] == ids) | (route_rows[1:2] == ids)
    order = jnp.arange(all_rows, dtype=jnp.int32)
    in_chunk = (order[None, :] // chunk_tokens) == jnp.arange(chunks, dtype=jnp.int32)[:, None]
    named = (named[None] & in_chunk[:, None, :]).reshape(chunks * experts, all_rows)
    earlier = (order[:, None] < order[None, :]).astype(bf16)
    slots = jnp.dot(named.astype(bf16), earlier, preferred_element_type=f32).astype(jnp.int32)
    slots = jnp.where(named, slots, -1)
    slots = jnp.pad(slots, ((0, 8), (0, 0)), constant_values=jnp.sum(valid_mask))
    slots = after(slots, dense[1])
    slot_blocks = jnp.stack([slots] + [swap(slots, "expert", ways, b) for b in range(1, group)])
    group_count = jnp.sum(slot_blocks[:, -8:, 0:LANES], axis=0).astype(f32)
    shard_count = sum_over(group_count, "shard", shards)
    slot_blocks = slot_blocks[:, :-8].reshape(group, chunks, experts, all_rows)
    chosen = jnp.concatenate(
        [
            lax.dynamic_slice_in_dim(slot_blocks, expert, 1, 2),
            lax.dynamic_slice_in_dim(slot_blocks, expert ^ group, 1, 2),
        ],
        axis=2,
    )
    shard_id = shard[None]
    e_ids = jnp.stack([expert, expert ^ group])
    routing, tile_counts = [], []
    for c in range(chunks):
        pos = chosen[:, c, :, starts[c] : starts[c] + rows].reshape(2 * group, rows)
        counts = jnp.max(pos, axis=1) + 1
        places = jnp.pad(pos.T, ((0, 0), (0, LANES - 2 * group)), constant_values=-1)
        ends = jnp.sum((counts.reshape(group, 2) + ROW - 1) // ROW * ROW, axis=0)
        tile_counts.append((ends + MLP - 1) // MLP)
        routing.append(((shard_id, e_ids, counts), pos, places))

    def chunk_rows(array, c):
        part = array[starts[c] : min(starts[c] + rows, token_count)]
        return jnp.pad(part, ((0, rows - part.shape[0]),) + ((0, 0),) * (part.ndim - 1))

    toks = [chunk_rows(tokens, c) for c in range(chunks)]
    local = jnp.arange(rows, dtype=jnp.int32)[:, None]
    kept, valids = [], []
    for c in range(chunks):
        base = firsts[c] - starts[c]
        mask = (local >= base) & (local < base + chunk_tokens)
        kept.append(mask)
        valids.append(jnp.where(mask, chunk_rows(valid_mask, c).astype(f32)[:, None], 0.0))

    forward = []
    for c in range(chunks):
        gates = (forward[-1][4],) if c else ()
        forward.append(
            attention_forward(shard_id, after(toks[c], *gates), dense, firsts[c] - starts[c], chunk_images)
        )
    attended = forward[-1][4]
    arrivals = []
    arrivals.append(exchange(forward[0][4], ways, group))
    near_tiles = gather_tiles(
        after(near, dense[-1], shard_count, chosen), "shard", shards, (attended, *arrivals[0][1:])
    )
    tiles = near_tiles + gather_tiles(after(far, attended), "shard", shards)
    for c in range(1, chunks):
        arrivals.append(exchange(after(forward[c][4], near_tiles[1]), ways, group))
    valid_count = shard_count + swap(after(shard_count, attended), "expert", ways, group)

    def expert_part(c, j, before, *gates):
        sources = [after(arrivals[c][0], *gates)] + arrivals[c][1:]
        results = expert_forward(
            j,
            *routing[c],
            sources,
            dense,
            tiles[j * shards : (j + 1) * shards],
            group,
            experts,
            capacity,
            router_lane,
            before,
        )
        return results[:group], results[group:]

    nears, held, given = [], [], []
    for c in range(chunks):
        gates = (given[-1][0],) if given else (attended,)
        near_given, near_held = expert_part(c, 0, (), *gates)
        nears.append(near_given)
        held.append([near_held])
        if c < chunks - 1:
            far_given, far_held = expert_part(c, 1, near_given, valid_count)
            given.append(far_given)
            held[c].append(far_held)
    valid_count = valid_count[0, 0]
    scale = token_count * ways * shards / valid_count

    blocks_out, squared, final_grads, input_grads = [], 0.0, [], []
    router_parts, biases, saved, early = [], [], [], ()
    arrived = None
    for c in range(chunks):
        if c == chunks - 1:
            far_given, far_held = expert_part(c, 1, nears[c], *final_grads)
            given.append(far_given)
            held[c].append(far_held)
        parts = given[c] if c == 0 else [given[c][0]] + [after(part, *arrived) for part in given[c][1:]]
        block_out = forward[c][3]
        if c == 0:
            block_out = after(block_out, nears[-1][0])
        for part in give_back(parts, ways, group):
            block_out = block_out + part.astype(f32)
        error = block_out - chunk_rows(teacher, c).astype(f32)
        squared = squared + jnp.sum(valids[c] * jnp.sum(error * error, axis=1, keepdims=True))
        fg = scale * valids[c] * error
        final_grads.append(fg)
        blocks_out.append(jnp.where(kept[c], block_out, 0.0).astype(bf16))
        arrived = exchange(fg.astype(bf16), ways, group)
        if c:
            early = weight_grads(
                (0, 1), shard_id, after(tile_counts[c - 1], fg), saved[c - 1], biases[c - 1], shards, early
            )
            arrived[0] = after(arrived[0], early[0])
            input_grads[c - 1] = [input_grads[c - 1][0]] + [
                after(part, *arrived[1:]) for part in input_grads[c - 1][1:]
            ]
            input_grads[c - 1] = give_back(input_grads[c - 1], ways, group)
        loads = [array for x, y, probs, _, slope in held[c] for array in (x, y, probs, slope)]
        results = expert_backward(
            *routing[c],
            arrived,
            dense,
            tiles,
            loads,
            group,
            capacity,
            router_lane,
        )
        input_grads.append(results[:group])
        pg_rows, hg, router_part, inner_part, outer_part = results[group:]
        router_parts.append(router_part)
        biases.append((inner_part, outer_part))
        saved.append(([(arrays[0], arrays[3]) for arrays in held[c]], (pg_rows, hg)))
    last = chunks - 1
    far_tiles = weight_grads(
        (1,), shard_id, after(tile_counts[last], *input_grads[0][1:]), saved[last], biases[last], shards, early[2:]
    )
    input_grads[last] = give_back(input_grads[last], ways, group)
    far_sums, far_rest = fold_tiles(*far_tiles, "shard", shards)
    before = None
    for c in range(chunks):
        qkv, att, weights, res, _ = forward[c]
        gate = far_sums if c == 0 else far_grad
        before = attention_backward(
            after(shard_id, gate),
            input_grads[c],
            final_grads[c],
            res,
            att,
            qkv,
            weights,
            toks[c],
            dense,
            firsts[c] - starts[c],
            chunk_images,
            before,
            starts[c],
            router_parts if c == last else (),
        )
        if c == 0:
            far_grad = far_rest()
            far_arrived = [
                swap(half, "expert", ways, group) for half in (far_grad[0, :hidden], far_grad[0, hidden:])
            ]
    token_grad, norm_part, *dense_parts = before
    dense_parts[0] = after(dense_parts[0], far_arrived[0])
    dense_sums, dense_rest = fold_tiles(*dense_parts, "shard", shards)
    near_tiles = weight_grads(
        (0,), shard_id, after(tile_counts[last], dense_sums), saved[last], biases[last], shards, early[:2]
    )
    dense_grad = dense_rest()
    near_tiles = (after(near_tiles[0], dense_grad, far_arrived[1]), near_tiles[1])
    near_sums, near_rest = fold_tiles(*near_tiles, "shard", shards)
    near_grad = near_rest()
    up_sum = near_grad[0, :hidden].astype(f32) + far_arrived[0].astype(f32)
    up_grad = jnp.concatenate(
        [up_sum[:, fold * hidden : (fold + 1) * hidden] for fold in range(folds)], axis=0
    )
    rest_sum = near_grad[0, hidden:].astype(f32) + far_arrived[1].astype(f32)
    down_grad = rest_sum[:hidden]
    inner_grad = rest_sum[hidden : hidden + 1, 0:hidden]
    outer_grad = rest_sum[hidden + 1 : hidden + 2, 0:shard_rows]
    dense_sum = sum_split(dense_grad[0], "expert", ways, expert, near_sums, near_grad)
    output = jnp.zeros((all_rows, width), bf16)
    for c in range(chunks):
        output = output + jnp.pad(blocks_out[c], ((starts[c], all_rows - starts[c] - rows), (0, 0)))

    norm_sum = sum_over(sum_over(norm_part.at[4].set(squared), "shard", shards), "expert", ways)
    norm_sum = lax.dynamic_slice_in_dim(norm_sum, shard * shard_rows, shard_rows, 1)
    loss_value = norm_sum[4, 0] / (2.0 * valid_count)
    return (
        output[:token_count],
        loss_value,
        token_grad[:token_count],
        dense_sum[:, : 3 * width],
        dense_sum[:, 3 * width : 4 * width],
        dense_sum[:, 4 * width : 4 * width + experts],
        norm_sum[0:2],
        norm_sum[2:4],
        up_grad[None],
        inner_grad,
        down_grad[None],
        outer_grad,
    )


def solution(mesh):
    in_specs = (
        P(("expert", "shard"), None),
        P(("expert", "shard"), None),
        P(("expert", "shard")),
        P(("expert", "shard"), None),
        P("shard", None),
        P("shard", None),
        P("shard", None),
        P(None, "shard"),
        P(None, "shard"),
        P("expert", None, "shard"),
        P("expert", "shard"),
        P("expert", "shard", None),
        P("expert", "shard"),
    )
    out_specs = (
        P(("expert", "shard"), None),
        P(),
        P(("expert", "shard"), None),
        P("shard", None),
        P("shard", None),
        P("shard", None),
        P(None, "shard"),
        P(None, "shard"),
        P("expert", None, "shard"),
        P("expert", "shard"),
        P("expert", "shard", None),
        P("expert", "shard"),
    )
    return jax.shard_map(
        per_device, mesh=mesh, in_specs=in_specs, out_specs=out_specs, check_vma=False
    )
```

```python
import functools

import jax
import jax.numpy as jnp
from jax import lax
from jax.experimental import pallas as pl
from jax.experimental.pallas import tpu as pltpu
from jax.sharding import PartitionSpec as P

HEADS = 8
HEAD_DIM = 64
SEQ = 197
EPS = 1e-06
ROW = 16
WIN = 208
TILE = 160
GATHER = 208
MLP = 256
SCATTER = 256
LANES = 128
NEG = -1e30
SCALING = HEAD_DIM ** (-0.5)
GELU_C = 0.7978845608028654
GELU_K = 0.044715
f32 = jnp.float32
bf16 = jnp.bfloat16
VMEM_SPEC = pl.BlockSpec(memory_space=pltpu.VMEM)
SMEM_SPEC = pl.BlockSpec(memory_space=pltpu.SMEM)
ANY_SPEC = pl.BlockSpec(memory_space=pl.ANY)
VMEM_LIMIT = 60 * 1024 * 1024
FORWARD_US = 12
BACKWARD_US = 20


def up_to(value, step):
    return (value + step - 1) // step * step


def dot(left, right):
    return jnp.dot(left, right, preferred_element_type=f32)


def dot_last(left, right):
    return lax.dot_general(left, right, (((1,), (1,)), ((), ())), preferred_element_type=f32)


def dot_first(left, right):
    return lax.dot_general(left, right, (((0,), (0,)), ((), ())), preferred_element_type=f32)


def swap(array, axis, ways, bit):
    return lax.ppermute(array, axis, [(i, i ^ bit) for i in range(ways)])


def cost(microseconds):
    return pl.CostEstimate(
        flops=int(microseconds * 1.15e9), bytes_accessed=1 << 20, transcendentals=0
    )


def params():
    return pltpu.CompilerParams(vmem_limit_bytes=VMEM_LIMIT)


def normalise(rows):
    mean = jnp.mean(rows, axis=-1, keepdims=True)
    centered = rows - mean
    variance = jnp.mean(centered * centered, axis=-1, keepdims=True)
    return centered, lax.rsqrt(variance + EPS)


def place_dense(shard, tiles, mixer, merge, normt, sems):
    copies = []
    columns = mixer.shape[1]
    last = tiles[0].shape[1] - LANES
    for k, tile in enumerate(tiles):
        copies.append(
            pltpu.make_async_copy(
                tile.at[0:ROW, last : last + LANES], normt.at[k], sems.at[2 * len(tiles) + k]
            )
        )
    for k, tile in enumerate(tiles):
        rows = tile.shape[0]
        base = pl.multiple_of((shard ^ k) * rows, rows)
        copies.append(
            pltpu.make_async_copy(
                tile.at[:, 0:columns], mixer.at[pl.ds(base, rows)], sems.at[2 * k]
            )
        )
        copies.append(
            pltpu.make_async_copy(
                tile.at[:, columns : columns + merge.shape[1]],
                merge.at[pl.ds(base, rows)],
                sems.at[2 * k + 1],
            )
        )
    return copies


def place_columns(shard, smalls, into, first):
    width = into.shape[1] // len(smalls)
    for k, small in enumerate(smalls):
        if width % LANES == 0:
            base = pl.multiple_of((shard ^ k) * width, width)
            into[:, pl.ds(base, width)] = small[:, first : first + width]
            continue
        for place in range(len(smalls)):

            @pl.when((shard ^ k) == place)
            def _():
                into[:, place * width : (place + 1) * width] = small[:, first : first + width]


def place_norms(shard, normt, norms):
    tiles = [normt[k][0:8].astype(f32) for k in range(normt.shape[0])]
    place_columns(shard, tiles, norms, 0)


def pack_kernel(mixer, merge, router, gain, shift, up, inner, down, outer, dense, near, row, sems):
    columns, width = mixer.shape[1], merge.shape[1]
    own, hidden = gain.shape[1], up.shape[2]
    last = columns + width
    moves = [
        (mixer, dense.at[:, 0:columns]),
        (merge, dense.at[:, columns:last]),
        (down.at[0], near.at[hidden : 2 * hidden]),
    ]
    for fold in range(width // hidden):
        at = slice(fold * hidden, (fold + 1) * hidden)
        moves.append((up.at[0, at], near.at[0:hidden, at]))
    copies = [pltpu.make_async_copy(source, into, sems.at[i]) for i, (source, into) in enumerate(moves)]
    for copy in copies:
        copy.start()
    dense[:, last : last + 2 * LANES] = jnp.zeros((dense.shape[0], 2 * LANES), bf16)
    dense[:, last : last + router.shape[1]] = router[...]
    row[...] = jnp.zeros(row.shape, f32)
    row[0:2, 0:own] = gain[...].astype(f32)
    row[2:4, 0:own] = shift[...].astype(f32)
    dense[0:ROW, last + LANES : last + 2 * LANES] = row[:, 0:LANES].astype(bf16)
    row[...] = jnp.zeros(row.shape, f32)
    row[0:1, 0:hidden] = inner[...].astype(f32)
    row[1:2, 0:own] = outer[...].astype(f32)
    near[2 * hidden : 2 * hidden + ROW] = row[...].astype(bf16)
    for copy in copies:
        copy.wait()


def pack(mixer, merge, router, gain, shift, up, inner, down, outer):
    own, width = merge.shape
    hidden = up.shape[2]
    return pl.pallas_call(
        pack_kernel,
        name="pack",
        out_shape=(
            jax.ShapeDtypeStruct((own, mixer.shape[1] + width + 2 * LANES), bf16),
            jax.ShapeDtypeStruct((2 * hidden + ROW, width), bf16),
        ),
        in_specs=[ANY_SPEC] * 2 + [VMEM_SPEC] * 3 + [ANY_SPEC, VMEM_SPEC, ANY_SPEC, VMEM_SPEC],
        out_specs=(VMEM_SPEC, VMEM_SPEC),
        scratch_shapes=[
            pltpu.VMEM((ROW, width), f32),
            pltpu.SemaphoreType.DMA((3 + width // hidden,)),
        ],
        compiler_params=params(),
        cost_estimate=cost(2),
    )(mixer, merge, router, gain, shift, up, inner, down, outer)


def row_tiles(rows):
    return [slice(first, min(first + TILE, rows)) for first in range(0, rows, TILE)]


def image_window(base, image):
    first = base + image * SEQ
    start = pl.multiple_of(first // ROW * ROW, ROW)
    offset = first - start
    rows = lax.broadcasted_iota(jnp.int32, (WIN, 1), 0)
    columns = lax.broadcasted_iota(jnp.int32, (1, WIN), 1)
    row_in = (rows >= offset) & (rows < offset + SEQ)
    column_in = (columns >= offset) & (columns < offset + SEQ)
    return start, row_in, column_in


def attention_forward_kernel(n_tiles, base, images, *refs):
    shard_ref, tok = refs[0], refs[1]
    dense = refs[2 : 2 + n_tiles]
    qkv, att, weights, res, normed_two, mixer, merge, normt, norms, sems = refs[2 + n_tiles :]
    shard = shard_ref[0]
    width = tok.shape[1]
    copies = place_dense(shard, dense, mixer, merge, normt, sems)
    for copy in copies:
        copy.start()
    for copy in copies:
        copy.wait()
    place_norms(shard, normt, norms)
    for rows in row_tiles(tok.shape[0]):
        centered, rate = normalise(tok[rows].astype(f32))
        normed = (centered * rate * norms[0:1] + norms[2:3]).astype(bf16)
        qkv[rows] = dot(normed, mixer[...]).astype(bf16)
    att[...] = jnp.zeros(att.shape, bf16)
    lane = lax.broadcasted_iota(jnp.int32, (1, LANES), 1)

    def image_step(image, carry):
        start, row_in, column_in = image_window(base, image)
        window = pl.ds(start, WIN)
        for slab in range(width // LANES):
            q = qkv[window, slab * LANES : (slab + 1) * LANES]
            k = qkv[window, width + slab * LANES : width + (slab + 1) * LANES]
            v = qkv[window, 2 * width + slab * LANES : 2 * width + (slab + 1) * LANES]
            outs = []
            for half in range(2):
                mine = (lane >= half * HEAD_DIM) & (lane < (half + 1) * HEAD_DIM)
                scores = dot_last(jnp.where(mine, q, jnp.zeros_like(q)), k) * SCALING
                scores = jnp.where(column_in, scores, NEG)
                top = jnp.max(scores, axis=-1, keepdims=True)
                powers = jnp.exp(scores - top)
                total = jnp.sum(powers, axis=-1, keepdims=True)
                low = (powers * jnp.where(row_in, 1.0 / total, 0.0)).astype(bf16)
                weights[image, 2 * slab + half] = low
                outs.append(dot(low, v))
            out = jnp.where(lane < HEAD_DIM, outs[0], outs[1]).astype(bf16)
            columns = slice(slab * LANES, (slab + 1) * LANES)
            att[window, columns] = att[window, columns] + out
        return carry

    lax.fori_loop(0, images, image_step, 0)
    for rows in row_tiles(tok.shape[0]):
        residual = tok[rows].astype(f32) + dot(att[rows], merge[...])
        res[rows] = residual
        centered, rate = normalise(residual)
        normed_two[rows] = (centered * rate * norms[1:2] + norms[3:4]).astype(bf16)


def attention_forward(shard, tok, dense, base, images):
    rows, width = tok.shape
    n = len(dense)
    return pl.pallas_call(
        functools.partial(attention_forward_kernel, n, base, images),
        name="attention_forward",
        out_shape=(
            jax.ShapeDtypeStruct((rows, 3 * width), bf16),
            jax.ShapeDtypeStruct((rows, width), bf16),
            jax.ShapeDtypeStruct((images, HEADS, WIN, WIN), bf16),
            jax.ShapeDtypeStruct((rows, width), f32),
            jax.ShapeDtypeStruct((rows, width), bf16),
        ),
        in_specs=[SMEM_SPEC, VMEM_SPEC] + [ANY_SPEC] * n,
        out_specs=(VMEM_SPEC,) * 5,
        scratch_shapes=[
            pltpu.VMEM((width, 3 * width), bf16),
            pltpu.VMEM((width, width), bf16),
            pltpu.VMEM((n, ROW, LANES), bf16),
            pltpu.VMEM((8, width), f32),
            pltpu.SemaphoreType.DMA((3 * n,)),
        ],
        compiler_params=params(),
        cost_estimate=cost(7),
    )(shard, tok, *dense)


def weight_copies(shard, dense, tiles, router, up, down, bias, sems, router_lane):
    n = len(dense)
    width, hidden = up.shape[2], up.shape[3]
    folds = width // hidden
    routers, weights = [], [[] for _ in range(len(tiles) // n)]
    for k, tile in enumerate(dense):
        rows = tile.shape[0]
        base = pl.multiple_of((shard ^ k) * rows, rows)
        routers.append(
            pltpu.make_async_copy(
                tile.at[:, router_lane : router_lane + LANES], router.at[pl.ds(base, rows)], sems.at[0, 0, k]
            )
        )
    for j in range(len(weights)):
        for k in range(n):
            tile = tiles[j * n + k]
            for fold in range(folds):
                at = slice(fold * hidden, (fold + 1) * hidden)
                weights[j].append(
                    pltpu.make_async_copy(
                        tile.at[0:hidden, at], up.at[j, k, at], sems.at[1 + j, fold, k]
                    )
                )
            weights[j].append(
                pltpu.make_async_copy(
                    tile.at[hidden : 2 * hidden], down.at[j, k], sems.at[1 + j, folds, k]
                )
            )
            weights[j].append(
                pltpu.make_async_copy(
                    tile.at[2 * hidden : 2 * hidden + ROW], bias.at[j, k], sems.at[1 + j, folds + 1, k]
                )
            )
    return routers, weights


def block_starts(group, counts, js):
    starts = []
    for j in js:
        at, firsts = jnp.int32(0), []
        for b in range(group):
            firsts.append(pl.multiple_of(at, ROW))
            at = at + (counts[2 * b + j] + ROW - 1) // ROW * ROW
        starts.append((firsts, pl.multiple_of(at, ROW)))
    return starts


def gather_rows(js, group, counts, pos, blocks, into, starts):
    width = into.shape[2]
    row = lax.broadcasted_iota(jnp.int32, (GATHER, 1), 0)
    for b in range(group):
        hot = [
            jnp.where(pos[2 * b + j : 2 * b + j + 1, :] == row, 1.0, 0.0).astype(bf16) for j in js
        ]
        rows = dot(jnp.concatenate(hot, axis=0), blocks[b]).astype(bf16)
        for i, j in enumerate(js):
            base = starts[i][0][b]
            into[i, pl.ds(base, GATHER), :] = rows[i * GATHER : (i + 1) * GATHER]

            def more(step, carry, i=i, j=j, base=base):
                some = jnp.where(pos[2 * b + j : 2 * b + j + 1, :] == row + step * GATHER, 1.0, 0.0)
                at = pl.multiple_of(base + step * GATHER, ROW)
                into[i, pl.ds(at, GATHER), :] = dot(some.astype(bf16), blocks[b]).astype(bf16)
                return carry

            lax.fori_loop(1, (counts[2 * b + j] + GATHER - 1) // GATHER, more, 0)
    for i in range(len(js)):
        into[i, pl.ds(starts[i][1], MLP), :] = jnp.zeros((MLP, width), bf16)


def scatter_rows(js, group, counts, places, source, outs, staged, sems, starts, total, before=()):
    column = lax.broadcasted_iota(jnp.int32, (1, SCATTER), 1)

    def leave(b):
        return pltpu.make_async_copy(staged.at[b % 2], outs[b], sems.at[b % 2])

    for b in range(group):
        mine = [places[:, 2 * b + j : 2 * b + j + 1] for j in js]
        hot = jnp.concatenate(
            [jnp.where(place == column, 1.0, 0.0).astype(bf16) for place in mine], axis=1
        )
        rows = jnp.concatenate(
            [source[i, pl.ds(starts[i][0][b], SCATTER), :] for i in range(len(js))], axis=0
        )
        if b >= 2:
            leave(b - 2).wait()
        value = dot(hot, rows)
        if before:
            value = value + before[b][...].astype(f32)
        staged[b % 2] = value.astype(bf16)
        most = counts[2 * b + js[0]]
        for j in js[1:]:
            most = jnp.maximum(most, counts[2 * b + j])

        @pl.when(most > SCATTER)
        def _():
            total[...] = value
            for i, j in enumerate(js):

                def more(step, carry, i=i):
                    some = jnp.where(mine[i] == column + step * SCATTER, 1.0, 0.0).astype(bf16)
                    at = pl.multiple_of(starts[i][0][b] + step * SCATTER, ROW)
                    total[...] += dot(some, source[i, pl.ds(at, SCATTER), :])
                    return carry

                lax.fori_loop(1, (counts[2 * b + j] + SCATTER - 1) // SCATTER, more, 0)
            staged[b % 2] = total[...].astype(bf16)

        leave(b).start()
    for b in range(max(0, group - 2), group):
        leave(b).wait()


def block_copies(refs, blocks, sems):
    return [pltpu.make_async_copy(ref, blocks.at[b], sems.at[b]) for b, ref in enumerate(refs)]


def tile_at(i):
    return pl.ds(pl.multiple_of(i * MLP, MLP), MLP)


def drain(copies, tiles):
    for back in (2, 1):

        @pl.when(tiles >= back)
        def _():
            for copy in copies(tiles - back):
                copy.wait()


def expert_forward_kernel(n, group, experts, router_lane, j, *refs):
    shard_ref, e_ref, counts, pos, places = refs[:5]
    refs = refs[5:]
    sources, dense, tiles_in, refs = refs[:group], refs[group : group + n], refs[group + n : group + 2 * n], refs[group + 2 * n :]
    before, refs = refs[: group * j], refs[group * j :]
    outs, refs = refs[:group], refs[group:]
    x_out, y_out, probs_out, act_out, slope_out = refs[:5]
    blocks, up, down, bias, router, outer, x_rows, scaled, total, staged, act, slope, y, probs = refs[5:19]
    sems, block_sems, leave_sems, out_sems, x_sems = refs[19:]
    shard = shard_ref[0]
    hidden_width = up.shape[3]
    width = up.shape[2]
    arrivals = block_copies(sources, blocks, block_sems)
    routers, weights = weight_copies(shard, dense, tiles_in, router, up, down, bias, sems, router_lane)
    for copy in arrivals:
        copy.start()
    for copy in arrivals:
        copy.wait()
    for copy in routers + weights[0]:
        copy.start()
    starts = block_starts(group, counts, (j,))
    gather_rows((j,), group, counts, pos, blocks, x_rows, starts)
    for copy in routers:
        copy.wait()
    lane = lax.broadcasted_iota(jnp.int32, (1, LANES), 1)
    tiles = (starts[0][1] + MLP - 1) // MLP

    def saves(i):
        slot = lax.rem(i, 2)
        return [
            pltpu.make_async_copy(source.at[slot], into.at[0, tile_at(i)], out_sems.at[m, slot])
            for m, (source, into) in enumerate(
                ((act, act_out), (slope, slope_out), (y, y_out), (probs, probs_out))
            )
        ]

    def save_x(i):
        return pltpu.make_async_copy(x_rows.at[0, tile_at(i)], x_out.at[0, tile_at(i)], x_sems.at[0, i])

    for copy in weights[0]:
        copy.wait()
    place_columns(shard, [bias[0, k][0:8].astype(f32) for k in range(n)], outer.at[0], 0)

    def tile_step(i, carry):
        slot = lax.rem(i, 2)

        @pl.when(i >= 2)
        def _():
            for copy in saves(i - 2):
                copy.wait()

        save_x(i).start()
        x = x_rows[0, tile_at(i), :]
        logits = jnp.where(lane < experts, dot(x, router[...]), NEG)
        powers = jnp.exp(logits - jnp.max(logits, axis=-1, keepdims=True))
        shares = powers * (1.0 / jnp.sum(powers, axis=-1, keepdims=True))
        probs[slot] = shares
        gate = jnp.sum(jnp.where(lane == e_ref[j], shares, 0.0), axis=-1, keepdims=True)
        for k in range(n):
            hidden = dot(x, up[0, k]) + bias[0, k, 0:1, 0:hidden_width].astype(f32)
            square = hidden * hidden
            share = 0.5 * jnp.tanh(hidden * (GELU_C + GELU_C * GELU_K * square)) + 0.5
            active = hidden * share
            columns = slice(k * hidden_width, (k + 1) * hidden_width)
            act[slot, :, columns] = active.astype(bf16)
            slope[slot, :, columns] = (
                share
                + (active - active * share) * (2.0 * GELU_C + 6.0 * GELU_C * GELU_K * square)
            ).astype(bf16)
        acc = jnp.broadcast_to(outer[0, 1:2], (MLP, width))
        for k in range(n):
            acc = acc + dot(act[slot, :, k * hidden_width : (k + 1) * hidden_width], down[0, k])
        low = acc.astype(bf16)
        y[slot] = low
        for copy in saves(i):
            copy.start()
        scaled[0, tile_at(i), :] = (gate * low.astype(f32)).astype(bf16)
        return carry

    lax.fori_loop(0, tiles, tile_step, 0)
    drain(saves, tiles)

    def wait_x(i, carry):
        save_x(i).wait()
        return carry

    lax.fori_loop(0, tiles, wait_x, 0)
    scaled[0, tile_at(tiles), :] = jnp.zeros((MLP, width), bf16)
    scatter_rows((j,), group, counts, places, scaled, outs, staged, leave_sems, starts, total, before)


def expert_rows(group, capacity):
    return up_to(group * up_to(capacity, ROW), MLP) + MLP


def expert_forward(j, scalars, pos, places, sources, dense, tiles, group, experts, capacity, router_lane, before=()):
    n = len(dense)
    width = sources[0].shape[1]
    tokens = pos.shape[1]
    hidden = (tiles[0].shape[0] - ROW) // 2
    rows = expert_rows(group, capacity)
    return pl.pallas_call(
        functools.partial(expert_forward_kernel, n, group, experts, router_lane, j),
        name="expert_forward",
        out_shape=[jax.ShapeDtypeStruct((tokens, width), bf16)] * group
        + [jax.ShapeDtypeStruct((1, rows, width), bf16)] * 2
        + [jax.ShapeDtypeStruct((1, rows, LANES), f32)]
        + [jax.ShapeDtypeStruct((1, rows, hidden * n), bf16)] * 2,
        in_specs=[SMEM_SPEC] * 3
        + [VMEM_SPEC] * 2
        + [ANY_SPEC] * (group + 2 * n)
        + [VMEM_SPEC] * len(before),
        out_specs=[ANY_SPEC] * (group + 5),
        scratch_shapes=[
            pltpu.VMEM((group, tokens, width), bf16),
            pltpu.VMEM((1, n, width, hidden), bf16),
            pltpu.VMEM((1, n, hidden, width), bf16),
            pltpu.VMEM((1, n, ROW, width), bf16),
            pltpu.VMEM((width, LANES), bf16),
            pltpu.VMEM((1, 8, width), f32),
            pltpu.VMEM((1, rows, width), bf16),
            pltpu.VMEM((1, rows, width), bf16),
            pltpu.VMEM((tokens, width), f32),
            pltpu.VMEM((2, tokens, width), bf16),
            pltpu.VMEM((2, MLP, hidden * n), bf16),
            pltpu.VMEM((2, MLP, hidden * n), bf16),
            pltpu.VMEM((2, MLP, width), bf16),
            pltpu.VMEM((2, MLP, LANES), f32),
            pltpu.SemaphoreType.DMA((2, width // hidden + 2, n)),
            pltpu.SemaphoreType.DMA((group,)),
            pltpu.SemaphoreType.DMA((2,)),
            pltpu.SemaphoreType.DMA((4, 2)),
            pltpu.SemaphoreType.DMA((1, rows // MLP)),
        ],
        compiler_params=params(),
        cost_estimate=cost(FORWARD_US),
    )(*scalars, pos, places, *sources, *dense, *tiles, *before)


def expert_backward_kernel(n, group, router_lane, *refs):
    shard_ref, e_ref, counts, pos, places = refs[:5]
    refs = refs[5:]
    sources, dense, tiles_in, refs = refs[:group], refs[group : group + n], refs[group + n : group + 3 * n], refs[group + 3 * n :]
    saved_in, refs = (refs[0:4], refs[4:8]), refs[8:]
    outs, refs = refs[:group], refs[group:]
    pg_out, hg_out, router_grad, inner_grad, outer_grad = refs[:5]
    blocks, up, down, bias, router, f_rows, b_rows, total, staged, hg, pg, slope, x, y, probs = refs[5:20]
    sems, block_sems, leave_sems, out_sems, in_sems = refs[20:]
    shard = shard_ref[0]
    hidden_width = up.shape[3]
    width = up.shape[2]
    arrivals = block_copies(sources, blocks, block_sems)
    routers, weights = weight_copies(shard, dense, tiles_in, router, up, down, bias, sems, router_lane)
    for copy in arrivals:
        copy.start()
    router_grad[...] = jnp.zeros(router_grad.shape, f32)
    inner_grad[...] = jnp.zeros(inner_grad.shape, f32)
    outer_grad[...] = jnp.zeros(outer_grad.shape, f32)
    for copy in arrivals:
        copy.wait()
    for copy in routers + weights[0]:
        copy.start()
    starts = block_starts(group, counts, (0, 1))
    gather_rows((0, 1), group, counts, pos, blocks, f_rows, starts)
    for copy in routers:
        copy.wait()
    lane = lax.broadcasted_iota(jnp.int32, (1, LANES), 1)
    for j in range(2):
        tiles = (starts[j][1] + MLP - 1) // MLP

        def saves(i, j=j):
            slot = lax.rem(i, 2)
            return (
                pltpu.make_async_copy(hg.at[slot], hg_out.at[j, tile_at(i)], out_sems.at[0, slot]),
                pltpu.make_async_copy(pg.at[slot], pg_out.at[j, tile_at(i)], out_sems.at[1, slot]),
            )

        def loads(i, j=j):
            slot = lax.rem(i, 2)
            return [
                pltpu.make_async_copy(source.at[0, tile_at(i)], into.at[slot], in_sems.at[m, slot])
                for m, (source, into) in enumerate(zip(saved_in[j], (x, y, probs, slope)))
            ]

        @pl.when(tiles >= 1)
        def _():
            for copy in loads(0):
                copy.start()

        for copy in weights[j]:
            copy.wait()
        if j == 0:
            for copy in weights[1]:
                copy.start()

        def tile_step(i, carry):
            slot = lax.rem(i, 2)

            @pl.when(i + 1 < tiles)
            def _():
                for copy in loads(i + 1):
                    copy.start()

            @pl.when(i >= 2)
            def _():
                for copy in saves(i - 2):
                    copy.wait()

            for copy in loads(i):
                copy.wait()
            f = f_rows[j, tile_at(i), :].astype(f32)
            shares = probs[slot]
            mine = lane == e_ref[j]
            gate = jnp.sum(jnp.where(mine, shares, 0.0), axis=-1, keepdims=True)
            wide = gate * f
            pg[slot] = wide.astype(bf16)
            gate_grad = jnp.sum(f * y[slot].astype(f32), axis=-1, keepdims=True)
            logit = gate_grad * gate * (jnp.where(mine, 1.0, 0.0) - shares)
            high = logit.astype(bf16)
            rest = (logit - high.astype(f32)).astype(bf16)
            outer_grad[j : j + 1] += jnp.sum(wide, axis=0, keepdims=True)
            for k in range(n):
                columns = slice(k * hidden_width, (k + 1) * hidden_width)
                grad = dot_last(pg[slot], down[j, k]) * slope[slot, :, columns].astype(f32)
                hg[slot, :, columns] = grad.astype(bf16)
                inner_grad[j : j + 1, columns] += jnp.sum(grad, axis=0, keepdims=True)
            for copy in saves(i):
                copy.start()
            turned = x[slot].T
            router_grad[...] += dot(turned, high) + dot(turned, rest)
            acc = dot_last(high, router[...]) + dot_last(rest, router[...])
            for k in range(n):
                acc = acc + dot_last(hg[slot, :, k * hidden_width : (k + 1) * hidden_width], up[j, k])
            b_rows[j, tile_at(i), :] = acc.astype(bf16)
            return carry

        lax.fori_loop(0, tiles, tile_step, 0)
        drain(saves, tiles)
        b_rows[j, tile_at(tiles), :] = jnp.zeros((MLP, width), bf16)
    scatter_rows((0, 1), group, counts, places, b_rows, outs, staged, leave_sems, starts, total)


def expert_backward(scalars, pos, places, sources, dense, tiles, saved, group, capacity, router_lane):
    n = len(dense)
    width = sources[0].shape[1]
    tokens = pos.shape[1]
    hidden = (tiles[0].shape[0] - ROW) // 2
    rows = expert_rows(group, capacity)
    return pl.pallas_call(
        functools.partial(expert_backward_kernel, n, group, router_lane),
        name="expert_backward",
        out_shape=[jax.ShapeDtypeStruct((tokens, width), bf16)] * group
        + [
            jax.ShapeDtypeStruct((2, rows, width), bf16),
            jax.ShapeDtypeStruct((2, rows, hidden * n), bf16),
            jax.ShapeDtypeStruct((width, LANES), f32),
            jax.ShapeDtypeStruct((8, hidden * n), f32),
            jax.ShapeDtypeStruct((8, width), f32),
        ],
        in_specs=[SMEM_SPEC] * 3 + [VMEM_SPEC] * 2 + [ANY_SPEC] * (group + 3 * n + 8),
        out_specs=[ANY_SPEC] * (group + 2) + [VMEM_SPEC] * 3,
        scratch_shapes=[
            pltpu.VMEM((group, tokens, width), bf16),
            pltpu.VMEM((2, n, width, hidden), bf16),
            pltpu.VMEM((2, n, hidden, width), bf16),
            pltpu.VMEM((2, n, ROW, width), bf16),
            pltpu.VMEM((width, LANES), bf16),
            pltpu.VMEM((2, rows, width), bf16),
            pltpu.VMEM((2, rows, width), bf16),
            pltpu.VMEM((tokens, width), f32),
            pltpu.VMEM((2, tokens, width), bf16),
            pltpu.VMEM((2, MLP, hidden * n), bf16),
            pltpu.VMEM((2, MLP, width), bf16),
            pltpu.VMEM((2, MLP, hidden * n), bf16),
            pltpu.VMEM((2, MLP, width), bf16),
            pltpu.VMEM((2, MLP, width), bf16),
            pltpu.VMEM((2, MLP, LANES), f32),
            pltpu.SemaphoreType.DMA((3, width // hidden + 2, n)),
            pltpu.SemaphoreType.DMA((group,)),
            pltpu.SemaphoreType.DMA((2,)),
            pltpu.SemaphoreType.DMA((2, 2)),
            pltpu.SemaphoreType.DMA((4, 2)),
        ],
        compiler_params=params(),
        cost_estimate=cost(BACKWARD_US),
    )(*scalars, pos, places, *sources, *dense, *tiles, *saved)


def put_columns(shard, k, n, source, row, into):
    width = source.shape[1] // n
    if width % LANES == 0:
        base = pl.multiple_of((shard ^ k) * width, width)
        into[:, 0:width] = source[row : row + 1, pl.ds(base, width)].astype(into.dtype)
        return
    for place in range(n):

        @pl.when((shard ^ k) == place)
        def _():
            into[:, 0:width] = source[row : row + 1, place * width : (place + 1) * width].astype(into.dtype)


def weight_grads_kernel(n, experts, added, shard_ref, tiles_ref, *refs):
    saved, refs = refs[: 2 * len(experts) + 2], refs[2 * len(experts) + 2 :]
    inner_part, outer_part, refs = refs[0], refs[1], refs[2:]
    before, refs = refs[:added], refs[added:]
    results, refs = refs[: 2 * len(experts)], refs[2 * len(experts) :]
    x, pg, act, hg, up_total, down_total, row, sems = refs
    width, hidden = up_total.shape[1:]
    folds = width // hidden
    shard = shard_ref[0]
    for turn, j in enumerate(experts):
        tiles = tiles_ref[j]
        for k in range(n):
            up_total[k] = jnp.zeros((width, hidden), f32)
            down_total[k] = jnp.zeros((width, hidden), f32)

        def loads(i, j=j, turn=turn):
            slot = lax.rem(i, 2)
            sources = (
                saved[2 * turn].at[0, tile_at(i)],
                saved[-2].at[j, tile_at(i)],
                saved[2 * turn + 1].at[0, tile_at(i)],
                saved[-1].at[j, tile_at(i)],
            )
            return [
                pltpu.make_async_copy(source, into.at[slot], sems.at[m, slot])
                for m, (source, into) in enumerate(zip(sources, (x, pg, act, hg)))
            ]

        @pl.when(tiles >= 1)
        def _():
            for copy in loads(0):
                copy.start()

        def tile_step(i, carry):
            slot = lax.rem(i, 2)

            @pl.when(i + 1 < tiles)
            def _():
                for copy in loads(i + 1):
                    copy.start()

            for copy in loads(i):
                copy.wait()
            turned = x[slot].T
            turned_grad = pg[slot].T
            for k in range(n):
                columns = slice(k * hidden, (k + 1) * hidden)
                up_total[k] += dot(turned, hg[slot, :, columns])
                down_total[k] += dot(turned_grad, act[slot, :, columns])
            return carry

        lax.fori_loop(0, tiles, tile_step, 0)
        row[8:16] = outer_part[...]
        for k in range(n):
            into = results[2 * turn + 1 - k % 2].at[k // 2]
            base = before[2 * turn + 1 - k % 2].at[k // 2] if added else None

            def put(rows, columns, value):
                if added:
                    value = value + base[rows, columns].astype(f32)
                into[rows, columns] = value.astype(bf16)

            for fold in range(folds):
                at = slice(fold * hidden, (fold + 1) * hidden)
                put(slice(0, hidden), at, up_total[k, at])
            put(slice(hidden, 2 * hidden), slice(0, width), down_total[k].T)
            row[0:8] = jnp.zeros((8, width), f32)
            row[0:1, 0:hidden] = inner_part[j : j + 1, k * hidden : (k + 1) * hidden]
            put_columns(shard, k, n, row, 8 + j, row.at[1:2])
            row[8:16] = outer_part[...]
            put(slice(2 * hidden, 2 * hidden + 8), slice(0, width), row[0:8])
            into[2 * hidden + 8 : 2 * hidden + ROW] = jnp.zeros((ROW - 8, width), bf16)


def weight_grads(experts, shard, tiles, saved, biases, n, before=()):
    rows_in, grads = saved
    _, rows, width = grads[0].shape
    hidden = grads[1].shape[2] // n
    held = [array for j in experts for array in rows_in[j]] + list(grads)
    shape = jax.ShapeDtypeStruct((n // 2, 2 * hidden + ROW, width), bf16)
    return pl.pallas_call(
        functools.partial(weight_grads_kernel, n, experts, len(before)),
        name="weight_grads",
        out_shape=(shape,) * (2 * len(experts)),
        in_specs=[SMEM_SPEC] * 2 + [ANY_SPEC] * len(held) + [VMEM_SPEC] * (2 + len(before)),
        out_specs=(VMEM_SPEC,) * (2 * len(experts)),
        scratch_shapes=[
            pltpu.VMEM((2, MLP, width), bf16),
            pltpu.VMEM((2, MLP, width), bf16),
            pltpu.VMEM((2, MLP, hidden * n), bf16),
            pltpu.VMEM((2, MLP, hidden * n), bf16),
            pltpu.VMEM((n, width, hidden), f32),
            pltpu.VMEM((n, width, hidden), f32),
            pltpu.VMEM((ROW, width), f32),
            pltpu.SemaphoreType.DMA((4, 2)),
        ],
        compiler_params=params(),
        cost_estimate=cost(8 * len(experts)),
    )(shard, tiles, *held, *biases, *before)


def norm_backward(rows, gain, grad):
    centered, rate = normalise(rows)
    unit = centered * rate
    scaled = grad * gain
    back = rate * (
        scaled
        - jnp.mean(scaled, axis=-1, keepdims=True)
        - unit * jnp.mean(scaled * unit, axis=-1, keepdims=True)
    )
    return (
        back,
        jnp.sum(grad * unit, axis=0, keepdims=True),
        jnp.sum(grad, axis=0, keepdims=True),
        unit,
    )


def attention_backward_kernel(n_tiles, parts, base, images, overlap, last, *refs):
    shard_ref, refs = refs[0], refs[1:]
    grads, refs = refs[:parts], refs[parts:]
    fg, res, att, qkv, weights, tok = refs[:6]
    dense, refs = refs[6 : 6 + n_tiles], refs[6 + n_tiles :]
    before = None
    if overlap:
        before, refs = refs[:6], refs[6:]
    if last:
        router_parts, refs = refs[:last], refs[last:]
        token_grad, norm_grad, send, keep = refs[:4]
        mixer, merge, normt, norms, dres, datt, sems, low, normed, mg, mixer_grad, merge_grad = refs[4:]
    else:
        token_grad, norm_grad, normed, mg, low = refs[:5]
        mixer, merge, normt, norms, dres, datt, sems = refs[5:]
    shard = shard_ref[0]
    width = tok.shape[1]
    n_rows = tok.shape[0]
    copies = place_dense(shard, dense, mixer, merge, normt, sems)
    for copy in copies:
        copy.start()
    for copy in copies:
        copy.wait()
    place_norms(shard, normt, norms)
    norm_grad[...] = before[1][...] if overlap else jnp.zeros(norm_grad.shape, f32)
    for rows in row_tiles(n_rows):
        grad = grads[0][rows].astype(f32)
        for other in grads[1:]:
            grad = grad + other[rows].astype(f32)
        back, gain, shift, _ = norm_backward(res[rows], norms[1:2], grad)
        norm_grad[1:2] += gain
        norm_grad[3:4] += shift
        total = fg[rows] + back
        dres[rows] = total
        low[rows] = total.astype(bf16)
        datt[rows] = dot_last(low[rows], merge[...]).astype(bf16)
    mg[...] = jnp.zeros(mg.shape, bf16)
    if last:
        merge_term = dot_first(att[...], low[...])
        merge_grad[...] = merge_term + dot_first(before[5][...], before[4][...]) if overlap else merge_term
    lane = lax.broadcasted_iota(jnp.int32, (1, LANES), 1)

    def image_step(image, carry):
        start, _, _ = image_window(base, image)
        window = pl.ds(start, WIN)
        for slab in range(width // LANES):
            q_at = slice(slab * LANES, (slab + 1) * LANES)
            k_at = slice(width + slab * LANES, width + (slab + 1) * LANES)
            v_at = slice(2 * width + slab * LANES, 2 * width + (slab + 1) * LANES)
            q, k, v = qkv[window, q_at], qkv[window, k_at], qkv[window, v_at]
            do = datt[window, q_at]
            parts = []
            for half in range(2):
                head = 2 * slab + half
                mine = (lane >= half * HEAD_DIM) & (lane < (half + 1) * HEAD_DIM)
                zero = jnp.zeros_like(q)
                low = weights[image, head]
                dv = dot_first(low, do)
                dw = dot_last(jnp.where(mine, do, zero), v)
                wide = low.astype(f32)
                inner = jnp.sum(wide * dw, axis=-1, keepdims=True)
                ds = (wide * (dw - inner)).astype(bf16)
                parts.append((dot(ds, k) * SCALING, dot_first(ds, q) * SCALING, dv))
            for at, first, second in zip((q_at, k_at, v_at), parts[0], parts[1]):
                both = jnp.where(lane < HEAD_DIM, first, second).astype(bf16)
                mg[window, at] = mg[window, at] + both
        return carry

    lax.fori_loop(0, images, image_step, 0)
    shift_rows = token_grad.shape[0] - n_rows if overlap else 0
    if overlap:
        token_grad[0:shift_rows] = before[0][0:shift_rows]
    for rows in row_tiles(n_rows):
        grad = dot_last(mg[rows], mixer[...])
        back, gain, shift, unit = norm_backward(tok[rows].astype(f32), norms[0:1], grad)
        norm_grad[0:1] += gain
        norm_grad[2:3] += shift
        total = dres[rows] + back
        if overlap and rows.start < overlap:
            both = before[0][shift_rows : shift_rows + overlap]
            token_grad[shift_rows : shift_rows + overlap] = total[0:overlap] + both
            token_grad[shift_rows + overlap : shift_rows + rows.stop] = total[overlap:]
        else:
            token_grad[shift_rows + rows.start : shift_rows + rows.stop] = total
        normed[rows] = (unit * norms[0:1] + norms[2:3]).astype(bf16)
    if last:
        for c in range(3):
            columns = slice(c * width, (c + 1) * width)
            term = dot_first(normed[...], mg[:, columns])
            if overlap:
                term = term + dot_first(before[2][...], before[3][:, columns])
            mixer_grad[:, columns] = term
        for k in range(n_tiles):
            own = width // n_tiles
            at = pl.ds(pl.multiple_of((shard ^ k) * own, own), own)
            into = (send if k % 2 else keep).at[k // 2]
            into[:, 0 : 3 * width] = mixer_grad[at].astype(bf16)
            into[:, 3 * width : 4 * width] = merge_grad[at].astype(bf16)
            into[:, 4 * width : 4 * width + LANES] = sum(part[at] for part in router_parts).astype(bf16)


def attention_backward(shard, grads, fg, res, att, qkv, weights, tok, dense, base, images, before, start, router_parts):
    rows, width = tok.shape
    n = len(dense)
    overlap = before[0].shape[0] - start if before else 0
    token_shape = jax.ShapeDtypeStruct((start + rows if before else rows, width), f32)
    norm_shape = jax.ShapeDtypeStruct((8, width), f32)
    totals = [
        pltpu.VMEM((rows, width), bf16),
        pltpu.VMEM((rows, width), bf16),
        pltpu.VMEM((rows, 3 * width), bf16),
        pltpu.VMEM((width, 3 * width), f32),
        pltpu.VMEM((width, width), f32),
    ]
    if router_parts:
        tile = jax.ShapeDtypeStruct((n // 2, width // n, 4 * width + LANES), bf16)
        shapes = (token_shape, norm_shape, tile, tile)
    else:
        shapes = (
            token_shape,
            norm_shape,
            jax.ShapeDtypeStruct((rows, width), bf16),
            jax.ShapeDtypeStruct((rows, 3 * width), bf16),
            jax.ShapeDtypeStruct((rows, width), bf16),
        )
    held = (*grads, fg, res, att, qkv, weights, tok)
    more = (*(before or ()), *router_parts)
    return pl.pallas_call(
        functools.partial(
            attention_backward_kernel, n, len(grads), base, images, overlap, len(router_parts)
        ),
        name="attention_backward",
        out_shape=shapes,
        in_specs=[SMEM_SPEC] + [VMEM_SPEC] * len(held) + [ANY_SPEC] * n + [VMEM_SPEC] * len(more),
        out_specs=(VMEM_SPEC,) * len(shapes),
        scratch_shapes=[
            pltpu.VMEM((width, 3 * width), bf16),
            pltpu.VMEM((width, width), bf16),
            pltpu.VMEM((n, ROW, LANES), bf16),
            pltpu.VMEM((8, width), f32),
            pltpu.VMEM((rows, width), f32),
            pltpu.VMEM((rows, width), bf16),
            pltpu.SemaphoreType.DMA((3 * n,)),
        ]
        + (totals if router_parts else []),
        compiler_params=params(),
        cost_estimate=cost(40),
    )(shard, *held, *dense, *more)


def bits_of(ways):
    bit = ways // 2
    while bit:
        yield bit
        bit //= 2


def gather_tiles(array, axis, ways, gate=None):
    tiles = {0: array}
    for step, bit in enumerate(bits_of(ways)):
        for k in list(tiles):
            sent = after(tiles[k], *gate) if gate is not None and step else tiles[k]
            tiles[k | bit] = swap(sent, axis, ways, bit)
    return [tiles[k] for k in range(ways)]


def fold_tiles(send, keep, axis, ways):
    sums = (keep.astype(f32) + swap(send, axis, ways, 1).astype(f32)).astype(bf16)

    def rest():
        tiles = sums
        for bit in [bit for bit in reversed(list(bits_of(ways))) if bit > 1]:
            tiles = (tiles[0::2].astype(f32) + swap(tiles[1::2], axis, ways, bit).astype(f32)).astype(bf16)
        return tiles

    return sums, rest


def sum_over(array, axis, ways):
    for bit in bits_of(ways):
        array = array + swap(array, axis, ways, bit)
    return array


def sum_split(array, axis, ways, index, gate, last_gate):
    half = array.shape[0] // 2
    mine = index & 1
    kept = lax.dynamic_slice_in_dim(array, mine * half, half, 0)
    sent = lax.dynamic_slice_in_dim(array, (1 - mine) * half, half, 0)
    part = after(kept.astype(f32) + swap(sent, axis, ways, 1).astype(f32), gate)
    for bit in [bit for bit in reversed(list(bits_of(ways))) if bit > 1]:
        low = part.astype(bf16)
        part = low.astype(f32) + swap(low, axis, ways, bit).astype(f32)
    low = after(part.astype(bf16), last_gate)
    other = swap(low, axis, ways, 1)
    first = jnp.where(mine == 0, low, other)
    second = jnp.where(mine == 0, other, low)
    return jnp.concatenate([first, second], axis=0).astype(f32)


def exchange(array, ways, group):
    return [array] + [swap(array, "expert", ways, b) for b in range(1, group)]


def give_back(blocks, ways, group):
    return [blocks[0]] + [swap(blocks[b], "expert", ways, b) for b in range(1, group)]


def after(value, *others):
    return lax.optimization_barrier((value, *others))[0]


def per_device(
    tokens,
    teacher,
    valid_mask,
    routes,
    mixer_weight,
    merge_weight,
    router_weight,
    norm_gain,
    norm_shift,
    up_weight,
    inner_bias,
    down_weight,
    outer_bias,
):
    ways = lax.axis_size("expert")
    shards = lax.axis_size("shard")
    shard = lax.axis_index("shard").astype(jnp.int32)
    expert = lax.axis_index("expert").astype(jnp.int32)
    token_count, width = tokens.shape
    images = token_count // SEQ
    experts = router_weight.shape[1]
    group = ways // 2
    chunks = 2 if images % 2 == 0 else 1
    chunk_images = images // chunks
    chunk_tokens = chunk_images * SEQ
    capacity = min(chunk_tokens, max(2, 4 * token_count // experts))
    firsts = [c * chunk_tokens for c in range(chunks)]
    starts = [first // 8 * 8 for first in firsts]
    last = max(first - start + (chunk_images - 1) * SEQ for first, start in zip(firsts, starts))
    rows = up_to(last // ROW * ROW + WIN, ROW)
    all_rows = starts[-1] + rows
    shard_rows = width // shards
    hidden = up_weight.shape[2]
    router_lane = 4 * width
    folds = width // hidden

    dense_own, near = pack(
        mixer_weight, merge_weight, router_weight, norm_gain, norm_shift, up_weight, inner_bias, down_weight, outer_bias
    )
    dense = gather_tiles(dense_own, "shard", shards)
    far = swap(near, "expert", ways, group)

    route_rows = jnp.pad(routes, ((0, all_rows - token_count), (0, 0)), constant_values=-1).T
    ids = jnp.arange(experts, dtype=jnp.int32)[:, None]
    named = (route_rows[0:1] == ids) | (route_rows[1:2] == ids)
    order = jnp.arange(all_rows, dtype=jnp.int32)
    in_chunk = (order[None, :] // chunk_tokens) == jnp.arange(chunks, dtype=jnp.int32)[:, None]
    named = (named[None] & in_chunk[:, None, :]).reshape(chunks * experts, all_rows)
    earlier = (order[:, None] < order[None, :]).astype(bf16)
    slots = jnp.dot(named.astype(bf16), earlier, preferred_element_type=f32).astype(jnp.int32)
    slots = jnp.where(named, slots, -1)
    slots = jnp.pad(slots, ((0, 8), (0, 0)), constant_values=jnp.sum(valid_mask))
    slots = after(slots, dense[1])
    slot_blocks = jnp.stack([slots] + [swap(slots, "expert", ways, b) for b in range(1, group)])
    group_count = jnp.sum(slot_blocks[:, -8:, 0:LANES], axis=0).astype(f32)
    shard_count = sum_over(group_count, "shard", shards)
    slot_blocks = slot_blocks[:, :-8].reshape(group, chunks, experts, all_rows)
    chosen = jnp.concatenate(
        [
            lax.dynamic_slice_in_dim(slot_blocks, expert, 1, 2),
            lax.dynamic_slice_in_dim(slot_blocks, expert ^ group, 1, 2),
        ],
        axis=2,
    )
    shard_id = shard[None]
    e_ids = jnp.stack([expert, expert ^ group])
    routing, tile_counts = [], []
    for c in range(chunks):
        pos = chosen[:, c, :, starts[c] : starts[c] + rows].reshape(2 * group, rows)
        counts = jnp.max(pos, axis=1) + 1
        places = jnp.pad(pos.T, ((0, 0), (0, LANES - 2 * group)), constant_values=-1)
        ends = jnp.sum((counts.reshape(group, 2) + ROW - 1) // ROW * ROW, axis=0)
        tile_counts.append((ends + MLP - 1) // MLP)
        routing.append(((shard_id, e_ids, counts), pos, places))

    def chunk_rows(array, c):
        part = array[starts[c] : min(starts[c] + rows, token_count)]
        return jnp.pad(part, ((0, rows - part.shape[0]),) + ((0, 0),) * (part.ndim - 1))

    toks = [chunk_rows(tokens, c) for c in range(chunks)]
    local = jnp.arange(rows, dtype=jnp.int32)[:, None]
    kept, valids = [], []
    for c in range(chunks):
        base = firsts[c] - starts[c]
        mask = (local >= base) & (local < base + chunk_tokens)
        kept.append(mask)
        valids.append(jnp.where(mask, chunk_rows(valid_mask, c).astype(f32)[:, None], 0.0))

    forward = []
    for c in range(chunks):
        gates = (forward[-1][4],) if c else ()
        forward.append(
            attention_forward(shard_id, after(toks[c], *gates), dense, firsts[c] - starts[c], chunk_images)
        )
    attended = forward[-1][4]
    arrivals = []
    arrivals.append(exchange(forward[0][4], ways, group))
    near_tiles = gather_tiles(
        after(near, dense[-1], shard_count, chosen), "shard", shards, (attended, *arrivals[0][1:])
    )
    tiles = near_tiles + gather_tiles(after(far, attended), "shard", shards)
    for c in range(1, chunks):
        arrivals.append(exchange(after(forward[c][4], near_tiles[1]), ways, group))
    valid_count = shard_count + swap(after(shard_count, attended), "expert", ways, group)

    def expert_part(c, j, before, *gates):
        sources = [after(arrivals[c][0], *gates)] + arrivals[c][1:]
        results = expert_forward(
            j,
            *routing[c],
            sources,
            dense,
            tiles[j * shards : (j + 1) * shards],
            group,
            experts,
            capacity,
            router_lane,
            before,
        )
        return results[:group], results[group:]

    nears, held, given = [], [], []
    for c in range(chunks):
        gates = (given[-1][0],) if given else (attended,)
        near_given, near_held = expert_part(c, 0, (), *gates)
        nears.append(near_given)
        held.append([near_held])
        if c < chunks - 1:
            far_given, far_held = expert_part(c, 1, near_given, valid_count)
            given.append(far_given)
            held[c].append(far_held)
    valid_count = valid_count[0, 0]
    scale = token_count * ways * shards / valid_count

    blocks_out, squared, final_grads, input_grads = [], 0.0, [], []
    router_parts, biases, saved, early = [], [], [], ()
    arrived = None
    for c in range(chunks):
        if c == chunks - 1:
            far_given, far_held = expert_part(c, 1, nears[c], *final_grads)
            given.append(far_given)
            held[c].append(far_held)
        parts = given[c] if c == 0 else [given[c][0]] + [after(part, *arrived) for part in given[c][1:]]
        block_out = forward[c][3]
        if c == 0:
            block_out = after(block_out, nears[-1][0])
        for part in give_back(parts, ways, group):
            block_out = block_out + part.astype(f32)
        error = block_out - chunk_rows(teacher, c).astype(f32)
        squared = squared + jnp.sum(valids[c] * jnp.sum(error * error, axis=1, keepdims=True))
        fg = scale * valids[c] * error
        final_grads.append(fg)
        blocks_out.append(jnp.where(kept[c], block_out, 0.0).astype(bf16))
        arrived = exchange(fg.astype(bf16), ways, group)
        if c:
            early = weight_grads(
                (0, 1), shard_id, after(tile_counts[c - 1], fg), saved[c - 1], biases[c - 1], shards, early
            )
            arrived[0] = after(arrived[0], early[0])
            input_grads[c - 1] = [input_grads[c - 1][0]] + [
                after(part, *arrived[1:]) for part in input_grads[c - 1][1:]
            ]
            input_grads[c - 1] = give_back(input_grads[c - 1], ways, group)
        loads = [array for x, y, probs, _, slope in held[c] for array in (x, y, probs, slope)]
        results = expert_backward(
            *routing[c],
            arrived,
            dense,
            tiles,
            loads,
            group,
            capacity,
            router_lane,
        )
        input_grads.append(results[:group])
        pg_rows, hg, router_part, inner_part, outer_part = results[group:]
        router_parts.append(router_part)
        biases.append((inner_part, outer_part))
        saved.append(([(arrays[0], arrays[3]) for arrays in held[c]], (pg_rows, hg)))
    last = chunks - 1
    far_tiles = weight_grads(
        (1,), shard_id, after(tile_counts[last], *input_grads[0][1:]), saved[last], biases[last], shards, early[2:]
    )
    input_grads[last] = give_back(input_grads[last], ways, group)
    far_sums, far_rest = fold_tiles(*far_tiles, "shard", shards)
    before = None
    for c in range(chunks):
        qkv, att, weights, res, _ = forward[c]
        gate = far_sums if c == 0 else before[0]
        before = attention_backward(
            after(shard_id, gate),
            input_grads[c],
            final_grads[c],
            res,
            att,
            qkv,
            weights,
            toks[c],
            dense,
            firsts[c] - starts[c],
            chunk_images,
            before,
            starts[c],
            router_parts if c == last else (),
        )
        if c < last:
            before = (*before, att)
        if c == 0:
            far_grad = far_rest()
            far_arrived = [
                swap(half, "expert", ways, group) for half in (far_grad[0, :hidden], far_grad[0, hidden:])
            ]
    token_grad, norm_part, *dense_parts = before
    dense_sums, dense_rest = fold_tiles(*dense_parts, "shard", shards)
    near_tiles = weight_grads(
        (0,), shard_id, after(tile_counts[last], dense_sums), saved[last], biases[last], shards, early[:2]
    )
    dense_grad = dense_rest()
    near_tiles = (after(near_tiles[0], dense_grad, far_arrived[1]), near_tiles[1])
    near_sums, near_rest = fold_tiles(*near_tiles, "shard", shards)
    near_grad = near_rest()
    up_sum = near_grad[0, :hidden].astype(f32) + far_arrived[0].astype(f32)
    up_grad = jnp.concatenate(
        [up_sum[:, fold * hidden : (fold + 1) * hidden] for fold in range(folds)], axis=0
    )
    rest_sum = near_grad[0, hidden:].astype(f32) + far_arrived[1].astype(f32)
    down_grad = rest_sum[:hidden]
    inner_grad = rest_sum[hidden : hidden + 1, 0:hidden]
    outer_grad = rest_sum[hidden + 1 : hidden + 2, 0:shard_rows]
    dense_sum = sum_split(dense_grad[0], "expert", ways, expert, near_sums, near_grad)
    output = jnp.zeros((all_rows, width), bf16)
    for c in range(chunks):
        output = output + jnp.pad(blocks_out[c], ((starts[c], all_rows - starts[c] - rows), (0, 0)))

    norm_sum = sum_over(sum_over(norm_part.at[4].set(squared), "shard", shards), "expert", ways)
    norm_sum = lax.dynamic_slice_in_dim(norm_sum, shard * shard_rows, shard_rows, 1)
    loss_value = norm_sum[4, 0] / (2.0 * valid_count)
    return (
        output[:token_count],
        loss_value,
        token_grad[:token_count],
        dense_sum[:, : 3 * width],
        dense_sum[:, 3 * width : 4 * width],
        dense_sum[:, 4 * width : 4 * width + experts],
        norm_sum[0:2],
        norm_sum[2:4],
        up_grad[None],
        inner_grad,
        down_grad[None],
        outer_grad,
    )


def solution(mesh):
    in_specs = (
        P(("expert", "shard"), None),
        P(("expert", "shard"), None),
        P(("expert", "shard")),
        P(("expert", "shard"), None),
        P("shard", None),
        P("shard", None),
        P("shard", None),
        P(None, "shard"),
        P(None, "shard"),
        P("expert", None, "shard"),
        P("expert", "shard"),
        P("expert", "shard", None),
        P("expert", "shard"),
    )
    out_specs = (
        P(("expert", "shard"), None),
        P(),
        P(("expert", "shard"), None),
        P("shard", None),
        P("shard", None),
        P("shard", None),
        P(None, "shard"),
        P(None, "shard"),
        P("expert", None, "shard"),
        P("expert", "shard"),
        P("expert", "shard", None),
        P("expert", "shard"),
    )
    return jax.shard_map(
        per_device, mesh=mesh, in_specs=in_specs, out_specs=out_specs, check_vma=False
    )
```
